256 devices in a mesh: row: 8 (over z_lo, core), col: 16 (over y, x), samp: 2 (over z_hi).
Axes of the slice: x: 4, y: 4, z: 8 (z_hi: 2, z_lo: 4; z = z_hi * 4 + z_lo), core: 2. Of those that a mesh axis runs over, the one named last changes fastest.
Arguments:
- pair_in: bfloat16 [512, 512, 128], P('row', 'col'), may hold values from -6 to 6
- residue_index: int32 [512], replicated, may hold values from 0 to 47
- chain_index: int32 [512], replicated, may hold values from 0 to 2
- token_mask: int32 [512], replicated, may hold values 0 or 1
- relpos_weight: bfloat16 [66, 128], replicated, may hold values from -5 to 5
- tri_proj: bfloat16 [128, 640], replicated, may hold values from -0.5 to 0.5
- tri_out: bfloat16 [128, 128], replicated, may hold values from -0.5 to 0.5
- bias_proj: bfloat16 [128, 16], replicated, may hold values from -0.5 to 0.5
- single: bfloat16 [512, 384], P('row'), may hold values from -6 to 6
- ada_proj: bfloat16 [384, 2304], replicated, may hold values from -0.3125 to 0.3125
- noisy: bfloat16 [16, 512, 768], P('samp', 'row'), may hold values from -6 to 6
- qkv_proj: bfloat16 [768, 3, 768], P(None, None, 'col'), may hold values from -0.21875 to 0.21875
- out_proj: bfloat16 [768, 768], P('col'), may hold values from -0.21875 to 0.21875
- cotangent: bfloat16 [16, 512, 768], P('samp', 'row', 'col'), may hold values from -6 to 6
Outputs:
- pair_out: bfloat16 [512, 512, 128], P('row', 'col')
- block_out: bfloat16 [16, 512, 768], P('samp', 'row', 'col')
- grad_pair: float32 [512, 512, 128], P('row', 'col')
- grad_single: float32 [512, 384], P('row')
The draws below stay inside these ranges and needn't reach their ends.
All inputs are finite; a program needn't handle non-finite values.
Results may differ from the reference program's by a relative error of at most 0.012.
The reference program's roundings to bfloat16 on the way count: a program that leaves them out, or rounds other values in their place, can miss the bound.
Values may be sent and summed in bfloat16 or wider, within the bound.
A program may use at most 128 MiB of HBM per device.

```python
import jax
import jax.numpy as jnp
from jax import lax

PAIR_W = 128
SINGLE_W = 384
DW = 768
HEADS = 16
HEAD_DIM = 48
REL_BINS = 66
TOKENS = 512
SAMPLES = 16


def set_ends(values, stream_key, smallest, top_value):
    place = [jax.random.randint(jax.random.fold_in(stream_key, axis), (), 0, length) for axis, length in enumerate(values.shape)]
    longest = values.shape.index(max(values.shape))
    beside = place[:longest] + [(place[longest] + 1) % values.shape[longest]] + place[longest + 1:]
    return values.at[tuple(place)].set(smallest).at[tuple(beside)].set(top_value)


def steps_of(rng, dims, shards, least, high):
    def one(dim, parts):
        heights = jax.random.uniform(jax.random.fold_in(jax.random.fold_in(rng, 6), dim), (parts,), jnp.float32, least / len(shards), high / len(shards))
        return jnp.repeat(jnp.exp(heights), dims[dim] // parts).reshape((-1,) + (1,) * (len(dims) - dim - 1))

    factor_of = one(*shards[0])
    for cut in shards[1:]:
        factor_of = factor_of * one(*cut)
    return factor_of


def bell_draw(key, extent, scale, bound, pieces=(), kind=jnp.bfloat16):
    drawn = jax.random.normal(key, extent, jnp.float32) * scale
    if len(pieces) > 0:
        drawn = steps_of(key, extent, pieces, -0.22, 0.18) * drawn
    return jnp.clip(drawn, min=-bound, max=bound).astype(kind)


def setup_inputs(seed: int = 0) -> dict:
    arg_keys = jax.random.split(jax.random.key(seed), 15)
    return {
        "pair_in": bell_draw(arg_keys[0], (TOKENS, TOKENS, PAIR_W), 1.0, 6.0, ((0, 8), (1, 16))),
        "residue_index": set_ends(jax.random.randint(arg_keys[1], (TOKENS,), 0, 48), jax.random.fold_in(arg_keys[1], 1), 0, 47).astype(jnp.int32),
        "chain_index": set_ends(jax.random.randint(arg_keys[2], (TOKENS,), 0, 3), jax.random.fold_in(arg_keys[2], 1), 0, 2).astype(jnp.int32),
        "token_mask": set_ends((jax.random.randint(arg_keys[3], (TOKENS,), 0, 8) < 7).astype(jnp.int32), jax.random.fold_in(arg_keys[3], 1), 0, 1),
        "relpos_weight": bell_draw(arg_keys[4], (REL_BINS, PAIR_W), 1.0, 5.0),
        "tri_proj": bell_draw(arg_keys[5], (PAIR_W, 5 * PAIR_W), PAIR_W ** -0.5, 0.5),
        "tri_out": bell_draw(arg_keys[6], (PAIR_W, PAIR_W), PAIR_W ** -0.5, 0.5),
        "bias_proj": bell_draw(arg_keys[7], (PAIR_W, HEADS), PAIR_W ** -0.5, 0.5),
        "single": bell_draw(arg_keys[8], (TOKENS, SINGLE_W), 1.0, 6.0, ((0, 8),)),
        "ada_proj": bell_draw(arg_keys[9], (SINGLE_W, 3 * DW), SINGLE_W ** -0.5, 0.3125),
        "noisy": bell_draw(arg_keys[10], (SAMPLES, TOKENS, DW), 1.0, 6.0, ((0, 2), (1, 8))),
        "qkv_proj": bell_draw(arg_keys[11], (DW, 3, DW), DW ** -0.5, 0.21875, ((2, 16),)),
        "out_proj": bell_draw(arg_keys[12], (DW, DW), DW ** -0.5, 0.21875, ((0, 16),)),
        "cotangent": bell_draw(arg_keys[13], (SAMPLES, TOKENS, DW), 1.0, 6.0, ((0, 2), (1, 8), (2, 16))),
    }


EPSILON = 1e-05
HIGHEST = lax.Precision.HIGHEST

def normalize(values_in):
    average = lax.optimization_barrier(jnp.mean(values_in, -1, keepdims=True))
    centered = values_in - average
    variance = lax.optimization_barrier(jnp.mean(centered * centered, -1, keepdims=True))
    return centered * lax.rsqrt(variance + EPSILON)

def normalize_grad(values_in, upstream):
    average = lax.optimization_barrier(jnp.mean(values_in, -1, keepdims=True))
    centered = values_in - average
    variance = lax.optimization_barrier(jnp.mean(centered * centered, -1, keepdims=True))
    inv_std = lax.rsqrt(variance + EPSILON)
    unit_rows = centered * inv_std
    return inv_std * (upstream - lax.optimization_barrier(jnp.mean(upstream, -1, keepdims=True)) - unit_rows * lax.optimization_barrier(jnp.mean(upstream * unit_rows, -1, keepdims=True)))

def relative_embedding(res_rows, res_cols, chain_rows, chain_cols, relpos_weight):
    max_offset = (REL_BINS - 2) // 2
    offset = res_rows[:, None] - res_cols[None, :]
    bucket = jnp.where(chain_rows[:, None] == chain_cols[None, :], jnp.clip(offset + max_offset, 0, 2 * max_offset), REL_BINS - 1)
    onehot = (bucket[:, :, None] == jnp.arange(REL_BINS, dtype=jnp.int32)[None, None, :]).astype(jnp.float32)
    return jnp.einsum('ijr,rc->ijc', onehot, relpos_weight.astype(jnp.float32))

def reference(pair_in, residue_index, chain_index, token_mask, relpos_weight, tri_proj, tri_out, bias_proj, single, ada_proj, noisy, qkv_proj, out_proj, cotangent):
    pair_width = PAIR_W
    pair_full = pair_in.astype(jnp.float32) + relative_embedding(residue_index, residue_index, chain_index, chain_index, relpos_weight)
    normed_pair = normalize(pair_full).astype(jnp.bfloat16)
    projected = jnp.dot(normed_pair, tri_proj, preferred_element_type=jnp.float32)
    mask_f = token_mask.astype(jnp.float32)
    pair_mask = (mask_f[:, None] * mask_f[None, :])[:, :, None]
    left_side = (jax.nn.sigmoid(projected[..., pair_width:2 * pair_width]) * projected[..., :pair_width] * pair_mask).astype(jnp.bfloat16)
    right_side = (jax.nn.sigmoid(projected[..., 3 * pair_width:4 * pair_width]) * projected[..., 2 * pair_width:3 * pair_width] * pair_mask).astype(jnp.bfloat16)
    tri_gate = jax.nn.sigmoid(projected[..., 4 * pair_width:])
    triangle = jnp.einsum('ikc,jkc->ijc', left_side.astype(jnp.float32), right_side.astype(jnp.float32))
    update = jnp.dot(normalize(triangle).astype(jnp.bfloat16), tri_out, preferred_element_type=jnp.float32)
    pair_out = (pair_full + tri_gate * update).astype(jnp.bfloat16)
    bias_b = jnp.einsum('ijc,ch->hij', pair_out.astype(jnp.float32), bias_proj.astype(jnp.float32)).astype(jnp.bfloat16)
    bias_all = lax.optimization_barrier(bias_b).astype(jnp.float32)
    model_width = DW
    cvec = normalize(single.astype(jnp.float32)).astype(jnp.bfloat16)
    conditioning = jnp.dot(cvec, ada_proj, preferred_element_type=jnp.float32)
    ada_scale = jax.nn.sigmoid(conditioning[:, :model_width])
    ada_shift = conditioning[:, model_width:2 * model_width]
    out_gate = jax.nn.sigmoid(conditioning[:, 2 * model_width:])
    key_ok = token_mask > 0
    score_scale = 1.0 / HEAD_DIM ** 0.5
    qkv_f = qkv_proj.astype(jnp.float32)
    token_count = TOKENS

    def one_sample(sums, inputs):
        sample_in, grad_out = inputs
        normed_in = normalize(sample_in.astype(jnp.float32))
        hidden = (ada_scale * normed_in + ada_shift).astype(jnp.bfloat16)
        qkv_all = jnp.einsum('td,dqe->tqe', hidden.astype(jnp.float32), qkv_f).astype(jnp.bfloat16)
        queries = qkv_all[:, 0].reshape(token_count, HEADS, HEAD_DIM).astype(jnp.float32)
        key_rows = qkv_all[:, 1].reshape(token_count, HEADS, HEAD_DIM).astype(jnp.float32)
        value_rows = qkv_all[:, 2].reshape(token_count, HEADS, HEAD_DIM).astype(jnp.float32)
        scores = jnp.einsum('ihd,jhd->hij', queries, key_rows) * score_scale + bias_all
        scores = jnp.where(key_ok[None, None, :], scores, -1000000000.0)
        probs = jax.nn.softmax(scores, axis=-1)
        probs_b = probs.astype(jnp.bfloat16).astype(jnp.float32)
        attended = jnp.einsum('hij,jhd->ihd', probs_b, value_rows).astype(jnp.bfloat16).reshape(token_count, model_width)
        mixed = jnp.dot(attended, out_proj, preferred_element_type=jnp.float32)
        block = (sample_in.astype(jnp.float32) + out_gate * mixed).astype(jnp.bfloat16)
        grad_in = grad_out.astype(jnp.float32)
        d_mixed = (grad_in * out_gate).astype(jnp.bfloat16)
        d_gate = grad_in * mixed
        d_att = jnp.dot(d_mixed, out_proj.T, preferred_element_type=jnp.float32).astype(jnp.bfloat16)
        d_att = d_att.reshape(token_count, HEADS, HEAD_DIM).astype(jnp.float32)
        d_probs = jnp.einsum('ihd,jhd->hij', d_att, value_rows)
        d_scores = probs * (d_probs - lax.optimization_barrier(jnp.sum(probs * d_probs, -1, keepdims=True)))
        d_scaled = (d_scores * score_scale).astype(jnp.bfloat16).astype(jnp.float32)
        d_query = jnp.einsum('hij,jhd->ihd', d_scaled, key_rows).astype(jnp.bfloat16)
        d_keys = jnp.einsum('hij,ihd->jhd', d_scaled, queries).astype(jnp.bfloat16)
        d_values = jnp.einsum('hij,ihd->jhd', probs_b, d_att).astype(jnp.bfloat16)
        d_qkv = jnp.stack([d_query, d_keys, d_values], 1).reshape(token_count, 3, model_width)
        d_hidden = jnp.einsum('tqe,dqe->td', d_qkv.astype(jnp.float32), qkv_f)
        sums = (sums[0] + d_gate, sums[1] + d_hidden * normed_in, sums[2] + d_hidden, sums[3] + d_scores)
        return (sums, block)
    init = (jnp.zeros((token_count, model_width), jnp.float32), jnp.zeros((token_count, model_width), jnp.float32), jnp.zeros((token_count, model_width), jnp.float32), jnp.zeros((HEADS, token_count, token_count), jnp.float32))
    sums, block_out = lax.scan(one_sample, init, (noisy, cotangent))
    d_gate_sum, d_scale_sum, d_shift_sum, d_bias = sums
    w_ada = ada_proj.astype(jnp.float32)
    d_cvec = jnp.dot(d_scale_sum * ada_scale * (1.0 - ada_scale), w_ada[:, :model_width].T, precision=HIGHEST)
    d_cvec = d_cvec + jnp.dot(d_shift_sum, w_ada[:, model_width:2 * model_width].T, precision=HIGHEST)
    d_cvec = d_cvec + jnp.dot(d_gate_sum * out_gate * (1.0 - out_gate), w_ada[:, 2 * model_width:].T, precision=HIGHEST)
    grad_single = normalize_grad(single.astype(jnp.float32), d_cvec)
    grad_pair = jnp.einsum('hij,ch->ijc', d_bias, bias_proj.astype(jnp.float32), precision=HIGHEST)
    return (pair_out, block_out, grad_pair, grad_single)
```

```python
import jax
import jax.numpy as jnp
from jax import lax
from jax.experimental import pallas as pl
from jax.experimental.pallas import tpu as pltpu
from jax.sharding import PartitionSpec as P

HEAD_DIM = 48
REL_BINS = 66
EPSILON = 1e-05
HIGHEST = lax.Precision.HIGHEST
MESH = pl.DeviceIdType.MESH
F32 = jnp.float32
BF16 = jnp.bfloat16
NCOL = 16
NROW = 8


def dg(a, b, ca, cb, **kw):
    return lax.dot_general(a, b, (((ca,), (cb,)), ((), ())), preferred_element_type=F32, **kw)


def place():
    return lax.axis_index("row"), lax.axis_index("col"), lax.axis_index("samp")


def rmod(a, n):
    return lax.rem(a, n)


def ring_shift(oz, dest_core):
    if oz == 2:
        return 2 + 4 * dest_core
    return (0, 1, None, 7)[oz]


def row_dest(oz, cx):
    row, col, samp = place()
    z, core = samp * 4 + row // 2, rmod(row, 2)
    to_core = rmod(core + cx, 2)
    to_z = rmod(z + ring_shift(oz, to_core), 8)
    return rmod(to_z, 4) * 2 + to_core, col, to_z // 4


def row_source(oz, cx):
    row, col, samp = place()
    z, core = samp * 4 + row // 2, rmod(row, 2)
    from_core = rmod(core + cx, 2)
    from_z = rmod(z + 8 - ring_shift(oz, core), 8)
    return rmod(from_z, 4) * 2 + from_core, col, from_z // 4


ROW_IDS = [(oz, cx) for oz in range(4) for cx in range(2) if (oz, cx) != (0, 0)]


def remote(src, dst, ssem, rsem, to):
    return pltpu.make_async_remote_copy(
        src_ref=src, dst_ref=dst, send_sem=ssem, recv_sem=rsem, device_id=to, device_id_type=MESH
    )


def col_start(src_of, slot_of, ssem, rsem):
    row, col, samp = place()

    def one(o, _):
        to = rmod(col + o, NCOL)
        remote(src_of(to), slot_of(col), ssem.at[o], rsem.at[o], (row, to, samp)).start()
        return 0

    lax.fori_loop(1, NCOL, one, 0)


def col_wait(src_of, slot_of, ssem, rsem, recv=True, send=True):
    row, col, samp = place()

    def one(o, _):
        to = rmod(col + o, NCOL)
        came = rmod(col + NCOL - o, NCOL)
        if recv:
            remote(src_of(to), slot_of(came), ssem.at[o], rsem.at[o], (row, to, samp)).wait_recv()
        if send:
            remote(src_of(to), slot_of(came), ssem.at[o], rsem.at[o], (row, to, samp)).wait_send()
        return 0

    lax.fori_loop(1, NCOL, one, 0)


def row_start(src_of, slot_of, ssem, rsem):
    row = lax.axis_index("row")
    for oz, cx in ROW_IDS:
        to = row_dest(oz, cx)
        i = oz * 2 + cx
        remote(src_of(to[0]), slot_of(row), ssem.at[i], rsem.at[i], to).start()


def row_wait(src_of, slot_of, ssem, rsem, recv=True, send=True):
    for oz, cx in ROW_IDS:
        to, came = row_dest(oz, cx), row_source(oz, cx)
        i = oz * 2 + cx
        copy = remote(src_of(to[0]), slot_of(came[0]), ssem.at[i], rsem.at[i], to)
        if recv:
            copy.wait_recv()
        if send:
            copy.wait_send()


def signal(sem, to):
    pl.semaphore_signal(sem, inc=1, device_id=to, device_id_type=MESH)


def own_row_ids():
    return [o for o in range(1, 4)]


def pair_kernel(
    pair_ref, resr_ref, chr_ref, resc_ref, chc_ref, maskp_ref, relpos_ref, tri_ref, triout_ref,
    biasp_ref, kv_ref, dmx_ref,
    pairout_ref, bias_ref, kvall_ref, dmxall_ref,
    pf, gate, lrf, lbuf, recv_a, got, rcat, mtmp, tbuf, got_c, got_d, bias_f, bias_b, bias_got,
    sa, ra, sb, rb, sc, rc, sd, rd, se, re, skv, rkv, skf, rkf, sdm, rdm, loc,
):
    row, col, samp = place()
    core = rmod(row, 2)
    zlo = row // 2
    mate = (row + 1 - 2 * core, col, samp)
    barrier = pltpu.get_barrier_semaphore()
    for oz, cx in ROW_IDS:
        signal(barrier, row_source(oz, cx))

    def greet(o, _):
        signal(barrier, (row, rmod(col + o, NCOL), samp))
        return 0

    lax.fori_loop(1, NCOL, greet, 0)
    for o in own_row_ids():
        signal(barrier, (rmod(zlo + o, 4) * 2 + core, col, samp))
    signal(barrier, mate)
    pl.semaphore_wait(barrier, 7 + 15 + 3 + 1)

    kv_own = pltpu.make_async_copy(kv_ref, kvall_ref.at[row], loc.at[0])
    kv_own.start()
    kv_out = []
    for o in own_row_ids():
        to = (rmod(zlo + o, 4) * 2 + core, col, samp)
        kv_out.append(remote(kv_ref, kvall_ref.at[row], skv.at[o], rkv.at[o], to))
        kv_out[-1].start()
    kv_mate = remote(kv_ref, kvall_ref.at[row], skf.at[0], rkf.at[0], mate)
    kv_mate.start()
    dm_own = pltpu.make_async_copy(dmx_ref, dmxall_ref.at[col], loc.at[1])
    dm_own.start()
    dm_src, dm_slot = (lambda to: dmx_ref), (lambda c: dmxall_ref.at[c])

    def load(i, _):
        pf[pl.ds(i * 32, 32), :] = pair_ref[i].astype(F32)
        return 0

    lax.fori_loop(0, 64, load, 0, unroll=4)
    bins = lax.broadcasted_iota(jnp.int32, (64, 128), 1)
    resr, chr_ = resr_ref[...], chr_ref[...]
    relpos = relpos_ref[...]

    def stage1(lo, _):
        parts = []
        for hi in range(2):
            j = lo + 16 * hi
            off = jnp.clip(resr - resc_ref[pl.ds(j, 1), :] + 32, 0, 64)
            bucket = jnp.where(chr_ == chc_ref[pl.ds(j, 1), :], off, REL_BINS - 1)
            onehot = jnp.where(bucket == bins, 1.0, 0.0).astype(BF16)
            parts.append(
                pf[pl.ds(j, 64, stride=32), :] + jnp.dot(onehot, relpos, preferred_element_type=F32)
            )
        full = jnp.concatenate(parts, 0)
        for hi in range(2):
            pf[pl.ds(lo + 16 * hi, 64, stride=32), :] = parts[hi]
        mean = jnp.mean(full, -1, keepdims=True)
        cent = full - mean
        var = jnp.mean(cent * cent, -1, keepdims=True)
        zl = (cent * lax.rsqrt(var + EPSILON)).astype(BF16)
        pt = dg(tri_ref[:, :512], zl, 0, 1)
        mask = maskp_ref[pl.ds(lo, 1), :]
        left = jax.nn.sigmoid(pt[128:256]) * pt[:128] * mask
        right = jax.nn.sigmoid(pt[384:512]) * pt[256:384] * mask
        lrf[pl.ds(lo, 128, stride=16), :] = left
        lrf[pl.ds(2048 + lo, 128, stride=16), :] = right
        gate[lo] = jax.nn.sigmoid(
            jnp.dot(zl, tri_ref[:, 512:], preferred_element_type=F32)
        )
        return 0

    lax.fori_loop(0, 16, stage1, 0, unroll=2)

    def pack(c, _):
        for half in range(2):
            lbuf[half, c] = (
                lrf[pl.ds(half * 2048 + c * 128, 128), :].astype(BF16).reshape(8, 16, 128)
            )
        return 0

    lax.fori_loop(0, 16, pack, 0)

    a_src = [lambda to, h=h: lbuf.at[h, to] for h in range(2)]
    a_slot = [lambda c, h=h: recv_a.at[h, c] for h in range(2)]
    b_src = [lambda r, h=h: recv_a.at[h, :, r] for h in range(2)]
    b_slot = [lambda r, h=h: got.at[h, r] for h in range(2)]
    for h in range(2):
        pltpu.make_async_copy(lbuf.at[h, col], recv_a.at[h, col], loc.at[2 + h]).start()
        col_start(a_src[h], a_slot[h], sa.at[h], ra.at[h])
    col_start(dm_src, dm_slot, sdm, rdm)
    for h in range(2):
        pltpu.make_async_copy(lbuf.at[h, col], recv_a.at[h, col], loc.at[2 + h]).wait()
        col_wait(a_src[h], a_slot[h], sa.at[h], ra.at[h])
        pltpu.make_async_copy(recv_a.at[h, :, row], got.at[h, row], loc.at[4 + h]).start()
        row_start(b_src[h], b_slot[h], sb.at[h], rb.at[h])
    for o in own_row_ids():
        came = rmod(zlo + 4 - o, 4) * 2 + core
        remote(kv_ref, kvall_ref.at[came], skv.at[o], rkv.at[o], mate).wait_recv()
        remote(kvall_ref.at[came], kvall_ref.at[came], skf.at[o], rkf.at[o], mate).start()
    for h in (1, 0):
        pltpu.make_async_copy(recv_a.at[h, :, row], got.at[h, row], loc.at[4 + h]).wait()
        row_wait(b_src[h], b_slot[h], sb.at[h], rb.at[h])

    def turn(r, _):
        rcat[pl.ds(pl.multiple_of(r * 128, 128), 128), :] = (
            got[1, r].reshape(256, 128).astype(F32).T.astype(BF16)
        )
        return 0

    lax.fori_loop(0, 8, turn, 0)
    low = lax.broadcasted_iota(jnp.int32, (16, 128), 1) < 64

    def tri(rp, _):
        rhs = jnp.concatenate(
            [got[0, 2 * rp].reshape(256, 128), got[0, 2 * rp + 1].reshape(256, 128)], 1
        )
        mtmp[...] = jnp.dot(rcat[...], rhs, preferred_element_type=F32)

        def out(rj, _):
            for half in range(2):
                top = mtmp[pl.ds(rj * 128, 64), half * 128 : half * 128 + 128]
                bot = mtmp[pl.ds(rj * 128 + 64, 64), half * 128 : half * 128 + 128]
                for jh in range(2):
                    a = slice(jh * 32, jh * 32 + 16)
                    b = slice(jh * 32 + 16, jh * 32 + 32)
                    t = jnp.where(
                        low,
                        top[a] + pltpu.roll(bot[a], 64, 1),
                        pltpu.roll(top[b], 64, 1) + bot[b],
                    )
                    tbuf[2 * rp + half, 2 * rj + jh] = t.astype(BF16)
            return 0

        lax.fori_loop(0, 8, out, 0, unroll=2)
        return 0

    lax.fori_loop(0, 4, tri, 0)

    c_src, c_slot = (lambda r: tbuf.at[r]), (lambda r: got_c.at[r])
    d_src, d_slot = (lambda c: got_c.at[:, c]), (lambda c: got_d.at[c])
    own_c = pltpu.make_async_copy(tbuf.at[row], got_c.at[row], loc.at[6])
    own_c.start()
    row_start(c_src, c_slot, sc, rc)
    own_c.wait()
    row_wait(c_src, c_slot, sc, rc)
    own_d = pltpu.make_async_copy(got_c.at[:, col], got_d.at[col], loc.at[7])
    own_d.start()
    col_start(d_src, d_slot, sd, rd)
    own_d.wait()
    col_wait(d_src, d_slot, sd, rd)

    def widen(c, _):
        lrf[pl.ds(c * 128, 128), :] = got_d[c].reshape(128, 128).astype(F32)
        return 0

    lax.fori_loop(0, 16, widen, 0)
    triout = triout_ref[...]
    biasp = biasp_ref[...]

    def stage3(lo, _):
        t = lrf[pl.ds(lo, 128, stride=16), :]
        mean = jnp.mean(t, 0, keepdims=True)
        cent = t - mean
        var = jnp.mean(cent * cent, 0, keepdims=True)
        tn = (cent * lax.rsqrt(var + EPSILON)).astype(BF16)
        upd = dg(tn, triout, 0, 0) * gate[lo]
        outs = []
        for hi in range(2):
            at = pl.ds(lo + 16 * hi, 64, stride=32)
            val = (pf[at, :] + upd[hi * 64 : hi * 64 + 64]).astype(BF16)
            pf[at, :] = val.astype(F32)
            outs.append(val)
        bias_f[pl.ds(lo, 16, stride=16), :] = dg(biasp, jnp.concatenate(outs, 0), 0, 1)
        return 0

    lax.fori_loop(0, 16, stage3, 0, unroll=2)
    bias_b[...] = bias_f[...].astype(BF16).reshape(16, 16, 128)
    e_src, e_slot = (lambda c: bias_b.at[c]), (lambda c: bias_got.at[c])
    own_e = pltpu.make_async_copy(bias_b.at[col], bias_got.at[col], loc.at[8])
    own_e.start()
    col_start(e_src, e_slot, se, re)

    def store(i, _):
        pairout_ref[i] = pf[pl.ds(i * 32, 32), :].astype(BF16)
        return 0

    lax.fori_loop(0, 64, store, 0, unroll=4)
    own_e.wait()
    col_wait(e_src, e_slot, se, re)
    bias_ref[...] = bias_got[...].reshape(256, 128)

    kv_own.wait()
    dm_own.wait()
    for copy in kv_out:
        copy.wait_send()
    kv_mate.wait_send()
    mate_core = 1 - core
    for o in range(4):
        came = rmod(zlo + 4 - o, 4) * 2
        remote(kvall_ref.at[came + core], kvall_ref.at[came + mate_core], skf.at[o], rkf.at[o], mate).wait_recv()
        if o > 0:
            remote(kvall_ref.at[came + core], kvall_ref.at[came + core], skf.at[o], rkf.at[o], mate).wait_send()
    col_wait(dm_src, dm_slot, sdm, rdm)


def pair_stage(pair_in, resr, chr_, resc, chc, maskp, relpos, tri_proj, tri_out, bias_proj, kv, dmx):
    vm = pl.BlockSpec(memory_space=pltpu.VMEM)
    hbm = pl.BlockSpec(memory_space=pl.ANY)
    dma = pltpu.SemaphoreType.DMA
    return pl.pallas_call(
        pair_kernel,
        out_shape=(
            jax.ShapeDtypeStruct((64, 32, 128), BF16),
            jax.ShapeDtypeStruct((256, 128), BF16),
            jax.ShapeDtypeStruct((8, *kv.shape), BF16),
            jax.ShapeDtypeStruct((16, *dmx.shape), BF16),
        ),
        in_specs=[vm] * 12,
        out_specs=(vm, vm, hbm, hbm),
        scratch_shapes=[
            pltpu.VMEM((2048, 128), F32),
            pltpu.VMEM((16, 128, 128), F32),
            pltpu.VMEM((4096, 128), F32),
            pltpu.VMEM((2, 16, 8, 16, 128), BF16),
            pltpu.VMEM((2, 16, 8, 16, 128), BF16),
            pltpu.VMEM((2, 8, 16, 16, 128), BF16),
            pltpu.VMEM((1024, 256), BF16),
            pltpu.VMEM((1024, 256), F32),
            pltpu.VMEM((8, 16, 16, 128), BF16),
            pltpu.VMEM((8, 16, 16, 128), BF16),
            pltpu.VMEM((16, 8, 16, 128), BF16),
            pltpu.VMEM((256, 128), F32),
            pltpu.VMEM((16, 16, 128), BF16),
            pltpu.VMEM((16, 16, 128), BF16),
            dma((2, 16)), dma((2, 16)), dma((2, 8)), dma((2, 8)), dma((8,)), dma((8,)),
            dma((16,)), dma((16,)), dma((16,)), dma((16,)), dma((4,)), dma((4,)),
            dma((4,)), dma((4,)), dma((16,)), dma((16,)), dma((9,)),
        ],
        compiler_params=pltpu.CompilerParams(
            collective_id=1, has_side_effects=True, vmem_limit_bytes=48 * 1024 * 1024
        ),
        name="pair_stage",
    )(pair_in, resr, chr_, resc, chc, maskp, relpos, tri_proj, tri_out, bias_proj, kv, dmx)


def both(x, low, first):
    turned = pltpu.roll(x, 64, 1)
    return jnp.where(low, x, turned) if first else jnp.where(low, turned, x)


def attention_kernel(
    qd_ref, kv_ref, dmx_ref, wout_ref, bias_ref, keyok_ref, biasp_ref,
    mixed_ref, dq_ref, dkv_ref, gpair_ref,
    datt, mix_s, mix_r, dkv_s, dkv_r, dbias, db_s, db_r,
    sm, rm, sk, rk, sb, rb, loc, locm, lock,
):
    row, col, samp = place()
    barrier = pltpu.get_barrier_semaphore()

    def greet(o, _):
        signal(barrier, (row, rmod(col + o, NCOL), samp))
        return 0

    def greet_row(o, _):
        signal(barrier, (rmod(row + o, NROW), col, samp))
        return 0

    def greet_far(o, _):
        signal(barrier, (row, rmod(col + o, NCOL), 1 - samp))
        return 0

    lax.fori_loop(1, NCOL, greet, 0)
    lax.fori_loop(1, NROW, greet_row, 0)
    lax.fori_loop(0, NCOL, greet_far, 0)

    low = lax.broadcasted_iota(jnp.int32, (64, 128), 1) < 64
    diag = (
        (lax.broadcasted_iota(jnp.int32, (128, 128), 0) < 64)
        == (lax.broadcasted_iota(jnp.int32, (128, 128), 1) < 64)
    )

    def blockdiag(x):
        return jnp.where(diag, jnp.concatenate([x, x], 0), 0.0).astype(BF16)

    datt[...] = jnp.zeros_like(datt)

    def d_att(f, _):
        w = blockdiag(wout_ref[f].astype(F32))
        datt[...] += dg(dmx_ref[f], w, 1, 1)
        return 0

    lax.fori_loop(0, NCOL, d_att, 0)
    datt[...] = datt[...].astype(BF16).astype(F32)
    dbias[...] = jnp.zeros_like(dbias)
    scale = 1.0 / HEAD_DIM**0.5

    def mix_src(s4):
        return lambda f: mix_s.at[f, s4]

    def mix_slot(s4):
        return lambda h: mix_r.at[h, s4]

    def row_copy(s4, o):
        to, came = rmod(row + o, NROW), rmod(row + NROW - o, NROW)
        return to, came

    def pair_of_samples(s4, _):
        x = datt[pl.ds(pl.multiple_of(s4 * 64, 64), 64), :]
        folded = []
        for sh in range(2):
            s = s4 + 4 * sh
            kp = jnp.concatenate([kv_ref[r, 0, s] for r in range(8)], 0)
            vp = jnp.concatenate([kv_ref[r, 1, s] for r in range(8)], 0)
            qq = blockdiag(qd_ref[s].astype(F32))
            dd = blockdiag(both(x, low, sh == 0))
            sc = dg(kp, qq, 1, 1) * scale + bias_ref[...].astype(F32)
            sc = jnp.where(keyok_ref[...] > 0, sc, -1000000000.0)
            top = jnp.max(sc, 0, keepdims=True)
            top = jnp.maximum(top, pltpu.roll(top, 64, 1))
            ex = jnp.exp(sc - top)
            tot = jnp.sum(ex, 0, keepdims=True)
            tot = tot + pltpu.roll(tot, 64, 1)
            probs = ex / tot
            pb = probs.astype(BF16)
            m = dg(pb, vp, 0, 0)
            folded.append((m[:64], m[64:]))
            dp = dg(vp, dd, 1, 1)
            dot = jnp.sum(probs * dp, 0, keepdims=True)
            dot = dot + pltpu.roll(dot, 64, 1)
            ds = probs * (dp - dot)
            dbias[...] += ds
            dsb = (ds * scale).astype(BF16)
            mq = dg(dsb, kp, 0, 0)
            a, b = mq[:64], mq[64:]
            dq_ref[s] = (a + pltpu.roll(b, 64, 1)).astype(BF16)
            dk = jnp.dot(dsb, qq, preferred_element_type=F32).astype(BF16)
            dv = jnp.dot(pb, dd, preferred_element_type=F32).astype(BF16)
            for r in range(8):
                dkv_s[r, s4, sh] = dk[r * 32 : r * 32 + 32]
                dkv_s[r, s4, 2 + sh] = dv[r * 32 : r * 32 + 32]
        (a0, b0), (a1, b1) = folded
        att = jnp.where(low, a0 + pltpu.roll(b0, 64, 1), pltpu.roll(a1, 64, 1) + b1).astype(BF16)
        for f in range(NCOL):
            w = blockdiag(wout_ref[f].astype(F32))
            mix_s[f, s4] = jnp.dot(att, w, preferred_element_type=F32).astype(BF16)

        @pl.when(s4 == 0)
        def _():
            pl.semaphore_wait(barrier, 15 + 7 + 16)

        pltpu.make_async_copy(mix_s.at[col, s4], mix_r.at[col, s4], locm.at[s4]).start()
        pltpu.make_async_copy(dkv_s.at[row, s4], dkv_r.at[row, s4], lock.at[s4]).start()
        col_start(mix_src(s4), mix_slot(s4), sm.at[s4], rm.at[s4])

        def one(o, _):
            to, _came = row_copy(s4, o)
            remote(
                dkv_s.at[to, s4], dkv_r.at[row, s4], sk.at[s4, o], rk.at[s4, o], (to, col, samp)
            ).start()
            return 0

        lax.fori_loop(1, NROW, one, 0)
        return 0

    lax.fori_loop(0, 4, pair_of_samples, 0)

    db_s[...] = dbias[...].reshape(16, 16, 128)
    own_b = pltpu.make_async_copy(db_s.at[col], db_r.at[samp, col], loc.at[0])
    own_b.start()

    def db_send(o, _):
        to = rmod(col + o, NCOL)
        remote(db_s.at[to], db_r.at[samp, col], sb.at[1, o], rb.at[1, o], (row, to, 1 - samp)).start()
        return 0

    lax.fori_loop(0, NCOL, db_send, 0)
    near_src, near_slot = (lambda c: db_s.at[c]), (lambda c: db_r.at[samp, c])
    col_start(near_src, near_slot, sb.at[0], rb.at[0])

    for s4 in range(4):
        pltpu.make_async_copy(mix_s.at[col, s4], mix_r.at[col, s4], locm.at[s4]).wait()
        col_wait(mix_src(s4), mix_slot(s4), sm.at[s4], rm.at[s4])
        total = mix_r[0, s4].astype(F32)
        for h in range(1, NCOL):
            total = total + mix_r[h, s4].astype(F32)
        mixed_ref[s4] = total

    own_b.wait()
    col_wait(near_src, near_slot, sb.at[0], rb.at[0])

    def db_wait(o, _):
        to, came = rmod(col + o, NCOL), rmod(col + NCOL - o, NCOL)
        copy = remote(
            db_s.at[to], db_r.at[1 - samp, came], sb.at[1, o], rb.at[1, o], (row, to, 1 - samp)
        )
        copy.wait_recv()
        copy.wait_send()
        return 0

    lax.fori_loop(0, NCOL, db_wait, 0)
    dbias[...] = (db_r[0] + db_r[1]).reshape(256, 128)
    biasp = jnp.concatenate([biasp_ref[...]] * 3, 1)

    def grad(lo, _):
        d = dbias[pl.ds(lo, 16, stride=16), :]
        d1 = d.astype(BF16)
        rest = d - d1.astype(F32)
        d2 = rest.astype(BF16)
        d3 = (rest - d2.astype(F32)).astype(BF16)
        g = dg(jnp.concatenate([d1, d2, d3], 0), biasp, 0, 1)
        for hi in range(2):
            gpair_ref[pl.ds(lo + 16 * hi, 64, stride=32), :] = g[hi * 64 : hi * 64 + 64]
        return 0

    lax.fori_loop(0, 16, grad, 0, unroll=2)

    for s4 in range(4):
        pltpu.make_async_copy(dkv_s.at[row, s4], dkv_r.at[row, s4], lock.at[s4]).wait()

        def done(o, _):
            to, came = row_copy(s4, o)
            copy = remote(
                dkv_s.at[to, s4], dkv_r.at[came, s4], sk.at[s4, o], rk.at[s4, o], (to, col, samp)
            )
            copy.wait_recv()
            copy.wait_send()
            return 0

        lax.fori_loop(1, NROW, done, 0)
        total = dkv_r[0, s4].astype(F32)
        for r in range(1, NROW):
            total = total + dkv_r[r, s4].astype(F32)
        dkv_ref[s4] = total.astype(BF16)


def attention_stage(qd, kv_all, dmx_all, wout, bias, keyok, bias_proj):
    vm = pl.BlockSpec(memory_space=pltpu.VMEM)
    dma = pltpu.SemaphoreType.DMA
    return pl.pallas_call(
        attention_kernel,
        out_shape=(
            jax.ShapeDtypeStruct((4, 64, 128), F32),
            jax.ShapeDtypeStruct((8, 64, 128), BF16),
            jax.ShapeDtypeStruct((4, 4, 32, 128), BF16),
            jax.ShapeDtypeStruct((2048, 128), F32),
        ),
        in_specs=[vm] * 7,
        out_specs=(vm,) * 4,
        scratch_shapes=[
            pltpu.VMEM((256, 128), F32),
            pltpu.VMEM((16, 4, 64, 128), BF16),
            pltpu.VMEM((16, 4, 64, 128), BF16),
            pltpu.VMEM((8, 4, 4, 32, 128), BF16),
            pltpu.VMEM((8, 4, 4, 32, 128), BF16),
            pltpu.VMEM((256, 128), F32),
            pltpu.VMEM((16, 16, 128), F32),
            pltpu.VMEM((2, 16, 16, 128), F32),
            dma((4, 16)), dma((4, 16)), dma((4, 8)), dma((4, 8)), dma((2, 16)), dma((2, 16)),
            dma((1,)), dma((4,)), dma((4,)),
        ],
        compiler_params=pltpu.CompilerParams(
            collective_id=2, has_side_effects=True, vmem_limit_bytes=48 * 1024 * 1024
        ),
        name="attention_stage",
    )(qd, kv_all, dmx_all, wout, bias, keyok, bias_proj)


def total_kernel(x_ref, out_ref, parts, mine, s1, r1, s2, r2, loc):
    row, col, samp = place()
    me = samp * 16 + col
    barrier = pltpu.get_barrier_semaphore()

    def at(i):
        return row, rmod(i, 16), i // 16

    def greet(o, _):
        signal(barrier, at(rmod(me + o, 32)))
        return 0

    lax.fori_loop(1, 32, greet, 0)
    pl.semaphore_wait(barrier, 31)

    def send1(o, _):
        to = rmod(me + o, 32)
        remote(x_ref.at[to], parts.at[me], s1.at[o], r1.at[o], at(to)).start()
        return 0

    own = pltpu.make_async_copy(x_ref.at[me], parts.at[me], loc.at[0])
    own.start()
    lax.fori_loop(1, 32, send1, 0)
    own.wait()

    def wait1(o, _):
        to, came = rmod(me + o, 32), rmod(me + 32 - o, 32)
        copy = remote(x_ref.at[to], parts.at[came], s1.at[o], r1.at[o], at(to))
        copy.wait_recv()
        copy.wait_send()
        return 0

    lax.fori_loop(1, 32, wait1, 0)
    total = parts[0]
    for i in range(1, 32):
        total = total + parts[i]
    mine[...] = total

    def send2(o, _):
        to = rmod(me + o, 32)
        remote(mine, out_ref.at[me], s2.at[o], r2.at[o], at(to)).start()
        return 0

    lax.fori_loop(1, 32, send2, 0)
    own = pltpu.make_async_copy(mine, out_ref.at[me], loc.at[0])
    own.start()
    own.wait()

    def wait2(o, _):
        to, came = rmod(me + o, 32), rmod(me + 32 - o, 32)
        copy = remote(mine, out_ref.at[came], s2.at[o], r2.at[o], at(to))
        copy.wait_recv()
        copy.wait_send()
        return 0

    lax.fori_loop(1, 32, wait2, 0)


def total_stage(x):
    vm = pl.BlockSpec(memory_space=pltpu.VMEM)
    dma = pltpu.SemaphoreType.DMA
    return pl.pallas_call(
        total_kernel,
        out_shape=jax.ShapeDtypeStruct((32, 8, 128), F32),
        in_specs=[vm],
        out_specs=vm,
        scratch_shapes=[
            pltpu.VMEM((32, 8, 128), F32), pltpu.VMEM((8, 128), F32),
            dma((32,)), dma((32,)), dma((32,)), dma((32,)), dma((1,)),
        ],
        compiler_params=pltpu.CompilerParams(collective_id=3, has_side_effects=True),
        name="total_stage",
    )(x)


def normalize(values_in):
    average = jnp.mean(values_in, -1, keepdims=True)
    centered = values_in - average
    variance = jnp.mean(centered * centered, -1, keepdims=True)
    return centered * lax.rsqrt(variance + EPSILON)


def normalize_grad(values_in, upstream):
    average = jnp.mean(values_in, -1, keepdims=True)
    centered = values_in - average
    variance = jnp.mean(centered * centered, -1, keepdims=True)
    inv_std = lax.rsqrt(variance + EPSILON)
    unit_rows = centered * inv_std
    return inv_std * (
        upstream
        - jnp.mean(upstream, -1, keepdims=True)
        - unit_rows * jnp.mean(upstream * unit_rows, -1, keepdims=True)
    )


def pad_last(x, size):
    return jnp.pad(x, [(0, 0)] * (x.ndim - 1) + [(0, size - x.shape[-1])])


def lanes(x):
    x = pad_last(x, 64).reshape(2, 4, 64, 64)
    return jnp.concatenate([x[0], x[1]], -1)


def unlanes(x):
    x = x.reshape(4, 64, 128)
    return jnp.concatenate([x[:, :, :48], x[:, :, 64:112]], 0)


def on_device(
    pair_in, residue_index, chain_index, token_mask, relpos_weight, tri_proj, tri_out, bias_proj,
    single, ada_proj, noisy, qkv_proj, out_proj, cotangent,
):
    row, col = lax.axis_index("row"), lax.axis_index("col")
    row_at, col_at = row * 64, col * 32

    def rows_of(x):
        return lax.dynamic_slice_in_dim(x, row_at, 64)

    def cols_of(x):
        return lax.dynamic_slice_in_dim(x, col_at, 32)

    mask_f = token_mask.astype(F32)
    maskp = (
        jnp.swapaxes(cols_of(mask_f).reshape(2, 16), 0, 1)[:, :, None] * rows_of(mask_f)[None, None]
    ).reshape(16, 128)
    resr = jnp.broadcast_to(rows_of(residue_index)[:, None], (64, 128))
    chr_ = jnp.broadcast_to(rows_of(chain_index)[:, None], (64, 128))
    resc = jnp.broadcast_to(cols_of(residue_index)[:, None], (32, 128))
    chc = jnp.broadcast_to(cols_of(chain_index)[:, None], (32, 128))
    relpos = jnp.pad(relpos_weight, ((0, 128 - REL_BINS), (0, 0)))

    cvec = normalize(single.astype(F32)).astype(BF16)
    conditioning = jnp.dot(cvec, ada_proj, preferred_element_type=F32)
    ada_scale = jax.nn.sigmoid(conditioning[:, :768])
    ada_shift = conditioning[:, 768:1536]
    feat_at = col * 48
    gate_block = jax.nn.sigmoid(
        lax.dynamic_slice_in_dim(conditioning, 1536 + feat_at, 48, 1)
    )
    normed_in = normalize(noisy.astype(F32))
    hidden = (ada_scale * normed_in + ada_shift).astype(BF16).reshape(512, 768)
    wqkv = pad_last(qkv_proj, 64).reshape(768, 192)
    qkv = jnp.dot(hidden, wqkv, preferred_element_type=F32).astype(BF16)
    q = qkv[:, :64].reshape(8, 64, 64)
    qd = jnp.concatenate([q, q], -1)
    kv = (
        qkv[:, 64:].reshape(8, 2, 2, 16, 2, 64).transpose(4, 0, 1, 3, 2, 5).reshape(2, 8, 32, 128)
    )
    grad_in = cotangent.astype(F32)
    dmx = lanes((grad_in * gate_block).astype(BF16)).reshape(256, 128)

    pair_out, bias, kv_all, dmx_all = pair_stage(
        pair_in, resr, chr_, resc, chc, maskp, relpos, tri_proj, tri_out, bias_proj, kv, dmx
    )

    wout = jnp.pad(
        jnp.swapaxes(out_proj.reshape(48, 16, 48), 0, 1), ((0, 0), (0, 16), (0, 16))
    )
    wout = jnp.concatenate([wout, wout], -1)
    keyok = jnp.swapaxes(token_mask.reshape(16, 2, 16), 1, 2).reshape(256, 2)
    keyok = jnp.repeat(keyok, 64, 1)
    mixed_p, dq, dkv, grad_pair = attention_stage(
        qd, kv_all, dmx_all, wout, bias, keyok, bias_proj
    )
    mixed = unlanes(mixed_p)
    noisy_block = lax.dynamic_slice_in_dim(noisy, feat_at, 48, 2)
    block_out = (noisy_block.astype(F32) + gate_block * mixed).astype(BF16)
    d_gate = jnp.sum(grad_in * mixed, 0) * gate_block * (1.0 - gate_block)
    dkv = (
        dkv.reshape(4, 2, 2, 2, 16, 2, 64).transpose(2, 0, 3, 5, 4, 1, 6).reshape(512, 128)
    )
    d_qkv = jnp.concatenate([dq.reshape(512, 128)[:, :64], dkv], 1)
    d_hidden = dg(d_qkv, wqkv, 1, 1).reshape(8, 64, 768)
    d_scale = jnp.sum(d_hidden * normed_in, 0) * ada_scale * (1.0 - ada_scale)
    d_shift = jnp.sum(d_hidden, 0)
    w_gate = lax.dynamic_slice_in_dim(ada_proj, 1536 + feat_at, 48, 1)
    grads = jnp.concatenate([d_scale, d_shift, d_gate], 1)
    weights = jnp.concatenate([ada_proj[:, :1536], w_gate], 1)
    coarse = grads.astype(BF16)
    fine = (grads - coarse.astype(F32)).astype(BF16)
    d_cvec = dg(jnp.concatenate([coarse, fine], 0), weights, 1, 1)
    d_cvec = d_cvec[:64] + d_cvec[64:]
    d_cvec = total_stage(pad_last(d_cvec, 512).reshape(32, 8, 128)).reshape(64, 512)[:, :384]
    grad_single = normalize_grad(single.astype(F32), d_cvec)
    return pair_out, block_out, grad_pair.reshape(64, 32, 128), grad_single


def solution(mesh):
    return jax.shard_map(
        on_device,
        mesh=mesh,
        in_specs=(
            P("row", "col", None), P(), P(), P(), P(), P(), P(), P(), P("row", None), P(),
            P("samp", "row", None), P(None, None, "col"), P("col", None), P("samp", "row", "col"),
        ),
        out_specs=(
            P("row", "col", None), P("samp", "row", "col"), P("row", "col", None), P("row", None),
        ),
        check_vma=False,
    )
```

```python
import jax
import jax.numpy as jnp
from jax import lax
from jax.experimental import pallas as pl
from jax.experimental.pallas import tpu as pltpu
from jax.sharding import PartitionSpec as P

HEAD_DIM = 48
REL_BINS = 66
EPSILON = 1e-05
MESH = pl.DeviceIdType.MESH
F32 = jnp.float32
BF16 = jnp.bfloat16
NCOL = 16
NROW = 8


def dg(a, b, ca, cb, **kw):
    return lax.dot_general(a, b, (((ca,), (cb,)), ((), ())), preferred_element_type=F32, **kw)


def place():
    return lax.axis_index("row"), lax.axis_index("col"), lax.axis_index("samp")


def rmod(a, n):
    return lax.rem(a, n)


def ring_shift(oz, dest_core):
    if oz == 2:
        return 2 + 4 * dest_core
    return (0, 1, None, 7)[oz]


def row_dest(oz, cx):
    row, col, samp = place()
    z, core = samp * 4 + row // 2, rmod(row, 2)
    to_core = rmod(core + cx, 2)
    to_z = rmod(z + ring_shift(oz, to_core), 8)
    return rmod(to_z, 4) * 2 + to_core, col, to_z // 4


def row_source(oz, cx):
    row, col, samp = place()
    z, core = samp * 4 + row // 2, rmod(row, 2)
    from_core = rmod(core + cx, 2)
    from_z = rmod(z + 8 - ring_shift(oz, core), 8)
    return rmod(from_z, 4) * 2 + from_core, col, from_z // 4


ROW_IDS = [(oz, cx) for oz in range(4) for cx in range(2) if (oz, cx) != (0, 0)]


def remote(src, dst, ssem, rsem, to):
    return pltpu.make_async_remote_copy(
        src_ref=src, dst_ref=dst, send_sem=ssem, recv_sem=rsem, device_id=to, device_id_type=MESH
    )


def col_start(src_of, slot_of, ssem, rsem):
    row, col, samp = place()

    def one(o, _):
        to = rmod(col + o, NCOL)
        remote(src_of(to), slot_of(col), ssem.at[o], rsem.at[o], (row, to, samp)).start()
        return 0

    lax.fori_loop(1, NCOL, one, 0)


def col_wait(src_of, slot_of, ssem, rsem, recv=True, send=True):
    row, col, samp = place()

    def one(o, _):
        to = rmod(col + o, NCOL)
        came = rmod(col + NCOL - o, NCOL)
        if recv:
            remote(src_of(to), slot_of(came), ssem.at[o], rsem.at[o], (row, to, samp)).wait_recv()
        if send:
            remote(src_of(to), slot_of(came), ssem.at[o], rsem.at[o], (row, to, samp)).wait_send()
        return 0

    lax.fori_loop(1, NCOL, one, 0)


def row_start(src_of, slot_of, ssem, rsem):
    row = lax.axis_index("row")
    for oz, cx in ROW_IDS:
        to = row_dest(oz, cx)
        i = oz * 2 + cx
        remote(src_of(to[0]), slot_of(row), ssem.at[i], rsem.at[i], to).start()


def row_wait(src_of, slot_of, ssem, rsem, recv=True, send=True):
    for oz, cx in ROW_IDS:
        to, came = row_dest(oz, cx), row_source(oz, cx)
        i = oz * 2 + cx
        copy = remote(src_of(to[0]), slot_of(came[0]), ssem.at[i], rsem.at[i], to)
        if recv:
            copy.wait_recv()
        if send:
            copy.wait_send()


def signal(sem, to):
    pl.semaphore_signal(sem, inc=1, device_id=to, device_id_type=MESH)


def both(x, low, first):
    turned = pltpu.roll(x, 64, 1)
    return jnp.where(low, x, turned) if first else jnp.where(low, turned, x)


def layer_norm(x, axis):
    mean = jnp.mean(x, axis, keepdims=True)
    cent = x - mean
    var = jnp.mean(cent * cent, axis, keepdims=True)
    return cent * lax.rsqrt(var + EPSILON)


def two_parts(x):
    coarse = x.astype(BF16)
    return jnp.concatenate([coarse, (x - coarse.astype(F32)).astype(BF16)], 0)


def step_kernel(
    res_ref, chain_ref, mask_ref,
    pair_hbm, relpos_ref, tri_hbm, triout_ref, biasp_ref, single_ref, ada_hbm, noisy_hbm,
    qkvw_ref, outp_ref, cot_ref,
    pairout_ref, block_ref, gpair_ref, gsingle_ref,
    pair_in, tri_w, ada_w, noisy, idx_r, mrow, relpos_w,
    pf, gate, lrf, lbuf, recv_a, got, rcat, mtmp, tbuf, got_c, got_d, bias_f, bias_b, bias_got,
    cvec_s, scale_s, shift_s, wg_s, gate_t, g_t, noisy_t, normed, hidden, wqkv, q_t, kv_f,
    kv_own, kv_all, dmx_own, dmx_all, da_t, keyok, sraw, draw,
    mix_s, mix_r, dkv_s, dkv_m, dkv_o, dkv_r, dq_t, dkv_tok, dbias, db_s, db_r,
    dsc, dsh, dga, dc_s, dc_r, dc_p, gs_own, gs_all,
    sa, ra, sb, rb, sc, rc, sd, rd, se, re, skv, rkv, skf, rkf, sdm, rdm,
    sm, rm, sk, rk, sko, rko, sbb, rbb, st, rt, sp, rp_, sg, rg, loc, locm,
):
    row, col, samp = place()
    core = rmod(row, 2)
    zlo = row // 2
    mate = (row + 1 - 2 * core, col, samp)
    far = (row, col, 1 - samp)
    barrier = pltpu.get_barrier_semaphore()

    loads = [
        pltpu.make_async_copy(s, d, loc.at[10 + i])
        for i, (s, d) in enumerate(
            [(pair_hbm, pair_in), (tri_hbm, tri_w), (ada_hbm, ada_w), (noisy_hbm, noisy)]
        )
    ]
    for copy in loads:
        copy.start()
    for oz, cx in ROW_IDS:
        signal(barrier, row_source(oz, cx))

    def greet(o, _):
        signal(barrier, (row, rmod(col + o, NCOL), samp))
        return 0

    def greet_row(o, _):
        signal(barrier, (rmod(row + o, NROW), col, samp))
        return 0

    def greet_far(o, _):
        signal(barrier, (row, rmod(col + o, NCOL), 1 - samp))
        return 0

    lax.fori_loop(1, NCOL, greet, 0)
    lax.fori_loop(1, NROW, greet_row, 0)
    lax.fori_loop(0, NCOL, greet_far, 0)

    low = lax.broadcasted_iota(jnp.int32, (64, 128), 1) < 64
    low16 = lax.broadcasted_iota(jnp.int32, (16, 128), 1) < 64
    low1 = lax.broadcasted_iota(jnp.int32, (1, 128), 1) < 64
    diag = (lax.broadcasted_iota(jnp.int32, (128, 128), 0) < 64) == (
        lax.broadcasted_iota(jnp.int32, (128, 128), 1) < 64
    )

    def blockdiag(x):
        return jnp.where(diag, jnp.concatenate([x, x], 0), 0.0).astype(BF16)

    def indices(i, _):
        at = pl.ds(i, 1)
        idx_r[0, at, :] = jnp.full((1, 128), res_ref[row * 64 + i], jnp.int32)
        idx_r[1, at, :] = jnp.full((1, 128), chain_ref[row * 64 + i], jnp.int32)
        m = jnp.full((1, 128), mask_ref[row * 64 + i].astype(F32), F32)
        mrow[at, :] = m
        mrow[pl.ds(64 + i, 1), :] = m
        return 0

    lax.fori_loop(0, 64, indices, 0, unroll=4)
    mrow[...] = mrow[...].T
    relpos_w[...] = jnp.zeros_like(relpos_w)
    relpos_w[0:REL_BINS, :] = relpos_ref[...]
    loads[0].wait()

    def load(i, _):
        pf[pl.ds(i * 32, 32), :] = pair_in[i].astype(F32)
        return 0

    lax.fori_loop(0, 64, load, 0, unroll=4)
    loads[1].wait()
    bins = lax.broadcasted_iota(jnp.int32, (64, 128), 1)

    def stage1(lo, _):
        parts = []
        for hi in range(2):
            j = lo + 16 * hi
            off = jnp.clip(idx_r[0] - res_ref[col * 32 + j] + 32, 0, 64)
            bucket = jnp.where(idx_r[1] == chain_ref[col * 32 + j], off, REL_BINS - 1)
            onehot = jnp.where(bucket == bins, 1.0, 0.0).astype(BF16)
            parts.append(
                pf[pl.ds(j, 64, stride=32), :]
                + jnp.dot(onehot, relpos_w[...], preferred_element_type=F32)
            )
            pf[pl.ds(j, 64, stride=32), :] = parts[hi]
        zl = layer_norm(jnp.concatenate(parts, 0), -1).astype(BF16)
        pt = dg(tri_w[:, :512], zl, 0, 1)
        mask = mrow[0:1, :] * jnp.where(
            low1, mask_ref[col * 32 + lo].astype(F32), mask_ref[col * 32 + 16 + lo].astype(F32)
        )
        lrf[pl.ds(lo, 128, stride=16), :] = jax.nn.sigmoid(pt[128:256]) * pt[:128] * mask
        lrf[pl.ds(2048 + lo, 128, stride=16), :] = (
            jax.nn.sigmoid(pt[384:512]) * pt[256:384] * mask
        )
        gate[lo] = jax.nn.sigmoid(jnp.dot(zl, tri_w[:, 512:], preferred_element_type=F32))
        return 0

    lax.fori_loop(0, 16, stage1, 0, unroll=2)

    a_src = [lambda to, h=h: lbuf.at[h, to] for h in range(2)]
    a_slot = [lambda c, h=h: recv_a.at[h, c] for h in range(2)]
    b_src = [lambda r, h=h: recv_a.at[h, :, r] for h in range(2)]
    b_slot = [lambda r, h=h: got.at[h, r] for h in range(2)]
    own_a = [pltpu.make_async_copy(lbuf.at[h, col], recv_a.at[h, col], loc.at[h]) for h in range(2)]
    own_b = [
        pltpu.make_async_copy(recv_a.at[h, :, row], got.at[h, row], loc.at[2 + h])
        for h in range(2)
    ]
    for h in range(2):

        def pack(c, _):
            lbuf[h, c] = lrf[pl.ds(h * 2048 + c * 128, 128), :].astype(BF16).reshape(8, 16, 128)
            return 0

        lax.fori_loop(0, 16, pack, 0)
        if h == 0:
            pl.semaphore_wait(barrier, 7 + 15 + 7 + 16)
        own_a[h].start()
        col_start(a_src[h], a_slot[h], sa.at[h], ra.at[h])

    cvec = layer_norm(single_ref[...].astype(F32), -1).astype(BF16)
    cvec_s[...] = cvec
    wqkv[...] = jnp.zeros_like(wqkv)
    for p in range(3):
        wqkv[p * 64 : p * 64 + 48, :] = qkvw_ref[p]
    loads[2].wait()
    scale_s[...] = jax.nn.sigmoid(jnp.dot(cvec, ada_w[:, :768], preferred_element_type=F32))
    shift_s[...] = jnp.dot(cvec, ada_w[:, 768:1536], preferred_element_type=F32)
    loads[3].wait()

    def sample(s, _):
        at = pl.ds(pl.multiple_of(s * 64, 64), 64)
        n = layer_norm(noisy[at, :].astype(F32), -1)
        normed[at, :] = n
        hidden[at, :] = (scale_s[...] * n + shift_s[...]).astype(BF16)
        return 0

    lax.fori_loop(0, 8, sample, 0)
    kv_f[...] = dg(hidden[...], wqkv[64:, :], 1, 1)

    def kv_pack(t, _):
        r0 = kv_f[pl.ds(t * 32, 16), :]
        r1 = kv_f[pl.ds(t * 32 + 16, 16), :]
        to = pl.ds(pl.multiple_of(rmod(t, 2) * 16, 16), 16)
        kv_own[0, t // 2, to, :] = jnp.where(low16, r0, pltpu.roll(r1, 64, 1)).astype(BF16)
        kv_own[1, t // 2, to, :] = jnp.where(low16, pltpu.roll(r0, 64, 1), r1).astype(BF16)
        return 0

    lax.fori_loop(0, 16, kv_pack, 0, unroll=2)
    kv_keep = pltpu.make_async_copy(kv_own, kv_all.at[row], loc.at[4])
    kv_keep.start()
    kv_out = []
    for o in range(1, 4):
        to = (rmod(zlo + o, 4) * 2 + core, col, samp)
        kv_out.append(remote(kv_own, kv_all.at[row], skv.at[o], rkv.at[o], to))
    kv_mate = remote(kv_own, kv_all.at[row], skf.at[0], rkf.at[0], mate)

    own_a[0].wait()
    col_wait(a_src[0], a_slot[0], sa.at[0], ra.at[0])
    own_b[0].start()
    row_start(b_src[0], b_slot[0], sb.at[0], rb.at[0])
    kv_mate.start()
    for copy in kv_out:
        copy.start()

    feat = lax.broadcasted_iota(jnp.int32, (768, 64), 1)
    sel = jnp.where(
        (lax.broadcasted_iota(jnp.int32, (768, 64), 0) == col * 48 + feat) & (feat < 48), 1.0, 0.0
    ).astype(BF16)
    wg_s[...] = jnp.dot(ada_w[:, 1536:], sel, preferred_element_type=F32).astype(BF16)
    gate_t[...] = jax.nn.sigmoid(
        dg(wg_s[...], jnp.concatenate([cvec_s[...], cvec_s[...]], 0), 0, 1)
    )
    lane = lax.broadcasted_iota(jnp.int32, (64, 128), 1)
    tok = lax.broadcasted_iota(jnp.int32, (64, 128), 0)
    put = [jnp.where(lane == tok + 64 * h, 1.0, 0.0).astype(BF16) for h in range(2)]
    for u in range(4):
        g = jnp.dot(cot_ref[2 * u], put[0], preferred_element_type=F32) + jnp.dot(
            cot_ref[2 * u + 1], put[1], preferred_element_type=F32
        )
        g_t[u] = g
        dmx_own[:, u * 128 : u * 128 + 128] = (g * gate_t[:48, :]).astype(BF16)
    dm_src, dm_slot = (lambda to: dmx_own), (lambda c: dmx_all.at[c])
    dm_keep = pltpu.make_async_copy(dmx_own, dmx_all.at[col], loc.at[5])
    own_a[1].wait()
    col_wait(a_src[1], a_slot[1], sa.at[1], ra.at[1])
    own_b[1].start()
    row_start(b_src[1], b_slot[1], sb.at[1], rb.at[1])
    dm_keep.start()
    col_start(dm_src, dm_slot, sdm, rdm)
    q_t[...] = dg(wqkv[:64, :], hidden[...], 1, 1)
    noisy_t[...] = dg(sel, noisy[...], 0, 1)

    def key_mask(t, _):
        jb, lo = t // 16, rmod(t, 16)
        keyok[pl.ds(t, 1), :] = jnp.where(
            low1,
            mask_ref[jb * 32 + lo].astype(F32),
            mask_ref[jb * 32 + 16 + lo].astype(F32),
        )
        return 0

    lax.fori_loop(0, 256, key_mask, 0, unroll=4)

    for h in (1, 0):
        own_b[h].wait()
        row_wait(b_src[h], b_slot[h], sb.at[h], rb.at[h])

    def turn(r, _):
        rcat[pl.ds(pl.multiple_of(r * 128, 128), 128), :] = (
            got[1, r].reshape(256, 128).astype(F32).T.astype(BF16)
        )
        return 0

    lax.fori_loop(0, 8, turn, 0)

    def tri(rp, _):
        rhs = jnp.concatenate(
            [got[0, 2 * rp].reshape(256, 128), got[0, 2 * rp + 1].reshape(256, 128)], 1
        )
        mtmp[...] = jnp.dot(rcat[...], rhs, preferred_element_type=F32)

        def out(rj, _):
            for half in range(2):
                top = mtmp[pl.ds(rj * 128, 64), half * 128 : half * 128 + 128]
                bot = mtmp[pl.ds(rj * 128 + 64, 64), half * 128 : half * 128 + 128]
                for jh in range(2):
                    a = slice(jh * 32, jh * 32 + 16)
                    b = slice(jh * 32 + 16, jh * 32 + 32)
                    t = jnp.where(
                        low16,
                        top[a] + pltpu.roll(bot[a], 64, 1),
                        pltpu.roll(top[b], 64, 1) + bot[b],
                    )
                    tbuf[2 * rp + half, 2 * rj + jh] = t.astype(BF16)
            return 0

        lax.fori_loop(0, 8, out, 0, unroll=2)
        return 0

    lax.fori_loop(0, 4, tri, 0)

    c_src, c_slot = (lambda r: tbuf.at[r]), (lambda r: got_c.at[r])
    d_src, d_slot = (lambda c: got_c.at[:, c]), (lambda c: got_d.at[c])
    own_c = pltpu.make_async_copy(tbuf.at[row], got_c.at[row], loc.at[6])
    own_c.start()
    row_start(c_src, c_slot, sc, rc)

    for o in range(1, 4):
        came = rmod(zlo + 4 - o, 4) * 2 + core
        remote(kv_own, kv_all.at[came], skv.at[o], rkv.at[o], mate).wait_recv()
        remote(kv_all.at[came], kv_all.at[came], skf.at[o], rkf.at[o], mate).start()

    dm_keep.wait()
    col_wait(dm_src, dm_slot, sdm, rdm)
    da_t[...] = jnp.zeros_like(da_t)
    da_t[:48, :] = (
        jnp.dot(outp_ref[...], dmx_all[...].reshape(768, 512), preferred_element_type=F32)
        .astype(BF16)
        .astype(F32)
    )
    own_c.wait()
    row_wait(c_src, c_slot, sc, rc)
    own_d = pltpu.make_async_copy(got_c.at[:, col], got_d.at[col], loc.at[7])
    own_d.start()
    col_start(d_src, d_slot, sd, rd)

    kv_keep.wait()
    for copy in kv_out:
        copy.wait_send()
    kv_mate.wait_send()
    for o in range(4):
        came = rmod(zlo + 4 - o, 4) * 2
        remote(
            kv_all.at[came + core], kv_all.at[came + 1 - core], skf.at[o], rkf.at[o], mate
        ).wait_recv()
        if o > 0:
            remote(
                kv_all.at[came + core], kv_all.at[came + core], skf.at[o], rkf.at[o], mate
            ).wait_send()

    def half_of(ref, u, sh):
        tile = ref[:, pl.ds(pl.multiple_of(u * 128, 128), 128)].astype(F32)
        return blockdiag(both(tile, low, sh == 0))

    def keys(which, s):
        return jnp.concatenate([kv_all[r, which, s] for r in range(NROW)], 0)

    def raw(u, _):
        for sh in range(2):
            s = 2 * u + sh
            sraw[s] = jnp.dot(keys(0, s), half_of(q_t, u, sh), preferred_element_type=F32)
            draw[s] = jnp.dot(keys(1, s), half_of(da_t, u, sh), preferred_element_type=F32)
        return 0

    lax.fori_loop(0, 4, raw, 0)
    own_d.wait()
    col_wait(d_src, d_slot, sd, rd)

    def widen(c, _):
        lrf[pl.ds(c * 128, 128), :] = got_d[c].reshape(128, 128).astype(F32)
        return 0

    lax.fori_loop(0, 16, widen, 0)

    def stage3(lo, _):
        tn = layer_norm(lrf[pl.ds(lo, 128, stride=16), :], 0).astype(BF16)
        upd = dg(tn, triout_ref[...], 0, 0) * gate[lo]
        outs = []
        for hi in range(2):
            at = pl.ds(lo + 16 * hi, 64, stride=32)
            val = (pf[at, :] + upd[hi * 64 : hi * 64 + 64]).astype(BF16)
            pf[at, :] = val.astype(F32)
            outs.append(val)
        bias_f[pl.ds(lo, 16, stride=16), :] = dg(biasp_ref[...], jnp.concatenate(outs, 0), 1, 1)
        return 0

    lax.fori_loop(0, 16, stage3, 0, unroll=2)
    bias_b[...] = bias_f[...].astype(BF16).reshape(16, 16, 128)
    e_src, e_slot = (lambda c: bias_b.at[c]), (lambda c: bias_got.at[c])
    own_e = pltpu.make_async_copy(bias_b.at[col], bias_got.at[col], loc.at[8])
    own_e.start()
    col_start(e_src, e_slot, se, re)

    def store(i, _):
        pairout_ref[i] = pf[pl.ds(i * 32, 32), :].astype(BF16)
        return 0

    lax.fori_loop(0, 64, store, 0, unroll=4)
    dbias[...] = jnp.zeros_like(dbias)
    own_e.wait()
    col_wait(e_src, e_slot, se, re)

    scale = 1.0 / HEAD_DIM**0.5

    def mix_src(u):
        return lambda f: mix_s.at[u, f]

    def mix_slot(u):
        return lambda h: mix_r.at[u, h]

    def to_mate(u):
        return remote(dkv_s.at[:, 1 - core, u], dkv_m.at[u], sk.at[u], rk.at[u], mate)

    def to_chip(u, o):
        z = rmod(zlo + o, 4)
        return remote(
            dkv_o.at[u, z], dkv_r.at[u, zlo], sko.at[u, o], rko.at[u, o], (z * 2 + core, col, samp)
        )

    def pass_on(u):
        to_mate(u).wait_recv()
        for z in range(4):
            dkv_o[u, z] = (
                dkv_s[z, core, u].astype(F32) + dkv_m[u, z].astype(F32)
            ).astype(BF16)
        for o in range(1, 4):
            to_chip(u, o).start()

    def pair_of_samples(u, _):
        folded, dqs = [], []
        for sh in range(2):
            s = 2 * u + sh
            kp, vp = keys(0, s), keys(1, s)
            qq, dd = half_of(q_t, u, sh), half_of(da_t, u, sh)
            sco = sraw[s] * scale + bias_got[...].reshape(256, 128).astype(F32)
            sco = jnp.where(keyok[...] > 0, sco, -1000000000.0)
            top = jnp.max(sco, 0, keepdims=True)
            top = jnp.maximum(top, pltpu.roll(top, 64, 1))
            ex = jnp.exp(sco - top)
            tot = jnp.sum(ex, 0, keepdims=True)
            probs = ex * (1.0 / (tot + pltpu.roll(tot, 64, 1)))
            pb = probs.astype(BF16)
            folded.append(dg(vp, pb, 0, 0))
            dp = draw[s]
            dot = jnp.sum(probs * dp, 0, keepdims=True)
            ds = probs * (dp - (dot + pltpu.roll(dot, 64, 1)))
            dbias[...] += ds
            dsb = (ds * scale).astype(BF16)
            dqs.append(dg(kp, dsb, 0, 0))
            dk = dg(dsb, qq, 1, 1).astype(BF16)
            dv = dg(pb, dd, 1, 1).astype(BF16)
            for r in range(NROW):
                dkv_s[r // 2, r % 2, u, sh] = dk[r * 32 : r * 32 + 32]
                dkv_s[r // 2, r % 2, u, 2 + sh] = dv[r * 32 : r * 32 + 32]

        def fold(m0, m1):
            return jnp.where(
                low,
                m0[:64] + pltpu.roll(m0[64:], 64, 1),
                pltpu.roll(m1[:64], 64, 1) + m1[64:],
            ).astype(BF16)

        att = fold(*folded)
        dq_t[u] = fold(*dqs)
        mix_s[u] = dg(outp_ref[...], att[:48], 0, 0).astype(BF16).reshape(16, 48, 128)
        pltpu.make_async_copy(mix_s.at[u, col], mix_r.at[u, col], locm.at[u]).start()
        to_mate(u).start()
        col_start(mix_src(u), mix_slot(u), sm.at[u], rm.at[u])

        @pl.when(u > 0)
        def _():
            pass_on(u - 1)

        return 0

    lax.fori_loop(0, 4, pair_of_samples, 0)

    db_s[...] = dbias[...].reshape(16, 16, 128)
    own_db = pltpu.make_async_copy(db_s.at[col], db_r.at[samp, col], loc.at[9])
    own_db.start()

    def db_copy(o):
        to = rmod(col + o, NCOL)
        return remote(
            db_s.at[to], db_r.at[samp, col], sbb.at[1, o], rbb.at[1, o], (row, to, 1 - samp)
        )

    def db_send(o, _):
        db_copy(o).start()
        return 0

    pass_on(3)
    lax.fori_loop(0, NCOL, db_send, 0)
    near_src, near_slot = (lambda c: db_s.at[c]), (lambda c: db_r.at[samp, c])
    col_start(near_src, near_slot, sbb.at[0], rbb.at[0])

    dga[...] = jnp.zeros_like(dga)

    def mixed_of(u, _):
        pltpu.make_async_copy(mix_s.at[u, col], mix_r.at[u, col], locm.at[u]).wait()
        col_wait(mix_src(u), mix_slot(u), sm.at[u], rm.at[u])
        total = mix_r[u, 0].astype(F32)
        for h in range(1, NCOL):
            total = total + mix_r[u, h].astype(F32)
        lanes = pl.ds(pl.multiple_of(u * 128, 128), 128)
        out = noisy_t[:48, lanes] + gate_t[:48, :] * total
        block_ref[2 * u] = out[:, :64].astype(BF16)
        block_ref[2 * u + 1] = pltpu.roll(out, 64, 1)[:, :64].astype(BF16)
        dga[:48, :] += g_t[u] * total
        return 0

    lax.fori_loop(0, 4, mixed_of, 0)

    dsc[...] = jnp.zeros_like(dsc)
    dsh[...] = jnp.zeros_like(dsh)

    def hidden_grad(u, _):
        to_mate(u).wait_send()
        for o in range(1, 4):
            came = rmod(zlo + 4 - o, 4)
            remote(
                dkv_o.at[u, came], dkv_r.at[u, came], sko.at[u, o], rko.at[u, o], mate
            ).wait_recv()
            to_chip(u, o).wait_send()
        dkv_r[u, zlo] = dkv_o[u, zlo]
        tot = dkv_r[u, 0].astype(F32)
        for z in range(1, 4):
            tot = tot + dkv_r[u, z].astype(F32)
        for sh in range(2):
            for jb in range(2):
                a = tot[sh, jb * 16 : jb * 16 + 16]
                b = tot[2 + sh, jb * 16 : jb * 16 + 16]
                base = sh * 64 + jb * 32
                dkv_tok[base : base + 16, :] = jnp.where(low16, a, pltpu.roll(b, 64, 1)).astype(BF16)
                dkv_tok[base + 16 : base + 32, :] = jnp.where(
                    low16, pltpu.roll(a, 64, 1), b
                ).astype(BF16)
        dh = dg(dq_t[u], wqkv[:64, :], 0, 0) + jnp.dot(
            dkv_tok[...], wqkv[64:, :], preferred_element_type=F32
        )
        n = normed[pl.ds(pl.multiple_of(u * 128, 128), 128), :]
        w = dh * n
        dsc[...] += w[:64] + w[64:]
        dsh[...] += dh[:64] + dh[64:]
        return 0

    lax.fori_loop(0, 4, hidden_grad, 0)
    sg_ = scale_s[...]
    part = dg(two_parts(dsc[...] * sg_ * (1.0 - sg_)), ada_w[:, :768], 1, 1)
    part = part + dg(two_parts(dsh[...]), ada_w[:, 768:1536], 1, 1)
    part = part[:64] + part[64:]
    acc = dga[...]
    acc = (acc + pltpu.roll(acc, 64, 1)) * gate_t[...] * (1.0 - gate_t[...])
    coarse = acc.astype(BF16)
    fine = (acc - coarse.astype(F32)).astype(BF16)
    part = part + (dg(coarse, wg_s[...], 0, 1) + dg(fine, wg_s[...], 0, 1))[:64]
    dc_s[...] = part.reshape(8, 8, 384)

    half_col = col // 2
    even = rmod(col, 2) == 0

    def part_copy(o):
        g = rmod(half_col + o, 8)
        return remote(dc_s.at[g], dc_r.at[col], st.at[o], rt.at[col], (row, 2 * g, samp))

    @pl.when(jnp.logical_not(even))
    def _():
        part_copy(0).start()

    def part_send(o, _):
        part_copy(o).start()
        return 0

    lax.fori_loop(1, 8, part_send, 0)

    def own_copy(o):
        return remote(
            gs_own, gs_all.at[half_col], sg.at[o], rg.at[half_col], (row, rmod(col + o, NCOL), samp)
        )

    @pl.when(even)
    def _():
        dc_r[col] = dc_s[half_col]

        def arrived(o, _):
            came = rmod(col + o, NCOL)
            remote(dc_s.at[0], dc_r.at[came], st.at[0], rt.at[came], far).wait_recv()
            return 0

        lax.fori_loop(1, NCOL, arrived, 0)
        tot = dc_r[0]
        for c in range(1, NCOL):
            tot = tot + dc_r[c]
        dc_p[samp] = tot
        other = remote(dc_p.at[samp], dc_p.at[samp], sp.at[0], rp_.at[0], far)
        other.start()
        own = single_ref[...].astype(F32).reshape(8, 8, 384)
        mine = jnp.zeros((8, 384), F32)
        for g in range(8):
            mine = mine + jnp.where(half_col == g, own[g], 0.0)
        mean = jnp.mean(mine, -1, keepdims=True)
        cent = mine - mean
        inv = lax.rsqrt(jnp.mean(cent * cent, -1, keepdims=True) + EPSILON)
        unit = cent * inv
        remote(dc_p.at[samp], dc_p.at[1 - samp], sp.at[0], rp_.at[0], far).wait_recv()
        other.wait_send()
        up = dc_p[0] + dc_p[1]
        gs_own[...] = inv * (
            up - jnp.mean(up, -1, keepdims=True) - unit * jnp.mean(up * unit, -1, keepdims=True)
        )

        def tell(o, _):
            own_copy(o).start()
            return 0

        lax.fori_loop(1, NCOL, tell, 0)
        gs_all[half_col] = gs_own[...]

    own_db.wait()
    col_wait(near_src, near_slot, sbb.at[0], rbb.at[0])

    def db_wait(o, _):
        came = rmod(col + NCOL - o, NCOL)
        remote(db_s.at[came], db_r.at[1 - samp, came], sbb.at[1, o], rbb.at[1, o], far).wait_recv()
        db_copy(o).wait_send()
        return 0

    lax.fori_loop(0, NCOL, db_wait, 0)
    dbias[...] = (db_r[0] + db_r[1]).reshape(256, 128)
    biasp3 = jnp.concatenate([biasp_ref[...]] * 3, 0)

    def grad(lo, _):
        d = dbias[pl.ds(lo, 16, stride=16), :]
        d1 = d.astype(BF16)
        rest = d - d1.astype(F32)
        d2 = rest.astype(BF16)
        d3 = (rest - d2.astype(F32)).astype(BF16)
        g = dg(jnp.concatenate([d1, d2, d3], 0), biasp3, 0, 0)
        for hi in range(2):
            gpair_ref[pl.ds(lo + 16 * hi, 64, stride=32), :] = g[hi * 64 : hi * 64 + 64]
        return 0

    lax.fori_loop(0, 16, grad, 0, unroll=2)

    @pl.when(jnp.logical_not(even))
    def _():
        part_copy(0).wait_send()

    def part_sent(o, _):
        part_copy(o).wait_send()
        return 0

    lax.fori_loop(1, 8, part_sent, 0)

    @pl.when(even)
    def _():
        def told(o, _):
            own_copy(o).wait_send()
            return 0

        lax.fori_loop(1, NCOL, told, 0)

    def total_came(g):
        remote(gs_own, gs_all.at[g], sg.at[0], rg.at[g], far).wait_recv()

    @pl.when(jnp.logical_not(even))
    def _():
        total_came(half_col)

    def came_from(o, _):
        total_came(rmod(half_col + o, 8))
        return 0

    lax.fori_loop(1, 8, came_from, 0)
    gsingle_ref[...] = gs_all[...].reshape(64, 384)


def on_device(
    pair_in, residue_index, chain_index, token_mask, relpos_weight, tri_proj, tri_out, bias_proj,
    single, ada_proj, noisy, qkv_proj, out_proj, cotangent,
):
    vm = pl.BlockSpec(memory_space=pltpu.VMEM)
    sm = pl.BlockSpec(memory_space=pltpu.SMEM)
    hbm = pl.BlockSpec(memory_space=pl.ANY)
    dma = pltpu.SemaphoreType.DMA
    v = pltpu.VMEM
    pair_out, block_t, grad_pair, grad_single = pl.pallas_call(
        step_kernel,
        out_shape=(
            jax.ShapeDtypeStruct((64, 32, 128), BF16),
            jax.ShapeDtypeStruct((8, 48, 64), BF16),
            jax.ShapeDtypeStruct((2048, 128), F32),
            jax.ShapeDtypeStruct((64, 384), F32),
        ),
        in_specs=[sm, sm, sm, hbm, vm, hbm, vm, vm, vm, hbm, hbm, vm, vm, vm],
        out_specs=(vm,) * 4,
        scratch_shapes=[
            v((64, 32, 128), BF16), v((128, 640), BF16), v((384, 2304), BF16), v((512, 768), BF16),
            v((2, 64, 128), jnp.int32), v((128, 128), F32), v((128, 128), BF16),
            v((2048, 128), F32), v((16, 128, 128), F32), v((4096, 128), F32),
            v((2, 16, 8, 16, 128), BF16), v((2, 16, 8, 16, 128), BF16),
            v((2, 8, 16, 16, 128), BF16), v((1024, 256), BF16), v((1024, 256), F32),
            v((8, 16, 16, 128), BF16), v((8, 16, 16, 128), BF16), v((16, 8, 16, 128), BF16),
            v((256, 128), F32), v((16, 16, 128), BF16), v((16, 16, 128), BF16),
            v((64, 384), BF16), v((64, 768), F32), v((64, 768), F32), v((384, 64), BF16),
            v((64, 128), F32), v((4, 48, 128), F32), v((64, 512), F32), v((512, 768), F32),
            v((512, 768), BF16), v((192, 768), BF16), v((64, 512), F32), v((512, 128), F32),
            v((2, 8, 32, 128), BF16), v((8, 2, 8, 32, 128), BF16), v((48, 512), BF16),
            v((16, 48, 512), BF16), v((64, 512), F32), v((256, 128), F32), v((8, 256, 128), F32),
            v((8, 256, 128), F32),
            v((4, 16, 48, 128), BF16), v((4, 16, 48, 128), BF16), v((4, 2, 4, 4, 32, 128), BF16),
            v((4, 4, 4, 32, 128), BF16), v((4, 4, 4, 32, 128), BF16), v((4, 4, 4, 32, 128), BF16),
            v((4, 64, 128), BF16), v((128, 128), BF16), v((256, 128), F32), v((16, 16, 128), F32),
            v((2, 16, 16, 128), F32),
            v((64, 768), F32), v((64, 768), F32), v((64, 128), F32), v((8, 8, 384), F32),
            v((16, 8, 384), F32), v((2, 8, 384), F32), v((8, 384), F32), v((8, 8, 384), F32),
            dma((2, 16)), dma((2, 16)), dma((2, 8)), dma((2, 8)), dma((8,)), dma((8,)),
            dma((16,)), dma((16,)), dma((16,)), dma((16,)), dma((4,)), dma((4,)),
            dma((4,)), dma((4,)), dma((16,)), dma((16,)),
            dma((4, 16)), dma((4, 16)), dma((4,)), dma((4,)), dma((4, 4)), dma((4, 4)),
            dma((2, 16)), dma((2, 16)), dma((8,)), dma((16,)), dma((1,)), dma((1,)),
            dma((16,)), dma((8,)), dma((14,)), dma((4,)),
        ],
        compiler_params=pltpu.CompilerParams(
            collective_id=1, has_side_effects=True, vmem_limit_bytes=60 * 1024 * 1024
        ),
        name="step",
    )(
        residue_index, chain_index, token_mask, pair_in, relpos_weight, tri_proj, tri_out,
        bias_proj.T, single, ada_proj, noisy.reshape(512, 768), qkv_proj.transpose(1, 2, 0),
        out_proj, cotangent.transpose(0, 2, 1),
    )
    return pair_out, block_t.transpose(0, 2, 1), grad_pair.reshape(64, 32, 128), grad_single


def solution(mesh):
    return jax.shard_map(
        on_device,
        mesh=mesh,
        in_specs=(
            P("row", "col", None), P(), P(), P(), P(), P(), P(), P(), P("row", None), P(),
            P("samp", "row", None), P(None, None, "col"), P("col", None), P("samp", "row", "col"),
        ),
        out_specs=(
            P("row", "col", None), P("samp", "row", "col"), P("row", "col", None), P("row", None),
        ),
        check_vma=False,
    )
```

```python
import jax
import jax.numpy as jnp
from jax import lax
from jax.experimental import pallas as pl
from jax.experimental.pallas import tpu as pltpu
from jax.sharding import PartitionSpec as P

HEAD_DIM = 48
REL_BINS = 66
EPSILON = 1e-05
MESH = pl.DeviceIdType.MESH
F32 = jnp.float32
BF16 = jnp.bfloat16
NCOL = 16
NROW = 8


def dg(a, b, ca, cb, **kw):
    return lax.dot_general(a, b, (((ca,), (cb,)), ((), ())), preferred_element_type=F32, **kw)


def place():
    return lax.axis_index("row"), lax.axis_index("col"), lax.axis_index("samp")


def rmod(a, n):
    return lax.rem(a, n)


def ring_shift(oz, dest_core):
    if oz == 2:
        return 2 + 4 * dest_core
    return (0, 1, None, 7)[oz]


def row_dest(oz, cx):
    row, col, samp = place()
    z, core = samp * 4 + row // 2, rmod(row, 2)
    to_core = rmod(core + cx, 2)
    to_z = rmod(z + ring_shift(oz, to_core), 8)
    return rmod(to_z, 4) * 2 + to_core, col, to_z // 4


def row_source(oz, cx):
    row, col, samp = place()
    z, core = samp * 4 + row // 2, rmod(row, 2)
    from_core = rmod(core + cx, 2)
    from_z = rmod(z + 8 - ring_shift(oz, core), 8)
    return rmod(from_z, 4) * 2 + from_core, col, from_z // 4


ROW_IDS = [(oz, cx) for oz in range(4) for cx in range(2) if (oz, cx) != (0, 0)]


def remote(src, dst, ssem, rsem, to):
    return pltpu.make_async_remote_copy(
        src_ref=src, dst_ref=dst, send_sem=ssem, recv_sem=rsem, device_id=to, device_id_type=MESH
    )


def col_start(src_of, slot_of, ssem, rsem):
    row, col, samp = place()

    def one(o, _):
        to = rmod(col + o, NCOL)
        remote(src_of(to), slot_of(col), ssem.at[o], rsem.at[o], (row, to, samp)).start()
        return 0

    lax.fori_loop(1, NCOL, one, 0)


def col_wait(src_of, slot_of, ssem, rsem, recv=True, send=True):
    row, col, samp = place()

    def one(o, _):
        to = rmod(col + o, NCOL)
        came = rmod(col + NCOL - o, NCOL)
        if recv:
            remote(src_of(to), slot_of(came), ssem.at[o], rsem.at[o], (row, to, samp)).wait_recv()
        if send:
            remote(src_of(to), slot_of(came), ssem.at[o], rsem.at[o], (row, to, samp)).wait_send()
        return 0

    lax.fori_loop(1, NCOL, one, 0)


def row_start(src_of, slot_of, ssem, rsem):
    row = lax.axis_index("row")
    for oz, cx in ROW_IDS:
        to = row_dest(oz, cx)
        i = oz * 2 + cx
        remote(src_of(to[0]), slot_of(row), ssem.at[i], rsem.at[i], to).start()


def row_wait(src_of, slot_of, ssem, rsem, recv=True, send=True):
    for oz, cx in ROW_IDS:
        to, came = row_dest(oz, cx), row_source(oz, cx)
        i = oz * 2 + cx
        copy = remote(src_of(to[0]), slot_of(came[0]), ssem.at[i], rsem.at[i], to)
        if recv:
            copy.wait_recv()
        if send:
            copy.wait_send()


def signal(sem, to):
    pl.semaphore_signal(sem, inc=1, device_id=to, device_id_type=MESH)


def both(x, low, first):
    turned = pltpu.roll(x, 64, 1)
    return jnp.where(low, x, turned) if first else jnp.where(low, turned, x)


def layer_norm(x, axis):
    mean = jnp.mean(x, axis, keepdims=True)
    cent = x - mean
    var = jnp.mean(cent * cent, axis, keepdims=True)
    return cent * lax.rsqrt(var + EPSILON)


def two_parts(x):
    coarse = x.astype(BF16)
    return jnp.concatenate([coarse, (x - coarse.astype(F32)).astype(BF16)], 0)


def step_kernel(
    res_ref, chain_ref, mask_ref,
    pair_hbm, relpos_ref, tri_hbm, triout_ref, biasp_ref, single_ref, ada_hbm, noisy_hbm,
    qkvw_ref, outp_ref, cot_ref,
    pairout_hbm, block_hbm, gpair_hbm, gsingle_hbm,
    pairout_ref, block_ref, gpair_ref,
    pair_in, tri_w, ada_w, noisy, idx_r, mrow, relpos_w,
    zl_s, tri_t, pf, gate, lrf, lbuf, recv_a, got, rcat, mtmp, tbuf, got_c, got_d, bias_f, bias_b, bias_got,
    cvec_s, scale_s, shift_s, wg_s, gate_t, g_t, noisy_t, normed, hidden, wqkv, q_t, kv_f,
    kv_own, kv_all, dmx_own, dmx_all, da_t, keyok, sraw, draw,
    mix_s, mix_r, dkv_s, dkv_m, dkv_o, dkv_r, dq_t, dkv_tok, dbias, db_s, db_r,
    dsc, dsh, dga, dc_s, dc_r, dc_p, gs_own, gs_all,
    sa, ra, sb, rb, sc, rc, sd, rd, se, re, skv, rkv, skf, rkf, sdm, rdm,
    sm, rm, sk, rk, sko, rko, sbb, rbb, st, rt, sp, rp_, sg, rg, loc, locm,
):
    row, col, samp = place()
    core = rmod(row, 2)
    zlo = row // 2
    mate = (row + 1 - 2 * core, col, samp)
    far = (row, col, 1 - samp)
    barrier = pltpu.get_barrier_semaphore()

    loads = [
        pltpu.make_async_copy(s, d, loc.at[10 + i])
        for i, (s, d) in enumerate(
            [(pair_hbm, pair_in), (tri_hbm, tri_w), (ada_hbm, ada_w), (noisy_hbm, noisy)]
        )
    ]
    for copy in loads:
        copy.start()
    for oz, cx in ROW_IDS:
        signal(barrier, row_source(oz, cx))

    def greet(o, _):
        signal(barrier, (row, rmod(col + o, NCOL), samp))
        return 0

    def greet_row(o, _):
        signal(barrier, (rmod(row + o, NROW), col, samp))
        return 0

    def greet_far(o, _):
        signal(barrier, (row, rmod(col + o, NCOL), 1 - samp))
        return 0

    lax.fori_loop(1, NCOL, greet, 0)
    lax.fori_loop(1, NROW, greet_row, 0)
    lax.fori_loop(0, NCOL, greet_far, 0)

    low = lax.broadcasted_iota(jnp.int32, (64, 128), 1) < 64
    low16 = lax.broadcasted_iota(jnp.int32, (16, 128), 1) < 64
    low1 = lax.broadcasted_iota(jnp.int32, (1, 128), 1) < 64
    diag = (lax.broadcasted_iota(jnp.int32, (128, 128), 0) < 64) == (
        lax.broadcasted_iota(jnp.int32, (128, 128), 1) < 64
    )

    def blockdiag(x):
        return jnp.where(diag, jnp.concatenate([x, x], 0), 0.0).astype(BF16)

    def indices(i, _):
        at = pl.ds(i, 1)
        idx_r[0, at, :] = jnp.full((1, 128), res_ref[row * 64 + i], jnp.int32)
        idx_r[1, at, :] = jnp.full((1, 128), chain_ref[row * 64 + i], jnp.int32)
        m = jnp.full((1, 128), mask_ref[row * 64 + i].astype(F32), F32)
        mrow[at, :] = m
        mrow[pl.ds(64 + i, 1), :] = m
        return 0

    lax.fori_loop(0, 64, indices, 0, unroll=4)
    mrow[...] = mrow[...].T
    relpos_w[...] = jnp.zeros_like(relpos_w)
    relpos_w[0:REL_BINS, :] = relpos_ref[...]
    loads[0].wait()

    def load(i, _):
        pf[pl.ds(i * 32, 32), :] = pair_in[i].astype(F32)
        return 0

    lax.fori_loop(0, 64, load, 0, unroll=4)
    bins = lax.broadcasted_iota(jnp.int32, (64, 128), 1)

    def normed_rows(t, _):
        parts = []
        for q in range(2):
            for hi in range(2):
                j = 2 * t + q + 16 * hi
                off = jnp.clip(idx_r[0] - res_ref[col * 32 + j] + 32, 0, 64)
                bucket = jnp.where(idx_r[1] == chain_ref[col * 32 + j], off, REL_BINS - 1)
                onehot = jnp.where(bucket == bins, 1.0, 0.0).astype(BF16)
                parts.append(
                    pf[pl.ds(j, 64, stride=32), :]
                    + jnp.dot(onehot, relpos_w[...], preferred_element_type=F32)
                )
        for q in range(2):
            for hi in range(2):
                pf[pl.ds(2 * t + q + 16 * hi, 64, stride=32), :] = parts[2 * q + hi]
        at = pl.ds(pl.multiple_of(t * 256, 256), 256)
        zl_s[at, :] = layer_norm(jnp.concatenate(parts, 0), -1).astype(BF16)
        return 0

    lax.fori_loop(0, 8, normed_rows, 0)
    loads[1].wait()
    tri_t[...] = tri_w[:, :512].astype(F32).T.astype(BF16)

    def project(h, t):
        at = pl.ds(pl.multiple_of(t * 256, 256), 256)
        pt = dg(tri_t[h * 256 : h * 256 + 256, :], zl_s[at, :], 1, 1)
        val = jax.nn.sigmoid(pt[128:]) * pt[:128]
        for q in range(2):
            lo = 2 * t + q
            mask = mrow[0:1, :] * jnp.where(
                low1, mask_ref[col * 32 + lo].astype(F32), mask_ref[col * 32 + 16 + lo].astype(F32)
            )
            lrf[pl.ds(h * 2048 + lo, 128, stride=16), :] = val[:, q * 128 : q * 128 + 128] * mask

    a_src = [lambda to, h=h: lbuf.at[h, to] for h in range(2)]
    a_slot = [lambda c, h=h: recv_a.at[h, c] for h in range(2)]
    b_src = [lambda r, h=h: recv_a.at[h, :, r] for h in range(2)]
    b_slot = [lambda r, h=h: got.at[h, r] for h in range(2)]
    own_a = [pltpu.make_async_copy(lbuf.at[h, col], recv_a.at[h, col], loc.at[h]) for h in range(2)]
    own_b = [
        pltpu.make_async_copy(recv_a.at[h, :, row], got.at[h, row], loc.at[2 + h])
        for h in range(2)
    ]
    for h in range(2):

        def one_side(t, _):
            project(h, t)
            return 0

        lax.fori_loop(0, 8, one_side, 0)

        def pack(c, _):
            lbuf[h, c] = lrf[pl.ds(h * 2048 + c * 128, 128), :].astype(BF16).reshape(8, 16, 128)
            return 0

        lax.fori_loop(0, 16, pack, 0)
        if h == 0:
            pl.semaphore_wait(barrier, 7 + 15 + 7 + 16)
        own_a[h].start()
        col_start(a_src[h], a_slot[h], sa.at[h], ra.at[h])

    cvec = layer_norm(single_ref[...].astype(F32), -1).astype(BF16)
    cvec_s[...] = cvec
    wqkv[...] = jnp.zeros_like(wqkv)
    for p in range(3):
        wqkv[p * 64 : p * 64 + 48, :] = qkvw_ref[p]
    loads[2].wait()
    scale_s[...] = jax.nn.sigmoid(jnp.dot(cvec, ada_w[:, :768], preferred_element_type=F32))
    shift_s[...] = jnp.dot(cvec, ada_w[:, 768:1536], preferred_element_type=F32)
    loads[3].wait()

    def sample(s, _):
        at = pl.ds(pl.multiple_of(s * 64, 64), 64)
        n = layer_norm(noisy[at, :].astype(F32), -1)
        normed[at, :] = n
        hidden[at, :] = (scale_s[...] * n + shift_s[...]).astype(BF16)
        return 0

    lax.fori_loop(0, 8, sample, 0)
    own_a[0].wait()
    col_wait(a_src[0], a_slot[0], sa.at[0], ra.at[0])
    own_b[0].start()
    row_start(b_src[0], b_slot[0], sb.at[0], rb.at[0])

    feat = lax.broadcasted_iota(jnp.int32, (768, 64), 1)
    sel = jnp.where(
        (lax.broadcasted_iota(jnp.int32, (768, 64), 0) == col * 48 + feat) & (feat < 48), 1.0, 0.0
    ).astype(BF16)
    wg_s[...] = jnp.dot(ada_w[:, 1536:], sel, preferred_element_type=F32).astype(BF16)
    gate_t[...] = jax.nn.sigmoid(
        dg(wg_s[...], jnp.concatenate([cvec_s[...], cvec_s[...]], 0), 0, 1)
    )
    lane = lax.broadcasted_iota(jnp.int32, (64, 128), 1)
    tok = lax.broadcasted_iota(jnp.int32, (64, 128), 0)
    put = [jnp.where(lane == tok + 64 * h, 1.0, 0.0).astype(BF16) for h in range(2)]
    for u in range(4):
        g = jnp.dot(cot_ref[2 * u], put[0], preferred_element_type=F32) + jnp.dot(
            cot_ref[2 * u + 1], put[1], preferred_element_type=F32
        )
        g_t[u] = g
        dmx_own[:, u * 128 : u * 128 + 128] = (g * gate_t[:48, :]).astype(BF16)
    dm_src, dm_slot = (lambda to: dmx_own), (lambda c: dmx_all.at[c])
    dm_keep = pltpu.make_async_copy(dmx_own, dmx_all.at[col], loc.at[5])
    dm_keep.start()
    col_start(dm_src, dm_slot, sdm, rdm)
    kv_f[...] = dg(hidden[...], wqkv[64:, :], 1, 1)

    def kv_pack(t, _):
        r0 = kv_f[pl.ds(t * 32, 16), :]
        r1 = kv_f[pl.ds(t * 32 + 16, 16), :]
        to = pl.ds(pl.multiple_of(rmod(t, 2) * 16, 16), 16)
        kv_own[0, t // 2, to, :] = jnp.where(low16, r0, pltpu.roll(r1, 64, 1)).astype(BF16)
        kv_own[1, t // 2, to, :] = jnp.where(low16, pltpu.roll(r0, 64, 1), r1).astype(BF16)
        return 0

    lax.fori_loop(0, 16, kv_pack, 0, unroll=2)
    kv_keep = pltpu.make_async_copy(kv_own, kv_all.at[row], loc.at[4])
    kv_keep.start()
    kv_out = []
    for o in range(1, 4):
        to = (rmod(zlo + o, 4) * 2 + core, col, samp)
        kv_out.append(remote(kv_own, kv_all.at[row], skv.at[o], rkv.at[o], to))
    kv_mate = remote(kv_own, kv_all.at[row], skf.at[0], rkf.at[0], mate)
    own_a[1].wait()
    col_wait(a_src[1], a_slot[1], sa.at[1], ra.at[1])
    own_b[1].start()
    row_start(b_src[1], b_slot[1], sb.at[1], rb.at[1])
    kv_mate.start()
    for copy in kv_out:
        copy.start()

    def gates(t, _):
        at = pl.ds(pl.multiple_of(t * 256, 256), 256)
        gate[at, :] = jax.nn.sigmoid(
            jnp.dot(zl_s[at, :], tri_w[:, 512:], preferred_element_type=F32)
        )
        return 0

    lax.fori_loop(0, 8, gates, 0)
    q_t[...] = dg(wqkv[:64, :], hidden[...], 1, 1)
    noisy_t[...] = dg(sel, noisy[...], 0, 1)

    def key_mask(t, _):
        jb, lo = t // 16, rmod(t, 16)
        keyok[pl.ds(t, 1), :] = jnp.where(
            low1,
            mask_ref[jb * 32 + lo].astype(F32),
            mask_ref[jb * 32 + 16 + lo].astype(F32),
        )
        return 0

    lax.fori_loop(0, 256, key_mask, 0, unroll=4)

    for h in (1, 0):
        own_b[h].wait()
        row_wait(b_src[h], b_slot[h], sb.at[h], rb.at[h])

    def turn(r, _):
        rcat[pl.ds(pl.multiple_of(r * 128, 128), 128), :] = (
            got[1, r].reshape(256, 128).astype(F32).T.astype(BF16)
        )
        return 0

    lax.fori_loop(0, 8, turn, 0)

    c_src, c_slot = (lambda r: tbuf.at[r]), (lambda r: got_c.at[r])

    def tri(rp):
        rhs = jnp.concatenate(
            [got[0, 2 * rp].reshape(256, 128), got[0, 2 * rp + 1].reshape(256, 128)], 1
        )
        mtmp[...] = jnp.dot(rcat[...], rhs, preferred_element_type=F32)

        def out(rj, _):
            for half in range(2):
                top = mtmp[pl.ds(rj * 128, 64), half * 128 : half * 128 + 128]
                bot = mtmp[pl.ds(rj * 128 + 64, 64), half * 128 : half * 128 + 128]
                for jh in range(2):
                    a = slice(jh * 32, jh * 32 + 16)
                    b = slice(jh * 32 + 16, jh * 32 + 32)
                    t = jnp.where(
                        low16,
                        top[a] + pltpu.roll(bot[a], 64, 1),
                        pltpu.roll(top[b], 64, 1) + bot[b],
                    )
                    tbuf[2 * rp + half, 2 * rj + jh] = t.astype(BF16)
            return 0

        lax.fori_loop(0, 8, out, 0, unroll=2)

    own_c = pltpu.make_async_copy(tbuf.at[row], got_c.at[row], loc.at[6])
    for oz in (2, 1, 3, 0):
        tri(rmod(zlo + oz, 4))
        for cx in range(2):
            if (oz, cx) != (0, 0):
                to = row_dest(oz, cx)
                i = oz * 2 + cx
                remote(c_src(to[0]), c_slot(row), sc.at[i], rc.at[i], to).start()
    own_c.start()
    d_src, d_slot = (lambda c: got_c.at[:, c]), (lambda c: got_d.at[c])

    for o in range(1, 4):
        came = rmod(zlo + 4 - o, 4) * 2 + core
        remote(kv_own, kv_all.at[came], skv.at[o], rkv.at[o], mate).wait_recv()
        remote(kv_all.at[came], kv_all.at[came], skf.at[o], rkf.at[o], mate).start()

    dm_keep.wait()
    col_wait(dm_src, dm_slot, sdm, rdm)
    da_t[...] = jnp.zeros_like(da_t)
    da_t[:48, :] = (
        jnp.dot(outp_ref[...], dmx_all[...].reshape(768, 512), preferred_element_type=F32)
        .astype(BF16)
        .astype(F32)
    )
    own_c.wait()
    row_wait(c_src, c_slot, sc, rc)
    own_d = pltpu.make_async_copy(got_c.at[:, col], got_d.at[col], loc.at[7])
    own_d.start()
    col_start(d_src, d_slot, sd, rd)

    kv_keep.wait()
    for copy in kv_out:
        copy.wait_send()
    kv_mate.wait_send()
    for o in range(4):
        came = rmod(zlo + 4 - o, 4) * 2
        remote(
            kv_all.at[came + core], kv_all.at[came + 1 - core], skf.at[o], rkf.at[o], mate
        ).wait_recv()
        if o > 0:
            remote(
                kv_all.at[came + core], kv_all.at[came + core], skf.at[o], rkf.at[o], mate
            ).wait_send()

    def half_of(ref, u, sh):
        tile = ref[:, pl.ds(pl.multiple_of(u * 128, 128), 128)].astype(F32)
        return blockdiag(both(tile, low, sh == 0))

    def keys(which, s):
        return jnp.concatenate([kv_all[r, which, s] for r in range(NROW)], 0)

    def raw(u, _):
        for sh in range(2):
            s = 2 * u + sh
            sraw[s] = jnp.dot(keys(0, s), half_of(q_t, u, sh), preferred_element_type=F32)
            draw[s] = jnp.dot(keys(1, s), half_of(da_t, u, sh), preferred_element_type=F32)
        return 0

    lax.fori_loop(0, 4, raw, 0)
    own_d.wait()
    col_wait(d_src, d_slot, sd, rd)

    def widen(c, _):
        lrf[pl.ds(c * 128, 128), :] = got_d[c].reshape(128, 128).astype(F32)
        return 0

    lax.fori_loop(0, 16, widen, 0)

    def stage3(lo, _):
        tn = layer_norm(lrf[pl.ds(lo, 128, stride=16), :], 0).astype(BF16)
        upd = dg(tn, triout_ref[...], 0, 0) * gate[pl.ds(pl.multiple_of(lo * 128, 128), 128), :]
        outs = []
        for hi in range(2):
            at = pl.ds(lo + 16 * hi, 64, stride=32)
            val = (pf[at, :] + upd[hi * 64 : hi * 64 + 64]).astype(BF16)
            pf[at, :] = val.astype(F32)
            outs.append(val)
        bias_f[pl.ds(lo, 16, stride=16), :] = dg(biasp_ref[...], jnp.concatenate(outs, 0), 1, 1)
        return 0

    lax.fori_loop(0, 16, stage3, 0, unroll=2)
    bias_b[...] = bias_f[...].astype(BF16).reshape(16, 16, 128)
    e_src, e_slot = (lambda c: bias_b.at[c]), (lambda c: bias_got.at[c])
    own_e = pltpu.make_async_copy(bias_b.at[col], bias_got.at[col], loc.at[8])
    own_e.start()
    col_start(e_src, e_slot, se, re)

    def store(i, _):
        pairout_ref[i] = pf[pl.ds(i * 32, 32), :].astype(BF16)
        return 0

    lax.fori_loop(0, 64, store, 0, unroll=4)
    out_pair = pltpu.make_async_copy(pairout_ref, pairout_hbm, loc.at[14])
    out_pair.start()
    dbias[...] = jnp.zeros_like(dbias)
    own_e.wait()
    col_wait(e_src, e_slot, se, re)

    scale = 1.0 / HEAD_DIM**0.5

    def mix_src(u):
        return lambda f: mix_s.at[u, f]

    def mix_slot(u):
        return lambda h: mix_r.at[u, h]

    def to_mate(u):
        return remote(dkv_s.at[:, 1 - core, u], dkv_m.at[u], sk.at[u], rk.at[u], mate)

    def to_chip(u, o):
        z = rmod(zlo + o, 4)
        return remote(
            dkv_o.at[u, z], dkv_r.at[u, zlo], sko.at[u, o], rko.at[u, o], (z * 2 + core, col, samp)
        )

    def pass_on(u):
        to_mate(u).wait_recv()
        for z in range(4):
            dkv_o[u, z] = (
                dkv_s[z, core, u].astype(F32) + dkv_m[u, z].astype(F32)
            ).astype(BF16)
        for o in range(1, 4):
            to_chip(u, o).start()

    def pair_of_samples(u, _):
        folded, dqs = [], []
        for sh in range(2):
            s = 2 * u + sh
            kp, vp = keys(0, s), keys(1, s)
            qq, dd = half_of(q_t, u, sh), half_of(da_t, u, sh)
            sco = sraw[s] * scale + bias_got[...].reshape(256, 128).astype(F32)
            sco = jnp.where(keyok[...] > 0, sco, -1000000000.0)
            top = jnp.max(sco, 0, keepdims=True)
            top = jnp.maximum(top, pltpu.roll(top, 64, 1))
            ex = jnp.exp(sco - top)
            tot = jnp.sum(ex, 0, keepdims=True)
            probs = ex * (1.0 / (tot + pltpu.roll(tot, 64, 1)))
            pb = probs.astype(BF16)
            folded.append(dg(vp, pb, 0, 0))
            dp = draw[s]
            dot = jnp.sum(probs * dp, 0, keepdims=True)
            ds = probs * (dp - (dot + pltpu.roll(dot, 64, 1)))
            dbias[...] += ds
            dsb = (ds * scale).astype(BF16)
            dqs.append(dg(kp, dsb, 0, 0))
            dk = dg(dsb, qq, 1, 1).astype(BF16)
            dv = dg(pb, dd, 1, 1).astype(BF16)
            for r in range(NROW):
                dkv_s[r // 2, r % 2, u, sh] = dk[r * 32 : r * 32 + 32]
                dkv_s[r // 2, r % 2, u, 2 + sh] = dv[r * 32 : r * 32 + 32]

        def fold(m0, m1):
            return jnp.where(
                low,
                m0[:64] + pltpu.roll(m0[64:], 64, 1),
                pltpu.roll(m1[:64], 64, 1) + m1[64:],
            ).astype(BF16)

        att = fold(*folded)
        dq_t[u] = fold(*dqs)
        mix_s[u] = dg(outp_ref[...], att[:48], 0, 0).astype(BF16).reshape(16, 48, 128)
        pltpu.make_async_copy(mix_s.at[u, col], mix_r.at[u, col], locm.at[u]).start()
        to_mate(u).start()
        col_start(mix_src(u), mix_slot(u), sm.at[u], rm.at[u])

        @pl.when(u > 0)
        def _():
            pass_on(u - 1)

        return 0

    lax.fori_loop(0, 4, pair_of_samples, 0)

    db_s[...] = dbias[...].reshape(16, 16, 128)
    own_db = pltpu.make_async_copy(db_s.at[col], db_r.at[samp, col], loc.at[9])
    own_db.start()

    def db_copy(o):
        to = rmod(col + o, NCOL)
        return remote(
            db_s.at[to], db_r.at[samp, col], sbb.at[1, o], rbb.at[1, o], (row, to, 1 - samp)
        )

    def db_send(o, _):
        db_copy(o).start()
        return 0

    pass_on(3)
    lax.fori_loop(0, NCOL, db_send, 0)
    near_src, near_slot = (lambda c: db_s.at[c]), (lambda c: db_r.at[samp, c])
    col_start(near_src, near_slot, sbb.at[0], rbb.at[0])

    dga[...] = jnp.zeros_like(dga)

    def mixed_of(u, _):
        pltpu.make_async_copy(mix_s.at[u, col], mix_r.at[u, col], locm.at[u]).wait()
        col_wait(mix_src(u), mix_slot(u), sm.at[u], rm.at[u])
        total = mix_r[u, 0].astype(F32)
        for h in range(1, NCOL):
            total = total + mix_r[u, h].astype(F32)
        lanes = pl.ds(pl.multiple_of(u * 128, 128), 128)
        out = noisy_t[:48, lanes] + gate_t[:48, :] * total
        block_ref[2 * u] = out[:, :64].astype(BF16)
        block_ref[2 * u + 1] = pltpu.roll(out, 64, 1)[:, :64].astype(BF16)
        dga[:48, :] += g_t[u] * total
        return 0

    lax.fori_loop(0, 4, mixed_of, 0)
    out_block = pltpu.make_async_copy(block_ref, block_hbm, loc.at[15])
    out_block.start()

    dsc[...] = jnp.zeros_like(dsc)
    dsh[...] = jnp.zeros_like(dsh)

    def hidden_grad(u, _):
        to_mate(u).wait_send()
        for o in range(1, 4):
            came = rmod(zlo + 4 - o, 4)
            remote(
                dkv_o.at[u, came], dkv_r.at[u, came], sko.at[u, o], rko.at[u, o], mate
            ).wait_recv()
            to_chip(u, o).wait_send()
        dkv_r[u, zlo] = dkv_o[u, zlo]
        tot = dkv_r[u, 0].astype(F32)
        for z in range(1, 4):
            tot = tot + dkv_r[u, z].astype(F32)
        for sh in range(2):
            for jb in range(2):
                a = tot[sh, jb * 16 : jb * 16 + 16]
                b = tot[2 + sh, jb * 16 : jb * 16 + 16]
                base = sh * 64 + jb * 32
                dkv_tok[base : base + 16, :] = jnp.where(low16, a, pltpu.roll(b, 64, 1)).astype(BF16)
                dkv_tok[base + 16 : base + 32, :] = jnp.where(
                    low16, pltpu.roll(a, 64, 1), b
                ).astype(BF16)
        dh = dg(dq_t[u], wqkv[:64, :], 0, 0) + jnp.dot(
            dkv_tok[...], wqkv[64:, :], preferred_element_type=F32
        )
        n = normed[pl.ds(pl.multiple_of(u * 128, 128), 128), :]
        w = dh * n
        dsc[...] += w[:64] + w[64:]
        dsh[...] += dh[:64] + dh[64:]
        return 0

    lax.fori_loop(0, 4, hidden_grad, 0)
    sg_ = scale_s[...]
    part = dg(two_parts(dsc[...] * sg_ * (1.0 - sg_)), ada_w[:, :768], 1, 1)
    part = part + dg(two_parts(dsh[...]), ada_w[:, 768:1536], 1, 1)
    part = part[:64] + part[64:]
    acc = dga[...]
    acc = (acc + pltpu.roll(acc, 64, 1)) * gate_t[...] * (1.0 - gate_t[...])
    coarse = acc.astype(BF16)
    fine = (acc - coarse.astype(F32)).astype(BF16)
    part = part + (dg(coarse, wg_s[...], 0, 1) + dg(fine, wg_s[...], 0, 1))[:64]
    dc_s[...] = part.reshape(8, 8, 384)

    half_col = col // 2
    even = rmod(col, 2) == 0

    def part_copy(o):
        g = rmod(half_col + o, 8)
        return remote(dc_s.at[g], dc_r.at[col], st.at[o], rt.at[col], (row, 2 * g, samp))

    @pl.when(jnp.logical_not(even))
    def _():
        part_copy(0).start()

    def part_send(o, _):
        part_copy(o).start()
        return 0

    lax.fori_loop(1, 8, part_send, 0)

    own_db.wait()
    col_wait(near_src, near_slot, sbb.at[0], rbb.at[0])

    def db_wait(o, _):
        came = rmod(col + NCOL - o, NCOL)
        remote(db_s.at[came], db_r.at[1 - samp, came], sbb.at[1, o], rbb.at[1, o], far).wait_recv()
        db_copy(o).wait_send()
        return 0

    lax.fori_loop(0, NCOL, db_wait, 0)
    dbias[...] = (db_r[0] + db_r[1]).reshape(256, 128)
    biasp3 = jnp.concatenate([biasp_ref[...]] * 3, 0)

    def grad(lo, _):
        d = dbias[pl.ds(lo, 16, stride=16), :]
        d1 = d.astype(BF16)
        rest = d - d1.astype(F32)
        d2 = rest.astype(BF16)
        d3 = (rest - d2.astype(F32)).astype(BF16)
        g = dg(jnp.concatenate([d1, d2, d3], 0), biasp3, 0, 0)
        for hi in range(2):
            gpair_ref[pl.ds(lo + 16 * hi, 64, stride=32), :] = g[hi * 64 : hi * 64 + 64]
        return 0

    lax.fori_loop(0, 16, grad, 0, unroll=2)
    out_grad = pltpu.make_async_copy(gpair_ref, gpair_hbm, loc.at[16])
    out_grad.start()

    def own_copy(o):
        return remote(
            gs_own, gs_all.at[half_col], sg.at[o], rg.at[half_col], (row, rmod(col + o, NCOL), samp)
        )

    @pl.when(even)
    def _():
        dc_r[col] = dc_s[half_col]

        def arrived(o, _):
            came = rmod(col + o, NCOL)
            remote(dc_s.at[0], dc_r.at[came], st.at[0], rt.at[came], far).wait_recv()
            return 0

        lax.fori_loop(1, NCOL, arrived, 0)
        tot = dc_r[0]
        for c in range(1, NCOL):
            tot = tot + dc_r[c]
        dc_p[samp] = tot
        other = remote(dc_p.at[samp], dc_p.at[samp], sp.at[0], rp_.at[0], far)
        other.start()
        own = single_ref[...].astype(F32).reshape(8, 8, 384)
        mine = jnp.zeros((8, 384), F32)
        for g in range(8):
            mine = mine + jnp.where(half_col == g, own[g], 0.0)
        mean = jnp.mean(mine, -1, keepdims=True)
        cent = mine - mean
        inv = lax.rsqrt(jnp.mean(cent * cent, -1, keepdims=True) + EPSILON)
        unit = cent * inv
        remote(dc_p.at[samp], dc_p.at[1 - samp], sp.at[0], rp_.at[0], far).wait_recv()
        other.wait_send()
        up = dc_p[0] + dc_p[1]
        gs_own[...] = inv * (
            up - jnp.mean(up, -1, keepdims=True) - unit * jnp.mean(up * unit, -1, keepdims=True)
        )

        def tell(o, _):
            own_copy(o).start()
            return 0

        lax.fori_loop(1, NCOL, tell, 0)
        gs_all[half_col] = gs_own[...]

    @pl.when(jnp.logical_not(even))
    def _():
        part_copy(0).wait_send()

    def part_sent(o, _):
        part_copy(o).wait_send()
        return 0

    lax.fori_loop(1, 8, part_sent, 0)

    @pl.when(even)
    def _():
        def told(o, _):
            own_copy(o).wait_send()
            return 0

        lax.fori_loop(1, NCOL, told, 0)

    def total_came(g):
        remote(gs_own, gs_all.at[g], sg.at[0], rg.at[g], far).wait_recv()

    @pl.when(jnp.logical_not(even))
    def _():
        total_came(half_col)

    def came_from(o, _):
        total_came(rmod(half_col + o, 8))
        return 0

    lax.fori_loop(1, 8, came_from, 0)
    out_single = pltpu.make_async_copy(gs_all, gsingle_hbm, loc.at[17])
    out_single.start()
    for copy in (out_pair, out_block, out_grad, out_single):
        copy.wait()


def finish_kernel(*refs):
    n = 4
    ins, outs, bufs = refs[:n], refs[n : 2 * n], refs[2 * n : 3 * n]
    got, put = refs[3 * n], refs[3 * n + 1]
    reads = [pltpu.make_async_copy(ins[i], bufs[i], got.at[i]) for i in range(n)]
    writes = [pltpu.make_async_copy(bufs[i], outs[i], put.at[i]) for i in range(n)]
    for copy in reads:
        copy.start()
    for i in (3, 1, 0, 2):
        reads[i].wait()
        writes[i].start()
    for copy in writes:
        copy.wait()


def finished(arrays):
    hbm = pl.BlockSpec(memory_space=pl.ANY)
    return pl.pallas_call(
        finish_kernel,
        out_shape=[jax.ShapeDtypeStruct(x.shape, x.dtype) for x in arrays],
        in_specs=[hbm] * 4,
        out_specs=[hbm] * 4,
        scratch_shapes=[pltpu.VMEM(x.shape, x.dtype) for x in arrays]
        + [pltpu.SemaphoreType.DMA((4,)), pltpu.SemaphoreType.DMA((4,))],
        compiler_params=pltpu.CompilerParams(vmem_limit_bytes=60 * 1024 * 1024),
        name="finish",
    )(*arrays)


def on_device(
    pair_in, residue_index, chain_index, token_mask, relpos_weight, tri_proj, tri_out, bias_proj,
    single, ada_proj, noisy, qkv_proj, out_proj, cotangent,
):
    vm = pl.BlockSpec(memory_space=pltpu.VMEM)
    sm = pl.BlockSpec(memory_space=pltpu.SMEM)
    hbm = pl.BlockSpec(memory_space=pl.ANY)
    dma = pltpu.SemaphoreType.DMA
    v = pltpu.VMEM
    pair_out, block_t, grad_pair, grad_single = pl.pallas_call(
        step_kernel,
        out_shape=(
            jax.ShapeDtypeStruct((64, 32, 128), BF16),
            jax.ShapeDtypeStruct((8, 48, 64), BF16),
            jax.ShapeDtypeStruct((2048, 128), F32),
            jax.ShapeDtypeStruct((8, 8, 384), F32),
        ),
        in_specs=[sm, sm, sm, hbm, vm, hbm, vm, vm, vm, hbm, hbm, vm, vm, vm],
        out_specs=(hbm,) * 4,
        scratch_shapes=[
            v((64, 32, 128), BF16), v((8, 48, 64), BF16), v((2048, 128), F32),
            v((64, 32, 128), BF16), v((128, 640), BF16), v((384, 2304), BF16), v((512, 768), BF16),
            v((2, 64, 128), jnp.int32), v((128, 128), F32), v((128, 128), BF16),
            v((2048, 128), BF16), v((512, 128), BF16), v((2048, 128), F32), v((2048, 128), F32),
            v((4096, 128), F32),
            v((2, 16, 8, 16, 128), BF16), v((2, 16, 8, 16, 128), BF16),
            v((2, 8, 16, 16, 128), BF16), v((1024, 256), BF16), v((1024, 256), F32),
            v((8, 16, 16, 128), BF16), v((8, 16, 16, 128), BF16), v((16, 8, 16, 128), BF16),
            v((256, 128), F32), v((16, 16, 128), BF16), v((16, 16, 128), BF16),
            v((64, 384), BF16), v((64, 768), F32), v((64, 768), F32), v((384, 64), BF16),
            v((64, 128), F32), v((4, 48, 128), F32), v((64, 512), F32), v((512, 768), F32),
            v((512, 768), BF16), v((192, 768), BF16), v((64, 512), F32), v((512, 128), F32),
            v((2, 8, 32, 128), BF16), v((8, 2, 8, 32, 128), BF16), v((48, 512), BF16),
            v((16, 48, 512), BF16), v((64, 512), F32), v((256, 128), F32), v((8, 256, 128), F32),
            v((8, 256, 128), F32),
            v((4, 16, 48, 128), BF16), v((4, 16, 48, 128), BF16), v((4, 2, 4, 4, 32, 128), BF16),
            v((4, 4, 4, 32, 128), BF16), v((4, 4, 4, 32, 128), BF16), v((4, 4, 4, 32, 128), BF16),
            v((4, 64, 128), BF16), v((128, 128), BF16), v((256, 128), F32), v((16, 16, 128), F32),
            v((2, 16, 16, 128), F32),
            v((64, 768), F32), v((64, 768), F32), v((64, 128), F32), v((8, 8, 384), F32),
            v((16, 8, 384), F32), v((2, 8, 384), F32), v((8, 384), F32), v((8, 8, 384), F32),
            dma((2, 16)), dma((2, 16)), dma((2, 8)), dma((2, 8)), dma((8,)), dma((8,)),
            dma((16,)), dma((16,)), dma((16,)), dma((16,)), dma((4,)), dma((4,)),
            dma((4,)), dma((4,)), dma((16,)), dma((16,)),
            dma((4, 16)), dma((4, 16)), dma((4,)), dma((4,)), dma((4, 4)), dma((4, 4)),
            dma((2, 16)), dma((2, 16)), dma((8,)), dma((16,)), dma((1,)), dma((1,)),
            dma((16,)), dma((8,)), dma((18,)), dma((4,)),
        ],
        compiler_params=pltpu.CompilerParams(
            collective_id=1, has_side_effects=True, vmem_limit_bytes=60 * 1024 * 1024
        ),
        name="step",
    )(
        residue_index, chain_index, token_mask, pair_in, relpos_weight, tri_proj, tri_out,
        bias_proj.T, single, ada_proj, noisy.reshape(512, 768), qkv_proj.transpose(1, 2, 0),
        out_proj, cotangent.transpose(0, 2, 1),
    )
    pair_out, block_t, grad_pair, grad_single = finished(
        (pair_out, block_t, grad_pair, grad_single)
    )
    return (
        pair_out,
        block_t.transpose(0, 2, 1),
        grad_pair.reshape(64, 32, 128),
        grad_single.reshape(64, 384),
    )


def solution(mesh):
    return jax.shard_map(
        on_device,
        mesh=mesh,
        in_specs=(
            P("row", "col", None), P(), P(), P(), P(), P(), P(), P(), P("row", None), P(),
            P("samp", "row", None), P(None, None, "col"), P("col", None), P("samp", "row", "col"),
        ),
        out_specs=(
            P("row", "col", None), P("samp", "row", "col"), P("row", "col", None), P("row", None),
        ),
        check_vma=False,
    )
```

```python
import jax
import jax.numpy as jnp
from jax import lax
from jax.experimental import pallas as pl
from jax.experimental.pallas import tpu as pltpu
from jax.sharding import PartitionSpec as P

HEAD_DIM = 48
REL_BINS = 66
EPSILON = 1e-05
MESH = pl.DeviceIdType.MESH
F32 = jnp.float32
BF16 = jnp.bfloat16
NCOL = 16
NROW = 8


def dg(a, b, ca, cb, **kw):
    return lax.dot_general(a, b, (((ca,), (cb,)), ((), ())), preferred_element_type=F32, **kw)


def place():
    return lax.axis_index("row"), lax.axis_index("col"), lax.axis_index("samp")


def rmod(a, n):
    return lax.rem(a, n)


def ring_shift(oz, dest_core):
    if oz == 2:
        return 2 + 4 * dest_core
    return (0, 1, None, 7)[oz]


def row_dest(oz, cx):
    row, col, samp = place()
    z, core = samp * 4 + row // 2, rmod(row, 2)
    to_core = rmod(core + cx, 2)
    to_z = rmod(z + ring_shift(oz, to_core), 8)
    return rmod(to_z, 4) * 2 + to_core, col, to_z // 4


def row_source(oz, cx):
    row, col, samp = place()
    z, core = samp * 4 + row // 2, rmod(row, 2)
    from_core = rmod(core + cx, 2)
    from_z = rmod(z + 8 - ring_shift(oz, core), 8)
    return rmod(from_z, 4) * 2 + from_core, col, from_z // 4


ROW_IDS = [(oz, cx) for oz in range(4) for cx in range(2) if (oz, cx) != (0, 0)]


def remote(src, dst, ssem, rsem, to):
    return pltpu.make_async_remote_copy(
        src_ref=src, dst_ref=dst, send_sem=ssem, recv_sem=rsem, device_id=to, device_id_type=MESH
    )


def col_start(src_of, slot_of, ssem, rsem):
    row, col, samp = place()

    def one(o, _):
        to = rmod(col + o, NCOL)
        remote(src_of(to), slot_of(col), ssem.at[o], rsem.at[o], (row, to, samp)).start()
        return 0

    lax.fori_loop(1, NCOL, one, 0)


def col_wait(src_of, slot_of, ssem, rsem, recv=True, send=True):
    row, col, samp = place()

    def one(o, _):
        to = rmod(col + o, NCOL)
        came = rmod(col + NCOL - o, NCOL)
        if recv:
            remote(src_of(to), slot_of(came), ssem.at[o], rsem.at[o], (row, to, samp)).wait_recv()
        if send:
            remote(src_of(to), slot_of(came), ssem.at[o], rsem.at[o], (row, to, samp)).wait_send()
        return 0

    lax.fori_loop(1, NCOL, one, 0)


def row_start(src_of, slot_of, ssem, rsem):
    row = lax.axis_index("row")
    for oz, cx in ROW_IDS:
        to = row_dest(oz, cx)
        i = oz * 2 + cx
        remote(src_of(to[0]), slot_of(row), ssem.at[i], rsem.at[i], to).start()


def row_wait(src_of, slot_of, ssem, rsem, recv=True, send=True):
    for oz, cx in ROW_IDS:
        to, came = row_dest(oz, cx), row_source(oz, cx)
        i = oz * 2 + cx
        copy = remote(src_of(to[0]), slot_of(came[0]), ssem.at[i], rsem.at[i], to)
        if recv:
            copy.wait_recv()
        if send:
            copy.wait_send()


def signal(sem, to):
    pl.semaphore_signal(sem, inc=1, device_id=to, device_id_type=MESH)


def both(x, low, first):
    turned = pltpu.roll(x, 64, 1)
    return jnp.where(low, x, turned) if first else jnp.where(low, turned, x)


def layer_norm(x, axis):
    mean = jnp.mean(x, axis, keepdims=True)
    cent = x - mean
    var = jnp.mean(cent * cent, axis, keepdims=True)
    return cent * lax.rsqrt(var + EPSILON)


def two_parts(x):
    coarse = x.astype(BF16)
    return jnp.concatenate([coarse, (x - coarse.astype(F32)).astype(BF16)], 0)


def step_kernel(
    res_ref, chain_ref, mask_ref,
    pair_hbm, relpos_hbm, tri_hbm, triout_hbm, biasp_hbm, single_hbm, ada_hbm, noisy_hbm,
    qkvw_hbm, outp_hbm, cot_hbm,
    pairout_hbm, block_hbm, gpair_hbm, gsingle_hbm,
    pairout_ref, block_ref, gpair_ref,
    pair_in, tri_w, ada_w, noisy, relpos_ref, triout_ref, biasp_ref, single_ref, qkvw_ref, outp_ref,
    cot_ref, idx_r, mrow, relpos_w,
    zl_s, tri_t, pf, gate, lrf, lbuf, recv_a, got, rcat, mtmp, tbuf, got_c, got_d, bias_f, bias_b, bias_got,
    cvec_s, scale_s, shift_s, wg_s, gate_t, g_t, noisy_t, normed, hidden, wqkv, q_t, kv_f,
    kv_own, kv_all, dmx_own, dmx_all, da_t, keyok, sraw, draw,
    mix_s, mix_r, dkv_s, dkv_m, dkv_o, dkv_r, dq_t, dkv_tok, dbias, db_s, db_r,
    dsc, dsh, dga, dc_s, dc_r, dc_p, gs_own, gs_all,
    sa, ra, sb, rb, sc, rc, sd, rd, se, re, skv, rkv, skf, rkf, sdm, rdm,
    sm, rm, sk, rk, sko, rko, sbb, rbb, st, rt, sp, rp_, sg, rg, loc, locm,
):
    row, col, samp = place()
    core = rmod(row, 2)
    zlo = row // 2
    mate = (row + 1 - 2 * core, col, samp)
    far = (row, col, 1 - samp)
    barrier = pltpu.get_barrier_semaphore()

    loads = [
        pltpu.make_async_copy(s, d, loc.at[18 + i])
        for i, (s, d) in enumerate(
            [
                (pair_hbm, pair_in), (relpos_hbm, relpos_ref), (tri_hbm, tri_w),
                (single_hbm, single_ref), (qkvw_hbm, qkvw_ref), (ada_hbm, ada_w),
                (noisy_hbm, noisy), (cot_hbm, cot_ref), (triout_hbm, triout_ref),
                (biasp_hbm, biasp_ref), (outp_hbm, outp_ref),
            ]
        )
    ]
    for copy in loads:
        copy.start()
    for oz, cx in ROW_IDS:
        signal(barrier, row_source(oz, cx))

    def greet(o, _):
        signal(barrier, (row, rmod(col + o, NCOL), samp))
        return 0

    def greet_row(o, _):
        signal(barrier, (rmod(row + o, NROW), col, samp))
        return 0

    def greet_far(o, _):
        signal(barrier, (row, rmod(col + o, NCOL), 1 - samp))
        return 0

    lax.fori_loop(1, NCOL, greet, 0)
    lax.fori_loop(1, NROW, greet_row, 0)
    lax.fori_loop(0, NCOL, greet_far, 0)

    low = lax.broadcasted_iota(jnp.int32, (64, 128), 1) < 64
    low16 = lax.broadcasted_iota(jnp.int32, (16, 128), 1) < 64
    low1 = lax.broadcasted_iota(jnp.int32, (1, 128), 1) < 64
    diag = (lax.broadcasted_iota(jnp.int32, (128, 128), 0) < 64) == (
        lax.broadcasted_iota(jnp.int32, (128, 128), 1) < 64
    )

    def blockdiag(x):
        return jnp.where(diag, jnp.concatenate([x, x], 0), 0.0).astype(BF16)

    def indices(i, _):
        at = pl.ds(i, 1)
        idx_r[0, at, :] = jnp.full((1, 128), res_ref[row * 64 + i], jnp.int32)
        idx_r[1, at, :] = jnp.full((1, 128), chain_ref[row * 64 + i], jnp.int32)
        m = jnp.full((1, 128), mask_ref[row * 64 + i].astype(F32), F32)
        mrow[at, :] = m
        mrow[pl.ds(64 + i, 1), :] = m
        return 0

    lax.fori_loop(0, 64, indices, 0, unroll=4)
    mrow[...] = mrow[...].T
    relpos_w[...] = jnp.zeros_like(relpos_w)
    loads[1].wait()
    relpos_w[0:REL_BINS, :] = relpos_ref[...]
    loads[0].wait()

    def load(i, _):
        pf[pl.ds(i * 32, 32), :] = pair_in[i].astype(F32)
        return 0

    lax.fori_loop(0, 64, load, 0, unroll=4)
    bins = lax.broadcasted_iota(jnp.int32, (64, 128), 1)

    def normed_rows(t, _):
        parts = []
        for q in range(2):
            for hi in range(2):
                j = 2 * t + q + 16 * hi
                off = jnp.clip(idx_r[0] - res_ref[col * 32 + j] + 32, 0, 64)
                bucket = jnp.where(idx_r[1] == chain_ref[col * 32 + j], off, REL_BINS - 1)
                onehot = jnp.where(bucket == bins, 1.0, 0.0).astype(BF16)
                parts.append(
                    pf[pl.ds(j, 64, stride=32), :]
                    + jnp.dot(onehot, relpos_w[...], preferred_element_type=F32)
                )
        for q in range(2):
            for hi in range(2):
                pf[pl.ds(2 * t + q + 16 * hi, 64, stride=32), :] = parts[2 * q + hi]
        at = pl.ds(pl.multiple_of(t * 256, 256), 256)
        zl_s[at, :] = layer_norm(jnp.concatenate(parts, 0), -1).astype(BF16)
        return 0

    lax.fori_loop(0, 8, normed_rows, 0, unroll=2)
    loads[2].wait()
    tri_t[...] = tri_w[:, :512].astype(F32).T.astype(BF16)

    def project(h, t):
        at = pl.ds(pl.multiple_of(t * 256, 256), 256)
        pt = dg(tri_t[h * 256 : h * 256 + 256, :], zl_s[at, :], 1, 1)
        val = jax.nn.sigmoid(pt[128:]) * pt[:128]
        for q in range(2):
            lo = 2 * t + q
            mask = mrow[0:1, :] * jnp.where(
                low1, mask_ref[col * 32 + lo].astype(F32), mask_ref[col * 32 + 16 + lo].astype(F32)
            )
            lrf[pl.ds(h * 2048 + lo, 128, stride=16), :] = val[:, q * 128 : q * 128 + 128] * mask

    a_src = [lambda to, h=h: lbuf.at[h, to] for h in range(2)]
    a_slot = [lambda c, h=h: recv_a.at[h, c] for h in range(2)]
    b_src = [lambda r, h=h: recv_a.at[h, :, r] for h in range(2)]
    b_slot = [lambda r, h=h: got.at[h, r] for h in range(2)]
    own_a = [pltpu.make_async_copy(lbuf.at[h, col], recv_a.at[h, col], loc.at[h]) for h in range(2)]
    own_b = [
        pltpu.make_async_copy(recv_a.at[h, :, row], got.at[h, row], loc.at[2 + h])
        for h in range(2)
    ]
    for h in range(2):

        def one_side(t, _):
            project(h, t)
            return 0

        lax.fori_loop(0, 8, one_side, 0)

        def pack(c, _):
            lbuf[h, c] = lrf[pl.ds(h * 2048 + c * 128, 128), :].astype(BF16).reshape(8, 16, 128)
            return 0

        lax.fori_loop(0, 16, pack, 0)
        if h == 0:
            pl.semaphore_wait(barrier, 7 + 15 + 7 + 16)
        own_a[h].start()
        col_start(a_src[h], a_slot[h], sa.at[h], ra.at[h])

    for copy in loads[3:6]:
        copy.wait()
    cvec = layer_norm(single_ref[...].astype(F32), -1).astype(BF16)
    cvec_s[...] = cvec
    wqkv[...] = jnp.zeros_like(wqkv)
    for p in range(3):
        wqkv[p * 64 : p * 64 + 48, :] = qkvw_ref[p]
    scale_s[...] = jax.nn.sigmoid(jnp.dot(cvec, ada_w[:, :768], preferred_element_type=F32))
    shift_s[...] = jnp.dot(cvec, ada_w[:, 768:1536], preferred_element_type=F32)
    for copy in loads[6:]:
        copy.wait()

    def sample(s, _):
        at = pl.ds(pl.multiple_of(s * 64, 64), 64)
        n = layer_norm(noisy[at, :].astype(F32), -1)
        normed[at, :] = n
        hidden[at, :] = (scale_s[...] * n + shift_s[...]).astype(BF16)
        return 0

    lax.fori_loop(0, 8, sample, 0)
    own_a[0].wait()
    col_wait(a_src[0], a_slot[0], sa.at[0], ra.at[0])
    own_b[0].start()
    row_start(b_src[0], b_slot[0], sb.at[0], rb.at[0])

    feat = lax.broadcasted_iota(jnp.int32, (768, 64), 1)
    sel = jnp.where(
        (lax.broadcasted_iota(jnp.int32, (768, 64), 0) == col * 48 + feat) & (feat < 48), 1.0, 0.0
    ).astype(BF16)
    wg_s[...] = jnp.dot(ada_w[:, 1536:], sel, preferred_element_type=F32).astype(BF16)
    gate_t[...] = jax.nn.sigmoid(
        dg(wg_s[...], jnp.concatenate([cvec_s[...], cvec_s[...]], 0), 0, 1)
    )
    lane = lax.broadcasted_iota(jnp.int32, (64, 128), 1)
    tok = lax.broadcasted_iota(jnp.int32, (64, 128), 0)
    put = [jnp.where(lane == tok + 64 * h, 1.0, 0.0).astype(BF16) for h in range(2)]
    for u in range(4):
        g = jnp.dot(cot_ref[2 * u], put[0], preferred_element_type=F32) + jnp.dot(
            cot_ref[2 * u + 1], put[1], preferred_element_type=F32
        )
        g_t[u] = g
        dmx_own[:, u * 128 : u * 128 + 128] = (g * gate_t[:48, :]).astype(BF16)
    dm_src, dm_slot = (lambda to: dmx_own), (lambda c: dmx_all.at[c])
    dm_keep = pltpu.make_async_copy(dmx_own, dmx_all.at[col], loc.at[5])
    dm_keep.start()
    col_start(dm_src, dm_slot, sdm, rdm)
    kv_f[...] = dg(hidden[...], wqkv[64:, :], 1, 1)

    def kv_pack(t, _):
        r0 = kv_f[pl.ds(t * 32, 16), :]
        r1 = kv_f[pl.ds(t * 32 + 16, 16), :]
        to = pl.ds(pl.multiple_of(rmod(t, 2) * 16, 16), 16)
        kv_own[0, t // 2, to, :] = jnp.where(low16, r0, pltpu.roll(r1, 64, 1)).astype(BF16)
        kv_own[1, t // 2, to, :] = jnp.where(low16, pltpu.roll(r0, 64, 1), r1).astype(BF16)
        return 0

    lax.fori_loop(0, 16, kv_pack, 0, unroll=2)
    kv_keep = pltpu.make_async_copy(kv_own, kv_all.at[row], loc.at[4])
    kv_keep.start()
    kv_out = []
    for o in range(1, 4):
        to = (rmod(zlo + o, 4) * 2 + core, col, samp)
        kv_out.append(remote(kv_own, kv_all.at[row], skv.at[o], rkv.at[o], to))
    kv_mate = remote(kv_own, kv_all.at[row], skf.at[0], rkf.at[0], mate)
    own_a[1].wait()
    col_wait(a_src[1], a_slot[1], sa.at[1], ra.at[1])
    own_b[1].start()
    row_start(b_src[1], b_slot[1], sb.at[1], rb.at[1])

    def gates(t, _):
        at = pl.ds(pl.multiple_of(t * 256, 256), 256)
        gate[at, :] = jax.nn.sigmoid(
            jnp.dot(zl_s[at, :], tri_w[:, 512:], preferred_element_type=F32)
        )
        return 0

    lax.fori_loop(0, 8, gates, 0)
    for h in (1, 0):
        own_b[h].wait()
        row_wait(b_src[h], b_slot[h], sb.at[h], rb.at[h])

    def turn(r, _):
        rcat[pl.ds(pl.multiple_of(r * 128, 128), 128), :] = (
            got[1, r].reshape(256, 128).astype(F32).T.astype(BF16)
        )
        return 0

    lax.fori_loop(0, 8, turn, 0)

    c_src, c_slot = (lambda r: tbuf.at[r]), (lambda r: got_c.at[r])

    def tri(rp):
        rhs = jnp.concatenate(
            [got[0, 2 * rp].reshape(256, 128), got[0, 2 * rp + 1].reshape(256, 128)], 1
        )
        mtmp[...] = jnp.dot(rcat[...], rhs, preferred_element_type=F32)

        def out(rj, _):
            for half in range(2):
                top = mtmp[pl.ds(rj * 128, 64), half * 128 : half * 128 + 128]
                bot = mtmp[pl.ds(rj * 128 + 64, 64), half * 128 : half * 128 + 128]
                for jh in range(2):
                    a = slice(jh * 32, jh * 32 + 16)
                    b = slice(jh * 32 + 16, jh * 32 + 32)
                    t = jnp.where(
                        low16,
                        top[a] + pltpu.roll(bot[a], 64, 1),
                        pltpu.roll(top[b], 64, 1) + bot[b],
                    )
                    tbuf[2 * rp + half, 2 * rj + jh] = t.astype(BF16)
            return 0

        lax.fori_loop(0, 8, out, 0, unroll=2)

    own_c = pltpu.make_async_copy(tbuf.at[row], got_c.at[row], loc.at[6])
    for oz in (2, 1, 3, 0):
        tri(rmod(zlo + oz, 4))
        for cx in range(2):
            if (oz, cx) != (0, 0):
                to = row_dest(oz, cx)
                i = oz * 2 + cx
                remote(c_src(to[0]), c_slot(row), sc.at[i], rc.at[i], to).start()
    own_c.start()
    kv_mate.start()
    for copy in kv_out:
        copy.start()
    d_src, d_slot = (lambda c: got_c.at[:, c]), (lambda c: got_d.at[c])

    dm_keep.wait()
    col_wait(dm_src, dm_slot, sdm, rdm)
    da_t[...] = jnp.zeros_like(da_t)
    da_t[:48, :] = (
        jnp.dot(outp_ref[...], dmx_all[...].reshape(768, 512), preferred_element_type=F32)
        .astype(BF16)
        .astype(F32)
    )
    own_c.wait()
    row_wait(c_src, c_slot, sc, rc)
    own_d = pltpu.make_async_copy(got_c.at[:, col], got_d.at[col], loc.at[7])
    own_d.start()
    col_start(d_src, d_slot, sd, rd)

    q_t[...] = dg(wqkv[:64, :], hidden[...], 1, 1)
    noisy_t[...] = dg(sel, noisy[...], 0, 1)

    def key_mask(t, _):
        jb, lo = t // 16, rmod(t, 16)
        keyok[pl.ds(t, 1), :] = jnp.where(
            low1,
            mask_ref[jb * 32 + lo].astype(F32),
            mask_ref[jb * 32 + 16 + lo].astype(F32),
        )
        return 0

    lax.fori_loop(0, 256, key_mask, 0, unroll=4)

    for o in range(1, 4):
        came = rmod(zlo + 4 - o, 4) * 2 + core
        remote(kv_own, kv_all.at[came], skv.at[o], rkv.at[o], mate).wait_recv()
        remote(kv_all.at[came], kv_all.at[came], skf.at[o], rkf.at[o], mate).start()


    def half_of(ref, u, sh):
        tile = ref[:, pl.ds(pl.multiple_of(u * 128, 128), 128)].astype(F32)
        return blockdiag(both(tile, low, sh == 0))

    def keys(which, s):
        return jnp.concatenate([kv_all[r, which, s] for r in range(NROW)], 0)

    def raw(u, _):
        for sh in range(2):
            s = 2 * u + sh
            sraw[s] = jnp.dot(keys(0, s), half_of(q_t, u, sh), preferred_element_type=F32)
            draw[s] = jnp.dot(keys(1, s), half_of(da_t, u, sh), preferred_element_type=F32)
        return 0

    own_d.wait()
    col_wait(d_src, d_slot, sd, rd)

    def widen(c, _):
        lrf[pl.ds(c * 128, 128), :] = got_d[c].reshape(128, 128).astype(F32)
        return 0

    lax.fori_loop(0, 16, widen, 0)

    def stage3(t, _):
        tn = layer_norm(
            jnp.concatenate([lrf[pl.ds(2 * t + q, 128, stride=16), :] for q in range(2)], 1), 0
        ).astype(BF16)
        upd = dg(tn, triout_ref[...], 0, 0) * gate[pl.ds(pl.multiple_of(t * 256, 256), 256), :]
        spots = [pl.ds(2 * t + q + 16 * hi, 64, stride=32) for q in range(2) for hi in range(2)]
        outs = [
            (pf[at, :] + upd[i * 64 : i * 64 + 64]).astype(BF16) for i, at in enumerate(spots)
        ]
        for at, val in zip(spots, outs):
            pf[at, :] = val.astype(F32)
        tile = dg(biasp_ref[...], jnp.concatenate(outs, 0), 1, 1)
        for q in range(2):
            bias_f[pl.ds(2 * t + q, 16, stride=16), :] = tile[:, q * 128 : q * 128 + 128]
        return 0

    lax.fori_loop(0, 8, stage3, 0, unroll=2)
    bias_b[...] = bias_f[...].astype(BF16).reshape(16, 16, 128)
    e_src, e_slot = (lambda c: bias_b.at[c]), (lambda c: bias_got.at[c])
    own_e = pltpu.make_async_copy(bias_b.at[col], bias_got.at[col], loc.at[8])
    own_e.start()
    col_start(e_src, e_slot, se, re)

    kv_keep.wait()
    for copy in kv_out:
        copy.wait_send()
    kv_mate.wait_send()
    for o in range(4):
        came = rmod(zlo + 4 - o, 4) * 2
        remote(
            kv_all.at[came + core], kv_all.at[came + 1 - core], skf.at[o], rkf.at[o], mate
        ).wait_recv()
        if o > 0:
            remote(
                kv_all.at[came + core], kv_all.at[came + core], skf.at[o], rkf.at[o], mate
            ).wait_send()
    lax.fori_loop(0, 4, raw, 0)
    def store(i, _):
        pairout_ref[i] = pf[pl.ds(i * 32, 32), :].astype(BF16)
        return 0

    lax.fori_loop(0, 64, store, 0, unroll=4)
    out_pair = pltpu.make_async_copy(pairout_ref, pairout_hbm, loc.at[14])
    out_pair.start()
    dbias[...] = jnp.zeros_like(dbias)
    own_e.wait()
    col_wait(e_src, e_slot, se, re)

    scale = 1.0 / HEAD_DIM**0.5

    def mix_src(u):
        return lambda f: mix_s.at[u, f]

    def mix_slot(u):
        return lambda h: mix_r.at[u, h]

    def to_mate(u):
        return remote(dkv_s.at[:, 1 - core, u], dkv_m.at[u], sk.at[u], rk.at[u], mate)

    def to_chip(u, o):
        z = rmod(zlo + o, 4)
        return remote(
            dkv_o.at[u, z], dkv_r.at[u, zlo], sko.at[u, o], rko.at[u, o], (z * 2 + core, col, samp)
        )

    def pass_on(u):
        to_mate(u).wait_recv()
        for z in range(4):
            dkv_o[u, z] = (
                dkv_s[z, core, u].astype(F32) + dkv_m[u, z].astype(F32)
            ).astype(BF16)
        for o in range(1, 4):
            to_chip(u, o).start()

    def pair_of_samples(u, _):
        folded, dqs = [], []
        for sh in range(2):
            s = 2 * u + sh
            kp, vp = keys(0, s), keys(1, s)
            qq, dd = half_of(q_t, u, sh), half_of(da_t, u, sh)
            sco = sraw[s] * scale + bias_got[...].reshape(256, 128).astype(F32)
            sco = jnp.where(keyok[...] > 0, sco, -1000000000.0)
            top = jnp.max(sco, 0, keepdims=True)
            top = jnp.maximum(top, pltpu.roll(top, 64, 1))
            ex = jnp.exp(sco - top)
            tot = jnp.sum(ex, 0, keepdims=True)
            probs = ex * (1.0 / (tot + pltpu.roll(tot, 64, 1)))
            pb = probs.astype(BF16)
            folded.append(dg(vp, pb, 0, 0))
            dp = draw[s]
            dot = jnp.sum(probs * dp, 0, keepdims=True)
            ds = probs * (dp - (dot + pltpu.roll(dot, 64, 1)))
            dbias[...] += ds
            dsb = (ds * scale).astype(BF16)
            dqs.append(dg(kp, dsb, 0, 0))
            dk = dg(dsb, qq, 1, 1).astype(BF16)
            dv = dg(pb, dd, 1, 1).astype(BF16)
            for r in range(NROW):
                dkv_s[r // 2, r % 2, u, sh] = dk[r * 32 : r * 32 + 32]
                dkv_s[r // 2, r % 2, u, 2 + sh] = dv[r * 32 : r * 32 + 32]

        def fold(m0, m1):
            return jnp.where(
                low,
                m0[:64] + pltpu.roll(m0[64:], 64, 1),
                pltpu.roll(m1[:64], 64, 1) + m1[64:],
            ).astype(BF16)

        att = fold(*folded)
        dq_t[u] = fold(*dqs)
        mix_s[u] = dg(outp_ref[...], att[:48], 0, 0).astype(BF16).reshape(16, 48, 128)
        pltpu.make_async_copy(mix_s.at[u, col], mix_r.at[u, col], locm.at[u]).start()
        to_mate(u).start()
        col_start(mix_src(u), mix_slot(u), sm.at[u], rm.at[u])

        @pl.when(u > 0)
        def _():
            pass_on(u - 1)

        return 0

    lax.fori_loop(0, 4, pair_of_samples, 0)

    db_s[...] = dbias[...].astype(BF16).reshape(16, 16, 128)
    own_db = pltpu.make_async_copy(db_s.at[col], db_r.at[samp, col], loc.at[9])
    own_db.start()

    def db_copy(o):
        to = rmod(col + o, NCOL)
        return remote(
            db_s.at[to], db_r.at[samp, col], sbb.at[1, o], rbb.at[1, o], (row, to, 1 - samp)
        )

    def db_send(o, _):
        db_copy(o).start()
        return 0

    pass_on(3)
    lax.fori_loop(0, NCOL, db_send, 0)
    near_src, near_slot = (lambda c: db_s.at[c]), (lambda c: db_r.at[samp, c])
    col_start(near_src, near_slot, sbb.at[0], rbb.at[0])

    dga[...] = jnp.zeros_like(dga)

    def mixed_of(u, _):
        pltpu.make_async_copy(mix_s.at[u, col], mix_r.at[u, col], locm.at[u]).wait()
        col_wait(mix_src(u), mix_slot(u), sm.at[u], rm.at[u])
        total = mix_r[u, 0].astype(F32)
        for h in range(1, NCOL):
            total = total + mix_r[u, h].astype(F32)
        lanes = pl.ds(pl.multiple_of(u * 128, 128), 128)
        out = noisy_t[:48, lanes] + gate_t[:48, :] * total
        block_ref[2 * u] = out[:, :64].astype(BF16)
        block_ref[2 * u + 1] = pltpu.roll(out, 64, 1)[:, :64].astype(BF16)
        dga[:48, :] += g_t[u] * total
        return 0

    lax.fori_loop(0, 3, mixed_of, 0)

    dsc[...] = jnp.zeros_like(dsc)
    dsh[...] = jnp.zeros_like(dsh)

    def hidden_grad(u, _):
        to_mate(u).wait_send()
        for o in range(1, 4):
            came = rmod(zlo + 4 - o, 4)
            remote(
                dkv_o.at[u, came], dkv_r.at[u, came], sko.at[u, o], rko.at[u, o], mate
            ).wait_recv()
            to_chip(u, o).wait_send()
        dkv_r[u, zlo] = dkv_o[u, zlo]
        tot = dkv_r[u, 0].astype(F32)
        for z in range(1, 4):
            tot = tot + dkv_r[u, z].astype(F32)
        for sh in range(2):
            for jb in range(2):
                a = tot[sh, jb * 16 : jb * 16 + 16]
                b = tot[2 + sh, jb * 16 : jb * 16 + 16]
                base = sh * 64 + jb * 32
                dkv_tok[base : base + 16, :] = jnp.where(low16, a, pltpu.roll(b, 64, 1)).astype(BF16)
                dkv_tok[base + 16 : base + 32, :] = jnp.where(
                    low16, pltpu.roll(a, 64, 1), b
                ).astype(BF16)
        dh = dg(dq_t[u], wqkv[:64, :], 0, 0) + jnp.dot(
            dkv_tok[...], wqkv[64:, :], preferred_element_type=F32
        )
        n = normed[pl.ds(pl.multiple_of(u * 128, 128), 128), :]
        w = dh * n
        dsc[...] += w[:64] + w[64:]
        dsh[...] += dh[:64] + dh[64:]
        return 0

    lax.fori_loop(0, 3, hidden_grad, 0)
    mixed_of(3, 0)
    out_block = pltpu.make_async_copy(block_ref, block_hbm, loc.at[15])
    out_block.start()
    hidden_grad(3, 0)
    sg_ = scale_s[...]
    part = dg(two_parts(dsc[...] * sg_ * (1.0 - sg_)), ada_w[:, :768], 1, 1)
    part = part + dg(two_parts(dsh[...]), ada_w[:, 768:1536], 1, 1)
    part = part[:64] + part[64:]
    acc = dga[...]
    acc = (acc + pltpu.roll(acc, 64, 1)) * gate_t[...] * (1.0 - gate_t[...])
    coarse = acc.astype(BF16)
    fine = (acc - coarse.astype(F32)).astype(BF16)
    part = part + (dg(coarse, wg_s[...], 0, 1) + dg(fine, wg_s[...], 0, 1))[:64]
    dc_s[...] = part.reshape(8, 8, 384)

    half_col = col // 2
    even = rmod(col, 2) == 0

    def part_copy(o):
        g = rmod(half_col + o, 8)
        return remote(dc_s.at[g], dc_r.at[col], st.at[o], rt.at[col], (row, 2 * g, samp))

    @pl.when(jnp.logical_not(even))
    def _():
        part_copy(0).start()

    def part_send(o, _):
        part_copy(o).start()
        return 0

    lax.fori_loop(1, 8, part_send, 0)

    own_db.wait()
    col_wait(near_src, near_slot, sbb.at[0], rbb.at[0])

    def db_wait(o, _):
        came = rmod(col + NCOL - o, NCOL)
        remote(db_s.at[came], db_r.at[1 - samp, came], sbb.at[1, o], rbb.at[1, o], far).wait_recv()
        db_copy(o).wait_send()
        return 0

    lax.fori_loop(0, NCOL, db_wait, 0)
    dbias[...] = (db_r[0].astype(F32) + db_r[1].astype(F32)).reshape(256, 128)
    biasp3 = jnp.concatenate([biasp_ref[...]] * 3, 0)

    def grad(lo, _):
        d = dbias[pl.ds(lo, 16, stride=16), :]
        d1 = d.astype(BF16)
        rest = d - d1.astype(F32)
        d2 = rest.astype(BF16)
        d3 = (rest - d2.astype(F32)).astype(BF16)
        g = dg(jnp.concatenate([d1, d2, d3], 0), biasp3, 0, 0)
        for hi in range(2):
            gpair_ref[pl.ds(lo + 16 * hi, 64, stride=32), :] = g[hi * 64 : hi * 64 + 64]
        return 0

    lax.fori_loop(0, 16, grad, 0, unroll=2)
    out_grad = pltpu.make_async_copy(gpair_ref, gpair_hbm, loc.at[16])
    out_grad.start()

    def own_copy(o):
        return remote(
            gs_own, gs_all.at[half_col], sg.at[o], rg.at[half_col], (row, rmod(col + o, NCOL), samp)
        )

    @pl.when(even)
    def _():
        dc_r[col] = dc_s[half_col]

        def arrived(o, _):
            came = rmod(col + o, NCOL)
            remote(dc_s.at[0], dc_r.at[came], st.at[0], rt.at[came], far).wait_recv()
            return 0

        lax.fori_loop(1, NCOL, arrived, 0)
        tot = dc_r[0]
        for c in range(1, NCOL):
            tot = tot + dc_r[c]
        dc_p[samp] = tot
        other = remote(dc_p.at[samp], dc_p.at[samp], sp.at[0], rp_.at[0], far)
        other.start()
        own = single_ref[...].astype(F32).reshape(8, 8, 384)
        mine = jnp.zeros((8, 384), F32)
        for g in range(8):
            mine = mine + jnp.where(half_col == g, own[g], 0.0)
        mean = jnp.mean(mine, -1, keepdims=True)
        cent = mine - mean
        inv = lax.rsqrt(jnp.mean(cent * cent, -1, keepdims=True) + EPSILON)
        unit = cent * inv
        remote(dc_p.at[samp], dc_p.at[1 - samp], sp.at[0], rp_.at[0], far).wait_recv()
        other.wait_send()
        up = dc_p[0] + dc_p[1]
        gs_own[...] = inv * (
            up - jnp.mean(up, -1, keepdims=True) - unit * jnp.mean(up * unit, -1, keepdims=True)
        )

        def tell(o, _):
            own_copy(o).start()
            return 0

        lax.fori_loop(1, NCOL, tell, 0)
        gs_all[half_col] = gs_own[...]

    @pl.when(jnp.logical_not(even))
    def _():
        part_copy(0).wait_send()

    def part_sent(o, _):
        part_copy(o).wait_send()
        return 0

    lax.fori_loop(1, 8, part_sent, 0)

    @pl.when(even)
    def _():
        def told(o, _):
            own_copy(o).wait_send()
            return 0

        lax.fori_loop(1, NCOL, told, 0)

    def total_came(g):
        remote(gs_own, gs_all.at[g], sg.at[0], rg.at[g], far).wait_recv()

    @pl.when(jnp.logical_not(even))
    def _():
        total_came(half_col)

    def came_from(o, _):
        total_came(rmod(half_col + o, 8))
        return 0

    lax.fori_loop(1, 8, came_from, 0)
    out_single = pltpu.make_async_copy(gs_all, gsingle_hbm, loc.at[17])
    out_single.start()
    for copy in (out_pair, out_block, out_grad, out_single):
        copy.wait()


def finish_kernel(*refs):
    n = 4
    ins, outs, bufs = refs[:n], refs[n : 2 * n], refs[2 * n : 3 * n]
    got, put = refs[3 * n], refs[3 * n + 1]
    reads = [pltpu.make_async_copy(ins[i], bufs[i], got.at[i]) for i in range(n)]
    writes = [pltpu.make_async_copy(bufs[i], outs[i], put.at[i]) for i in range(n)]
    for copy in reads:
        copy.start()
    for i in (3, 1, 0, 2):
        reads[i].wait()
        writes[i].start()
    for copy in writes:
        copy.wait()


def finished(arrays):
    hbm = pl.BlockSpec(memory_space=pl.ANY)
    return pl.pallas_call(
        finish_kernel,
        out_shape=[jax.ShapeDtypeStruct(x.shape, x.dtype) for x in arrays],
        in_specs=[hbm] * 4,
        out_specs=[hbm] * 4,
        scratch_shapes=[pltpu.VMEM(x.shape, x.dtype) for x in arrays]
        + [pltpu.SemaphoreType.DMA((4,)), pltpu.SemaphoreType.DMA((4,))],
        compiler_params=pltpu.CompilerParams(vmem_limit_bytes=60 * 1024 * 1024),
        name="finish",
    )(*arrays)


def on_device(
    pair_in, residue_index, chain_index, token_mask, relpos_weight, tri_proj, tri_out, bias_proj,
    single, ada_proj, noisy, qkv_proj, out_proj, cotangent,
):
    sm = pl.BlockSpec(memory_space=pltpu.SMEM)
    hbm = pl.BlockSpec(memory_space=pl.ANY)
    dma = pltpu.SemaphoreType.DMA
    v = pltpu.VMEM
    pair_out, block_t, grad_pair, grad_single = pl.pallas_call(
        step_kernel,
        out_shape=(
            jax.ShapeDtypeStruct((64, 32, 128), BF16),
            jax.ShapeDtypeStruct((8, 48, 64), BF16),
            jax.ShapeDtypeStruct((2048, 128), F32),
            jax.ShapeDtypeStruct((8, 8, 384), F32),
        ),
        in_specs=[sm] * 3 + [hbm] * 11,
        out_specs=(hbm,) * 4,
        scratch_shapes=[
            v((64, 32, 128), BF16), v((8, 48, 64), BF16), v((2048, 128), F32),
            v((64, 32, 128), BF16), v((128, 640), BF16), v((384, 2304), BF16), v((512, 768), BF16),
            v((REL_BINS, 128), BF16), v((128, 128), BF16), v((16, 128), BF16), v((64, 384), BF16),
            v((3, 48, 768), BF16), v((48, 768), BF16), v((8, 48, 64), BF16),
            v((2, 64, 128), jnp.int32), v((128, 128), F32), v((128, 128), BF16),
            v((2048, 128), BF16), v((512, 128), BF16), v((2048, 128), F32), v((2048, 128), F32),
            v((4096, 128), F32),
            v((2, 16, 8, 16, 128), BF16), v((2, 16, 8, 16, 128), BF16),
            v((2, 8, 16, 16, 128), BF16), v((1024, 256), BF16), v((1024, 256), F32),
            v((8, 16, 16, 128), BF16), v((8, 16, 16, 128), BF16), v((16, 8, 16, 128), BF16),
            v((256, 128), F32), v((16, 16, 128), BF16), v((16, 16, 128), BF16),
            v((64, 384), BF16), v((64, 768), F32), v((64, 768), F32), v((384, 64), BF16),
            v((64, 128), F32), v((4, 48, 128), F32), v((64, 512), F32), v((512, 768), F32),
            v((512, 768), BF16), v((192, 768), BF16), v((64, 512), F32), v((512, 128), F32),
            v((2, 8, 32, 128), BF16), v((8, 2, 8, 32, 128), BF16), v((48, 512), BF16),
            v((16, 48, 512), BF16), v((64, 512), F32), v((256, 128), F32), v((8, 256, 128), F32),
            v((8, 256, 128), F32),
            v((4, 16, 48, 128), BF16), v((4, 16, 48, 128), BF16), v((4, 2, 4, 4, 32, 128), BF16),
            v((4, 4, 4, 32, 128), BF16), v((4, 4, 4, 32, 128), BF16), v((4, 4, 4, 32, 128), BF16),
            v((4, 64, 128), BF16), v((128, 128), BF16), v((256, 128), F32), v((16, 16, 128), BF16),
            v((2, 16, 16, 128), BF16),
            v((64, 768), F32), v((64, 768), F32), v((64, 128), F32), v((8, 8, 384), F32),
            v((16, 8, 384), F32), v((2, 8, 384), F32), v((8, 384), F32), v((8, 8, 384), F32),
            dma((2, 16)), dma((2, 16)), dma((2, 8)), dma((2, 8)), dma((8,)), dma((8,)),
            dma((16,)), dma((16,)), dma((16,)), dma((16,)), dma((4,)), dma((4,)),
            dma((4,)), dma((4,)), dma((16,)), dma((16,)),
            dma((4, 16)), dma((4, 16)), dma((4,)), dma((4,)), dma((4, 4)), dma((4, 4)),
            dma((2, 16)), dma((2, 16)), dma((8,)), dma((16,)), dma((1,)), dma((1,)),
            dma((16,)), dma((8,)), dma((29,)), dma((4,)),
        ],
        compiler_params=pltpu.CompilerParams(
            collective_id=1, has_side_effects=True, vmem_limit_bytes=60 * 1024 * 1024
        ),
        name="step",
    )(
        residue_index, chain_index, token_mask, pair_in, relpos_weight, tri_proj, tri_out,
        bias_proj.T, single, ada_proj, noisy.reshape(512, 768), qkv_proj.transpose(1, 2, 0),
        out_proj, cotangent.transpose(0, 2, 1),
    )
    pair_out, block_t, grad_pair, grad_single = finished(
        (pair_out, block_t, grad_pair, grad_single)
    )
    return (
        pair_out,
        block_t.transpose(0, 2, 1),
        grad_pair.reshape(64, 32, 128),
        grad_single.reshape(64, 384),
    )


def solution(mesh):
    return jax.shard_map(
        on_device,
        mesh=mesh,
        in_specs=(
            P("row", "col", None), P(), P(), P(), P(), P(), P(), P(), P("row", None), P(),
            P("samp", "row", None), P(None, None, "col"), P("col", None), P("samp", "row", "col"),
        ),
        out_specs=(
            P("row", "col", None), P("samp", "row", "col"), P("row", "col", None), P("row", None),
        ),
        check_vma=False,
    )
```

```python
import jax
import jax.numpy as jnp
from jax import lax
from jax.experimental import pallas as pl
from jax.experimental.pallas import tpu as pltpu
from jax.sharding import PartitionSpec as P

HEAD_DIM = 48
REL_BINS = 66
EPSILON = 1e-05
MESH = pl.DeviceIdType.MESH
F32 = jnp.float32
BF16 = jnp.bfloat16
NCOL = 16
NROW = 8


def dg(a, b, ca, cb, **kw):
    return lax.dot_general(a, b, (((ca,), (cb,)), ((), ())), preferred_element_type=F32, **kw)


def place():
    return lax.axis_index("row"), lax.axis_index("col"), lax.axis_index("samp")


def rmod(a, n):
    return lax.rem(a, n)


def ring_shift(oz, from_core):
    if oz == 2:
        return 2 + 4 * from_core
    return (0, 1, None, 7)[oz]


def row_dest(oz, cx):
    row, col, samp = place()
    z, core = samp * 4 + row // 2, rmod(row, 2)
    to_core = rmod(core + cx, 2)
    to_z = rmod(z + ring_shift(oz, core), 8)
    return rmod(to_z, 4) * 2 + to_core, col, to_z // 4


def row_source(oz, cx):
    row, col, samp = place()
    z, core = samp * 4 + row // 2, rmod(row, 2)
    from_core = rmod(core + cx, 2)
    from_z = rmod(z + 8 - ring_shift(oz, from_core), 8)
    return rmod(from_z, 4) * 2 + from_core, col, from_z // 4


def spot(row):
    return rmod(row, 2) * 4 + row // 2


ROW_IDS = [(oz, cx) for oz in range(4) for cx in range(2) if (oz, cx) != (0, 0)]


def remote(src, dst, ssem, rsem, to):
    return pltpu.make_async_remote_copy(
        src_ref=src, dst_ref=dst, send_sem=ssem, recv_sem=rsem, device_id=to, device_id_type=MESH
    )


def col_start(src_of, slot_of, ssem, rsem):
    row, col, samp = place()

    def one(o, _):
        to = rmod(col + o, NCOL)
        remote(src_of(to), slot_of(col), ssem.at[o], rsem.at[o], (row, to, samp)).start()
        return 0

    lax.fori_loop(1, NCOL, one, 0)


def col_wait(src_of, slot_of, ssem, rsem, recv=True, send=True):
    row, col, samp = place()

    def one(o, _):
        to = rmod(col + o, NCOL)
        came = rmod(col + NCOL - o, NCOL)
        if recv:
            remote(src_of(to), slot_of(came), ssem.at[o], rsem.at[o], (row, to, samp)).wait_recv()
        if send:
            remote(src_of(to), slot_of(came), ssem.at[o], rsem.at[o], (row, to, samp)).wait_send()
        return 0

    lax.fori_loop(1, NCOL, one, 0)


def row_start(src_of, slot_of, ssem, rsem):
    row = lax.axis_index("row")
    for oz, cx in ROW_IDS:
        to = row_dest(oz, cx)
        i = oz * 2 + cx
        remote(src_of(to[0]), slot_of(row), ssem.at[i], rsem.at[i], to).start()


def row_wait(src_of, slot_of, ssem, rsem, recv=True, send=True):
    for oz, cx in ROW_IDS:
        to, came = row_dest(oz, cx), row_source(oz, cx)
        i = oz * 2 + cx
        copy = remote(src_of(to[0]), slot_of(came[0]), ssem.at[i], rsem.at[i], to)
        if recv:
            copy.wait_recv()
        if send:
            copy.wait_send()


def signal(sem, to):
    pl.semaphore_signal(sem, inc=1, device_id=to, device_id_type=MESH)


def both(x, low, first):
    turned = pltpu.roll(x, 64, 1)
    return jnp.where(low, x, turned) if first else jnp.where(low, turned, x)


def sigmoid(x):
    return 0.5 * jnp.tanh(0.5 * x) + 0.5


def layer_norm(x, axis):
    mean = jnp.mean(x, axis, keepdims=True)
    cent = x - mean
    var = jnp.mean(cent * cent, axis, keepdims=True)
    return cent * lax.rsqrt(var + EPSILON)


def two_parts(x):
    coarse = x.astype(BF16)
    return jnp.concatenate([coarse, (x - coarse.astype(F32)).astype(BF16)], 0)


def step_kernel(
    res_ref, chain_ref, mask_ref,
    pair_hbm, relpos_hbm, tri_hbm, triout_hbm, biasp_hbm, single_hbm, ada_hbm, noisy_hbm,
    qkvw_hbm, outp_hbm, cot_hbm,
    pairout_hbm, block_hbm, gpair_hbm, gsingle_hbm,
    pairout_ref, block_ref, gpair_ref,
    pair_in, tri_w, ada_w, noisy, relpos_ref, triout_ref, biasp_ref, single_ref, qkvw_ref, outp_ref,
    cot_ref, idx_r, mrow, relpos_w,
    zl_s, tri_t, pf, gate, lrf, lbuf, recv_a, got, rcat, mtmp, tbuf, got_c, got_d, bias_f, bias_b, bias_got,
    cvec_s, scale_s, shift_s, wg_s, gate_t, g_t, noisy_t, normed, hidden, wqkv, q_t, kv_f,
    kv_own, kv_all, dmx_own, dmx_all, da_t, keyok, sraw, draw,
    mix_s, mix_r, dkv_s, dkv_m, dkv_o, dkv_r, dq_t, dkv_tok, dbias, db_s, db_r,
    dsc, dsh, dga, dc_s, dc_r, dc_p, gs_own, gs_all,
    sa, ra, sb, rb, sc, rc, sd, rd, se, re, skv, rkv, skf, rkf, sdm, rdm,
    sm, rm, sk, rk, sko, rko, sbb, rbb, st, rt, sp, rp_, sg, rg, loc, locm, ready,
):
    row, col, samp = place()
    core = rmod(row, 2)
    zlo = row // 2
    mate = (row + 1 - 2 * core, col, samp)
    far = (row, col, 1 - samp)
    barrier = pltpu.get_barrier_semaphore()

    loads = [
        pltpu.make_async_copy(s, d, loc.at[18 + i])
        for i, (s, d) in enumerate(
            [
                (pair_hbm, pair_in), (relpos_hbm, relpos_ref), (tri_hbm, tri_w),
                (single_hbm, single_ref), (qkvw_hbm, qkvw_ref), (ada_hbm, ada_w),
                (noisy_hbm, noisy), (cot_hbm, cot_ref), (triout_hbm, triout_ref),
                (biasp_hbm, biasp_ref), (outp_hbm, outp_ref),
            ]
        )
    ]
    for copy in loads:
        copy.start()
    for oz, cx in ROW_IDS:
        signal(barrier, row_source(oz, cx))

    def greet(o, _):
        signal(barrier, (row, rmod(col + o, NCOL), samp))
        return 0

    def greet_row(o, _):
        signal(barrier, (rmod(row + o, NROW), col, samp))
        return 0

    lax.fori_loop(1, NCOL, greet, 0)
    lax.fori_loop(1, NROW, greet_row, 0)
    signal(barrier, far)

    low = lax.broadcasted_iota(jnp.int32, (64, 128), 1) < 64
    low16 = lax.broadcasted_iota(jnp.int32, (16, 128), 1) < 64
    low1 = lax.broadcasted_iota(jnp.int32, (1, 128), 1) < 64
    diag = (lax.broadcasted_iota(jnp.int32, (128, 128), 0) < 64) == (
        lax.broadcasted_iota(jnp.int32, (128, 128), 1) < 64
    )

    def blockdiag(x):
        return jnp.where(diag, jnp.concatenate([x, x], 0), 0.0).astype(BF16)

    def indices(i, _):
        at = pl.ds(i, 1)
        idx_r[0, at, :] = jnp.full((1, 128), res_ref[row * 64 + i], jnp.int32)
        idx_r[1, at, :] = jnp.full((1, 128), chain_ref[row * 64 + i], jnp.int32)
        m = jnp.full((1, 128), mask_ref[row * 64 + i].astype(F32), F32)
        mrow[at, :] = m
        mrow[pl.ds(64 + i, 1), :] = m
        return 0

    lax.fori_loop(0, 64, indices, 0, unroll=4)
    mrow[...] = mrow[...].T
    relpos_w[...] = jnp.zeros_like(relpos_w)
    loads[1].wait()
    relpos_w[0:REL_BINS, :] = relpos_ref[...]
    loads[0].wait()

    def load(i, _):
        pf[pl.ds(i * 32, 32), :] = pair_in[i].astype(F32)
        return 0

    lax.fori_loop(0, 64, load, 0, unroll=4)
    bins = lax.broadcasted_iota(jnp.int32, (64, 128), 1)

    def normed_rows(t, _):
        parts = []
        for q in range(2):
            for hi in range(2):
                j = 2 * t + q + 16 * hi
                off = jnp.clip(idx_r[0] - res_ref[col * 32 + j] + 32, 0, 64)
                bucket = jnp.where(idx_r[1] == chain_ref[col * 32 + j], off, REL_BINS - 1)
                onehot = jnp.where(bucket == bins, 1.0, 0.0).astype(BF16)
                parts.append(
                    pf[pl.ds(j, 64, stride=32), :]
                    + jnp.dot(onehot, relpos_w[...], preferred_element_type=F32)
                )
        for q in range(2):
            for hi in range(2):
                pf[pl.ds(2 * t + q + 16 * hi, 64, stride=32), :] = parts[2 * q + hi]
        at = pl.ds(pl.multiple_of(t * 256, 256), 256)
        zl_s[at, :] = layer_norm(jnp.concatenate(parts, 0), -1).astype(BF16)
        return 0

    lax.fori_loop(0, 8, normed_rows, 0, unroll=2)
    loads[2].wait()
    tri_t[...] = tri_w[:, :512].astype(F32).T.astype(BF16)

    def project(h, t):
        at = pl.ds(pl.multiple_of(t * 256, 256), 256)
        pt = dg(tri_t[h * 256 : h * 256 + 256, :], zl_s[at, :], 1, 1)
        val = sigmoid(pt[128:]) * pt[:128]
        for q in range(2):
            lo = 2 * t + q
            mask = mrow[0:1, :] * jnp.where(
                low1, mask_ref[col * 32 + lo].astype(F32), mask_ref[col * 32 + 16 + lo].astype(F32)
            )
            lrf[pl.ds(h * 2048 + lo, 128, stride=16), :] = val[:, q * 128 : q * 128 + 128] * mask

    pieces = [(0, slice(0, 8)), (1, slice(0, 4)), (1, slice(4, 8))]
    a_src = [lambda to, h=h, p=p: lbuf.at[h, to, p] for h, p in pieces]
    a_slot = [lambda c, h=h, p=p: recv_a.at[h, c, p] for h, p in pieces]
    b_src = [lambda r, h=h: recv_a.at[h, :, spot(r)] for h in range(2)]
    b_slot = [lambda r, h=h: got.at[h, r] for h in range(2)]
    own_a = [pltpu.make_async_copy(lbuf.at[h, col], recv_a.at[h, col], loc.at[h]) for h in range(2)]
    own_b = [
        pltpu.make_async_copy(recv_a.at[h, :, spot(row)], got.at[h, row], loc.at[2 + h])
        for h in range(2)
    ]
    for h in range(2):

        def one_side(t, _):
            project(h, t)
            return 0

        lax.fori_loop(0, 8, one_side, 0, unroll=2)

        def pack(c, _):
            lbuf[h, c] = lrf[pl.ds(h * 2048 + c * 128, 128), :].astype(BF16).reshape(8, 16, 128)
            return 0

        lax.fori_loop(0, 16, pack, 0, unroll=2)
        if h == 0:
            pl.semaphore_wait(barrier, 7 + 15 + 7 + 1)
            signal(ready, far)
        own_a[h].start()
        for i in ((0,), (1, 2))[h]:
            col_start(a_src[i], a_slot[i], sa.at[i], ra.at[i])

    for copy in loads[3:6]:
        copy.wait()
    cvec = layer_norm(single_ref[...].astype(F32), -1).astype(BF16)
    cvec_s[...] = cvec
    wqkv[...] = jnp.zeros_like(wqkv)
    for p in range(3):
        wqkv[p * 64 : p * 64 + 48, :] = qkvw_ref[p]
    scale_s[...] = sigmoid(jnp.dot(cvec, ada_w[:, :768], preferred_element_type=F32))
    shift_s[...] = jnp.dot(cvec, ada_w[:, 768:1536], preferred_element_type=F32)
    for copy in loads[6:]:
        copy.wait()

    def sample(s, _):
        at = pl.ds(pl.multiple_of(s * 64, 64), 64)
        n = layer_norm(noisy[at, :].astype(F32), -1)
        normed[at, :] = n
        hidden[at, :] = (scale_s[...] * n + shift_s[...]).astype(BF16)
        return 0

    lax.fori_loop(0, 8, sample, 0)
    own_a[0].wait()
    col_wait(a_src[0], a_slot[0], sa.at[0], ra.at[0])
    own_b[0].start()
    row_start(b_src[0], b_slot[0], sb.at[0], rb.at[0])

    feat = lax.broadcasted_iota(jnp.int32, (768, 64), 1)
    sel = jnp.where(
        (lax.broadcasted_iota(jnp.int32, (768, 64), 0) == col * 48 + feat) & (feat < 48), 1.0, 0.0
    ).astype(BF16)
    wg_s[...] = jnp.dot(ada_w[:, 1536:], sel, preferred_element_type=F32).astype(BF16)
    gate_t[...] = sigmoid(
        dg(wg_s[...], jnp.concatenate([cvec_s[...], cvec_s[...]], 0), 0, 1)
    )
    lane = lax.broadcasted_iota(jnp.int32, (64, 128), 1)
    tok = lax.broadcasted_iota(jnp.int32, (64, 128), 0)
    put = [jnp.where(lane == tok + 64 * h, 1.0, 0.0).astype(BF16) for h in range(2)]
    for u in range(4):
        g = jnp.dot(cot_ref[2 * u], put[0], preferred_element_type=F32) + jnp.dot(
            cot_ref[2 * u + 1], put[1], preferred_element_type=F32
        )
        g_t[u] = g
        dmx_own[:, u * 128 : u * 128 + 128] = (g * gate_t[:48, :]).astype(BF16)
    dm_src, dm_slot = (lambda to: dmx_own), (lambda c: dmx_all.at[c])
    dm_keep = pltpu.make_async_copy(dmx_own, dmx_all.at[col], loc.at[5])
    dm_keep.start()
    col_start(dm_src, dm_slot, sdm, rdm)
    kv_f[...] = dg(hidden[...], wqkv[64:, :], 1, 1)

    def kv_pack(t, _):
        r0 = kv_f[pl.ds(t * 32, 16), :]
        r1 = kv_f[pl.ds(t * 32 + 16, 16), :]
        to = pl.ds(pl.multiple_of(rmod(t, 2) * 16, 16), 16)
        kv_own[0, t // 2, to, :] = jnp.where(low16, r0, pltpu.roll(r1, 64, 1)).astype(BF16)
        kv_own[1, t // 2, to, :] = jnp.where(low16, pltpu.roll(r0, 64, 1), r1).astype(BF16)
        return 0

    lax.fori_loop(0, 16, kv_pack, 0, unroll=2)
    kv_keep = pltpu.make_async_copy(kv_own, kv_all.at[row], loc.at[4])
    kv_keep.start()
    kv_out = []
    for o in range(1, 4):
        to = (rmod(zlo + o, 4) * 2 + core, col, samp)
        kv_out.append(remote(kv_own, kv_all.at[row], skv.at[o], rkv.at[o], to))
    kv_mate = remote(kv_own, kv_all.at[row], skf.at[0], rkf.at[0], mate)
    own_a[1].wait()
    for k in range(2):
        col_wait(a_src[1 + k], a_slot[1 + k], sa.at[1 + k], ra.at[1 + k])
        cx = rmod(core + k, 2)
        for oz in (2, 1, 3):
            to = row_dest(oz, cx)
            i = oz * 2 + cx
            remote(b_src[1](to[0]), b_slot[1](row), sb.at[1, i], rb.at[1, i], to).start()

        @pl.when(cx == 1)
        def _():
            remote(b_src[1](mate[0]), b_slot[1](row), sb.at[1, 1], rb.at[1, 1], mate).start()

    own_b[1].start()

    def gates(t, _):
        at = pl.ds(pl.multiple_of(t * 256, 256), 256)
        gate[at, :] = sigmoid(
            jnp.dot(zl_s[at, :], tri_w[:, 512:], preferred_element_type=F32)
        )
        return 0

    lax.fori_loop(0, 8, gates, 0)
    for h in (1, 0):
        own_b[h].wait()
        row_wait(b_src[h], b_slot[h], sb.at[h], rb.at[h])

    def turn(r, _):
        rcat[pl.ds(pl.multiple_of(r * 128, 128), 128), :] = (
            got[1, r].reshape(256, 128).astype(F32).T.astype(BF16)
        )
        return 0

    lax.fori_loop(0, 8, turn, 0)

    c_src = [lambda r, p=p: tbuf.at[r, p] for p in (slice(0, 8), slice(8, 16))]
    c_slot = [lambda r, p=p: got_c.at[spot(r), p] for p in (slice(0, 8), slice(8, 16))]
    own_c = [
        pltpu.make_async_copy(c_src[h](row), c_slot[h](row), loc.at[6 + 3 * h]) for h in range(2)
    ]

    def tri(rp, part):
        rhs = jnp.concatenate(
            [got[0, 2 * rp].reshape(256, 128), got[0, 2 * rp + 1].reshape(256, 128)], 1
        )
        mtmp[...] = jnp.dot(
            rcat[part * 512 : part * 512 + 512, :], rhs, preferred_element_type=F32
        )

        def out(rj, _):
            for half in range(2):
                top = mtmp[pl.ds(rj * 128, 64), half * 128 : half * 128 + 128]
                bot = mtmp[pl.ds(rj * 128 + 64, 64), half * 128 : half * 128 + 128]
                for jh in range(2):
                    a = slice(jh * 32, jh * 32 + 16)
                    b = slice(jh * 32 + 16, jh * 32 + 32)
                    t = jnp.where(
                        low16,
                        top[a] + pltpu.roll(bot[a], 64, 1),
                        pltpu.roll(top[b], 64, 1) + bot[b],
                    )
                    tbuf[2 * rp + half, part * 8 + 2 * rj + jh] = t.astype(BF16)
            return 0

        lax.fori_loop(0, 4, out, 0, unroll=2)

    for part in range(2):
        for oz in (2, 1, 3, 0):
            tri(rmod(zlo + oz, 4), part)
            for cx in range(2):
                if (oz, cx) != (0, 0):
                    to = row_dest(oz, cx)
                    i = oz * 2 + cx
                    remote(
                        c_src[part](to[0]), c_slot[part](row), sc.at[part, i], rc.at[part, i], to
                    ).start()
        own_c[part].start()
    kv_mate.start()
    for copy in kv_out:
        copy.start()
    d_own = pltpu.make_async_copy(got_c.at[:, col], got_d.at[col], loc.at[7])

    def d_copy(part, o):
        to = part * 8 + rmod(col + o, 8)
        return to, remote(
            got_c.at[:, to], got_d.at[col], sd.at[part, o], rd.at[col], (row, to, samp)
        )

    def d_start(part):
        def one(o, _):
            to, copy = d_copy(part, o)

            @pl.when(to != col)
            def _():
                copy.start()

            return 0

        lax.fori_loop(0, 8, one, 0)

    def d_wait():
        def came(o, _):
            c = rmod(col + o, NCOL)
            remote(got_c.at[:, c], got_d.at[c], sd.at[0, 0], rd.at[c], mate).wait_recv()
            return 0

        lax.fori_loop(1, NCOL, came, 0)
        for part in range(2):

            def sent(o, _):
                to, copy = d_copy(part, o)

                @pl.when(to != col)
                def _():
                    copy.wait_send()

                return 0

            lax.fori_loop(0, 8, sent, 0)

    dm_keep.wait()
    col_wait(dm_src, dm_slot, sdm, rdm)
    da_t[...] = jnp.zeros_like(da_t)
    da_t[:48, :] = (
        jnp.dot(outp_ref[...], dmx_all[...].reshape(768, 512), preferred_element_type=F32)
        .astype(BF16)
        .astype(F32)
    )
    for part in range(2):
        own_c[part].wait()
        row_wait(c_src[part], c_slot[part], sc.at[part], rc.at[part])
        d_start(part)
    d_own.start()

    q_t[...] = dg(wqkv[:64, :], hidden[...], 1, 1)
    noisy_t[...] = dg(sel, noisy[...], 0, 1)

    def key_mask(t, _):
        jb, lo = t // 16, rmod(t, 16)
        keyok[pl.ds(t, 1), :] = jnp.where(
            low1,
            mask_ref[jb * 32 + lo].astype(F32),
            mask_ref[jb * 32 + 16 + lo].astype(F32),
        )
        return 0

    lax.fori_loop(0, 256, key_mask, 0, unroll=4)

    for o in range(1, 4):
        came = rmod(zlo + 4 - o, 4) * 2 + core
        remote(kv_own, kv_all.at[came], skv.at[o], rkv.at[o], mate).wait_recv()
        remote(kv_all.at[came], kv_all.at[came], skf.at[o], rkf.at[o], mate).start()


    def half_of(ref, u, sh):
        tile = ref[:, pl.ds(pl.multiple_of(u * 128, 128), 128)].astype(F32)
        return blockdiag(both(tile, low, sh == 0))

    def keys(which, s):
        return jnp.concatenate([kv_all[r, which, s] for r in range(NROW)], 0)

    def raw(u, _):
        for sh in range(2):
            s = 2 * u + sh
            sraw[s] = jnp.dot(keys(0, s), half_of(q_t, u, sh), preferred_element_type=F32)
            draw[s] = jnp.dot(keys(1, s), half_of(da_t, u, sh), preferred_element_type=F32)
        return 0

    d_own.wait()
    d_wait()

    def widen(c, _):
        lrf[pl.ds(c * 128, 128), :] = got_d[c].reshape(128, 128).astype(F32)
        return 0

    lax.fori_loop(0, 16, widen, 0)

    def stage3(t, _):
        tn = layer_norm(
            jnp.concatenate([lrf[pl.ds(2 * t + q, 128, stride=16), :] for q in range(2)], 1), 0
        ).astype(BF16)
        upd = dg(tn, triout_ref[...], 0, 0) * gate[pl.ds(pl.multiple_of(t * 256, 256), 256), :]
        spots = [pl.ds(2 * t + q + 16 * hi, 64, stride=32) for q in range(2) for hi in range(2)]
        outs = [
            (pf[at, :] + upd[i * 64 : i * 64 + 64]).astype(BF16) for i, at in enumerate(spots)
        ]
        for at, val in zip(spots, outs):
            pf[at, :] = val.astype(F32)
        tile = dg(biasp_ref[...], jnp.concatenate(outs, 0), 1, 1)
        for q in range(2):
            bias_f[pl.ds(2 * t + q, 16, stride=16), :] = tile[:, q * 128 : q * 128 + 128]
        return 0

    lax.fori_loop(0, 8, stage3, 0, unroll=2)
    bias_b[...] = bias_f[...].astype(BF16).reshape(16, 16, 128)
    e_src, e_slot = (lambda c: bias_b.at[c]), (lambda c: bias_got.at[c])
    own_e = pltpu.make_async_copy(bias_b.at[col], bias_got.at[col], loc.at[8])
    own_e.start()
    col_start(e_src, e_slot, se, re)

    kv_keep.wait()
    for copy in kv_out:
        copy.wait_send()
    kv_mate.wait_send()
    for o in range(4):
        came = rmod(zlo + 4 - o, 4) * 2
        remote(
            kv_all.at[came + core], kv_all.at[came + 1 - core], skf.at[o], rkf.at[o], mate
        ).wait_recv()
        if o > 0:
            remote(
                kv_all.at[came + core], kv_all.at[came + core], skf.at[o], rkf.at[o], mate
            ).wait_send()
    lax.fori_loop(0, 4, raw, 0)
    def store(i, _):
        pairout_ref[i] = pf[pl.ds(i * 32, 32), :].astype(BF16)
        return 0

    lax.fori_loop(0, 64, store, 0, unroll=4)
    out_pair = pltpu.make_async_copy(pairout_ref, pairout_hbm, loc.at[14])
    out_pair.start()
    dbias[...] = jnp.zeros_like(dbias)
    own_e.wait()
    col_wait(e_src, e_slot, se, re)

    scale = 1.0 / HEAD_DIM**0.5

    def mix_src(u):
        return lambda f: mix_s.at[u, f]

    def mix_slot(u):
        return lambda h: mix_r.at[u, h]

    def to_mate(u):
        return remote(dkv_s.at[:, 1 - core, u], dkv_m.at[u], sk.at[u], rk.at[u], mate)

    def to_chip(u, o):
        z = rmod(zlo + o, 4)
        return remote(
            dkv_o.at[u, z], dkv_r.at[u, zlo], sko.at[u, o], rko.at[u, o], (z * 2 + core, col, samp)
        )

    def pass_on(u):
        to_mate(u).wait_recv()
        for z in range(4):
            dkv_o[u, z] = (
                dkv_s[z, core, u].astype(F32) + dkv_m[u, z].astype(F32)
            ).astype(BF16)
        for o in range(1, 4):
            to_chip(u, o).start()

    def pair_of_samples(u, _):
        folded, dqs = [], []
        for sh in range(2):
            s = 2 * u + sh
            kp, vp = keys(0, s), keys(1, s)
            qq, dd = half_of(q_t, u, sh), half_of(da_t, u, sh)
            sco = sraw[s] * scale + bias_got[...].reshape(256, 128).astype(F32)
            sco = jnp.where(keyok[...] > 0, sco, -1000000000.0)
            top = jnp.max(sco, 0, keepdims=True)
            top = jnp.maximum(top, pltpu.roll(top, 64, 1))
            ex = jnp.exp(sco - top)
            tot = jnp.sum(ex, 0, keepdims=True)
            probs = ex * (1.0 / (tot + pltpu.roll(tot, 64, 1)))
            pb = probs.astype(BF16)
            folded.append(dg(vp, pb, 0, 0))
            dp = draw[s]
            dot = jnp.sum(probs * dp, 0, keepdims=True)
            ds = probs * (dp - (dot + pltpu.roll(dot, 64, 1)))
            dbias[...] += ds
            dsb = (ds * scale).astype(BF16)
            dqs.append(dg(kp, dsb, 0, 0))
            dk = dg(dsb, qq, 1, 1).astype(BF16)
            dv = dg(pb, dd, 1, 1).astype(BF16)
            for r in range(NROW):
                dkv_s[r // 2, r % 2, u, sh] = dk[r * 32 : r * 32 + 32]
                dkv_s[r // 2, r % 2, u, 2 + sh] = dv[r * 32 : r * 32 + 32]

        def fold(m0, m1):
            return jnp.where(
                low,
                m0[:64] + pltpu.roll(m0[64:], 64, 1),
                pltpu.roll(m1[:64], 64, 1) + m1[64:],
            ).astype(BF16)

        att = fold(*folded)
        dq_t[u] = fold(*dqs)
        mix_s[u] = dg(outp_ref[...], att[:48], 0, 0).astype(BF16).reshape(16, 48, 128)
        pltpu.make_async_copy(mix_s.at[u, col], mix_r.at[u, col], locm.at[u]).start()
        to_mate(u).start()
        col_start(mix_src(u), mix_slot(u), sm.at[u], rm.at[u])

        @pl.when(u > 0)
        def _():
            pass_on(u - 1)

        return 0

    lax.fori_loop(0, 4, pair_of_samples, 0)

    db_s[...] = dbias[...].astype(BF16).reshape(16, 16, 128)
    own_db = pltpu.make_async_copy(db_s.at[col], db_r.at[samp, col], loc.at[29])
    own_db.start()

    def db_copy(o):
        to = rmod(col + o, NCOL)
        return remote(
            db_s.at[to], db_r.at[samp, col], sbb.at[1, o], rbb.at[1, o], (row, to, 1 - samp)
        )

    def db_send(o, _):
        db_copy(o).start()
        return 0

    pass_on(3)
    pl.semaphore_wait(ready, 1)
    lax.fori_loop(0, NCOL, db_send, 0)
    near_src, near_slot = (lambda c: db_s.at[c]), (lambda c: db_r.at[samp, c])
    col_start(near_src, near_slot, sbb.at[0], rbb.at[0])

    dga[...] = jnp.zeros_like(dga)

    def mixed_of(u, _):
        pltpu.make_async_copy(mix_s.at[u, col], mix_r.at[u, col], locm.at[u]).wait()
        col_wait(mix_src(u), mix_slot(u), sm.at[u], rm.at[u])
        total = mix_r[u, 0].astype(F32)
        for h in range(1, NCOL):
            total = total + mix_r[u, h].astype(F32)
        lanes = pl.ds(pl.multiple_of(u * 128, 128), 128)
        out = noisy_t[:48, lanes] + gate_t[:48, :] * total
        block_ref[2 * u] = out[:, :64].astype(BF16)
        block_ref[2 * u + 1] = pltpu.roll(out, 64, 1)[:, :64].astype(BF16)
        dga[:48, :] += g_t[u] * total
        return 0

    lax.fori_loop(0, 3, mixed_of, 0)

    dsc[...] = jnp.zeros_like(dsc)
    dsh[...] = jnp.zeros_like(dsh)

    def hidden_grad(u, _):
        to_mate(u).wait_send()
        for o in range(1, 4):
            came = rmod(zlo + 4 - o, 4)
            remote(
                dkv_o.at[u, came], dkv_r.at[u, came], sko.at[u, o], rko.at[u, o], mate
            ).wait_recv()
            to_chip(u, o).wait_send()
        dkv_r[u, zlo] = dkv_o[u, zlo]
        tot = dkv_r[u, 0].astype(F32)
        for z in range(1, 4):
            tot = tot + dkv_r[u, z].astype(F32)
        for sh in range(2):
            for jb in range(2):
                a = tot[sh, jb * 16 : jb * 16 + 16]
                b = tot[2 + sh, jb * 16 : jb * 16 + 16]
                base = sh * 64 + jb * 32
                dkv_tok[base : base + 16, :] = jnp.where(low16, a, pltpu.roll(b, 64, 1)).astype(BF16)
                dkv_tok[base + 16 : base + 32, :] = jnp.where(
                    low16, pltpu.roll(a, 64, 1), b
                ).astype(BF16)
        dh = dg(dq_t[u], wqkv[:64, :], 0, 0) + jnp.dot(
            dkv_tok[...], wqkv[64:, :], preferred_element_type=F32
        )
        n = normed[pl.ds(pl.multiple_of(u * 128, 128), 128), :]
        w = dh * n
        dsc[...] += w[:64] + w[64:]
        dsh[...] += dh[:64] + dh[64:]
        return 0

    lax.fori_loop(0, 3, hidden_grad, 0)
    mixed_of(3, 0)
    out_block = pltpu.make_async_copy(block_ref, block_hbm, loc.at[15])
    out_block.start()
    hidden_grad(3, 0)
    sg_ = scale_s[...]
    part = dg(two_parts(dsc[...] * sg_ * (1.0 - sg_)), ada_w[:, :768], 1, 1)
    part = part + dg(two_parts(dsh[...]), ada_w[:, 768:1536], 1, 1)
    part = part[:64] + part[64:]
    acc = dga[...]
    acc = (acc + pltpu.roll(acc, 64, 1)) * gate_t[...] * (1.0 - gate_t[...])
    coarse = acc.astype(BF16)
    fine = (acc - coarse.astype(F32)).astype(BF16)
    part = part + (dg(coarse, wg_s[...], 0, 1) + dg(fine, wg_s[...], 0, 1))[:64]
    dc_s[...] = part.reshape(8, 8, 384)

    half_col = col // 2
    even = rmod(col, 2) == 0

    def part_copy(o):
        g = rmod(half_col + o, 8)
        return remote(dc_s.at[g], dc_r.at[col], st.at[o], rt.at[col], (row, 2 * g, samp))

    @pl.when(jnp.logical_not(even))
    def _():
        part_copy(0).start()

    def part_send(o, _):
        part_copy(o).start()
        return 0

    lax.fori_loop(1, 8, part_send, 0)

    own_db.wait()
    col_wait(near_src, near_slot, sbb.at[0], rbb.at[0])

    def db_wait(o, _):
        came = rmod(col + NCOL - o, NCOL)
        remote(db_s.at[came], db_r.at[1 - samp, came], sbb.at[1, o], rbb.at[1, o], far).wait_recv()
        db_copy(o).wait_send()
        return 0

    lax.fori_loop(0, NCOL, db_wait, 0)
    dbias[...] = (db_r[0].astype(F32) + db_r[1].astype(F32)).reshape(256, 128)
    biasp3 = jnp.concatenate([biasp_ref[...]] * 3, 0)

    def grad(lo, _):
        d = dbias[pl.ds(lo, 16, stride=16), :]
        d1 = d.astype(BF16)
        rest = d - d1.astype(F32)
        d2 = rest.astype(BF16)
        d3 = (rest - d2.astype(F32)).astype(BF16)
        g = dg(jnp.concatenate([d1, d2, d3], 0), biasp3, 0, 0)
        for hi in range(2):
            gpair_ref[pl.ds(lo + 16 * hi, 64, stride=32), :] = g[hi * 64 : hi * 64 + 64]
        return 0

    lax.fori_loop(0, 16, grad, 0, unroll=2)
    out_grad = pltpu.make_async_copy(gpair_ref, gpair_hbm, loc.at[16])
    out_grad.start()

    def own_copy(o):
        return remote(
            gs_own, gs_all.at[half_col], sg.at[o], rg.at[half_col], (row, rmod(col + o, NCOL), samp)
        )

    @pl.when(even)
    def _():
        dc_r[col] = dc_s[half_col]

        def arrived(o, _):
            came = rmod(col + o, NCOL)
            remote(dc_s.at[0], dc_r.at[came], st.at[0], rt.at[came], far).wait_recv()
            return 0

        lax.fori_loop(1, NCOL, arrived, 0)
        tot = dc_r[0]
        for c in range(1, NCOL):
            tot = tot + dc_r[c]
        dc_p[samp] = tot
        other = remote(dc_p.at[samp], dc_p.at[samp], sp.at[0], rp_.at[0], far)
        other.start()
        own = single_ref[...].astype(F32).reshape(8, 8, 384)
        mine = jnp.zeros((8, 384), F32)
        for g in range(8):
            mine = mine + jnp.where(half_col == g, own[g], 0.0)
        mean = jnp.mean(mine, -1, keepdims=True)
        cent = mine - mean
        inv = lax.rsqrt(jnp.mean(cent * cent, -1, keepdims=True) + EPSILON)
        unit = cent * inv
        remote(dc_p.at[samp], dc_p.at[1 - samp], sp.at[0], rp_.at[0], far).wait_recv()
        other.wait_send()
        up = dc_p[0] + dc_p[1]
        gs_own[...] = inv * (
            up - jnp.mean(up, -1, keepdims=True) - unit * jnp.mean(up * unit, -1, keepdims=True)
        )

        def tell(o, _):
            own_copy(o).start()
            return 0

        lax.fori_loop(1, NCOL, tell, 0)
        gs_all[half_col] = gs_own[...]

    @pl.when(jnp.logical_not(even))
    def _():
        part_copy(0).wait_send()

    def part_sent(o, _):
        part_copy(o).wait_send()
        return 0

    lax.fori_loop(1, 8, part_sent, 0)

    @pl.when(even)
    def _():
        def told(o, _):
            own_copy(o).wait_send()
            return 0

        lax.fori_loop(1, NCOL, told, 0)

    def total_came(g):
        remote(gs_own, gs_all.at[g], sg.at[0], rg.at[g], far).wait_recv()

    @pl.when(jnp.logical_not(even))
    def _():
        total_came(half_col)

    def came_from(o, _):
        total_came(rmod(half_col + o, 8))
        return 0

    lax.fori_loop(1, 8, came_from, 0)
    out_single = pltpu.make_async_copy(gs_all, gsingle_hbm, loc.at[17])
    out_single.start()
    for copy in (out_pair, out_block, out_grad, out_single):
        copy.wait()


def finish_kernel(*refs):
    n = 4
    ins, outs, bufs = refs[:n], refs[n : 2 * n], refs[2 * n : 3 * n]
    got, put = refs[3 * n], refs[3 * n + 1]
    reads = [pltpu.make_async_copy(ins[i], bufs[i], got.at[i]) for i in range(n)]
    writes = [pltpu.make_async_copy(bufs[i], outs[i], put.at[i]) for i in range(n)]
    for copy in reads:
        copy.start()
    for i in (3, 1, 0, 2):
        reads[i].wait()
        writes[i].start()
    for copy in writes:
        copy.wait()


def finished(arrays):
    hbm = pl.BlockSpec(memory_space=pl.ANY)
    return pl.pallas_call(
        finish_kernel,
        out_shape=[jax.ShapeDtypeStruct(x.shape, x.dtype) for x in arrays],
        in_specs=[hbm] * 4,
        out_specs=[hbm] * 4,
        scratch_shapes=[pltpu.VMEM(x.shape, x.dtype) for x in arrays]
        + [pltpu.SemaphoreType.DMA((4,)), pltpu.SemaphoreType.DMA((4,))],
        compiler_params=pltpu.CompilerParams(vmem_limit_bytes=60 * 1024 * 1024),
        name="finish",
    )(*arrays)


def on_device(
    pair_in, residue_index, chain_index, token_mask, relpos_weight, tri_proj, tri_out, bias_proj,
    single, ada_proj, noisy, qkv_proj, out_proj, cotangent,
):
    sm = pl.BlockSpec(memory_space=pltpu.SMEM)
    hbm = pl.BlockSpec(memory_space=pl.ANY)
    dma = pltpu.SemaphoreType.DMA
    v = pltpu.VMEM
    pair_out, block_t, grad_pair, grad_single = pl.pallas_call(
        step_kernel,
        out_shape=(
            jax.ShapeDtypeStruct((64, 32, 128), BF16),
            jax.ShapeDtypeStruct((8, 48, 64), BF16),
            jax.ShapeDtypeStruct((2048, 128), F32),
            jax.ShapeDtypeStruct((8, 8, 384), F32),
        ),
        in_specs=[sm] * 3 + [hbm] * 11,
        out_specs=(hbm,) * 4,
        scratch_shapes=[
            v((64, 32, 128), BF16), v((8, 48, 64), BF16), v((2048, 128), F32),
            v((64, 32, 128), BF16), v((128, 640), BF16), v((384, 2304), BF16), v((512, 768), BF16),
            v((REL_BINS, 128), BF16), v((128, 128), BF16), v((16, 128), BF16), v((64, 384), BF16),
            v((3, 48, 768), BF16), v((48, 768), BF16), v((8, 48, 64), BF16),
            v((2, 64, 128), jnp.int32), v((128, 128), F32), v((128, 128), BF16),
            v((2048, 128), BF16), v((512, 128), BF16), v((2048, 128), F32), v((2048, 128), F32),
            v((4096, 128), F32),
            v((2, 16, 8, 16, 128), BF16), v((2, 16, 8, 16, 128), BF16),
            v((2, 8, 16, 16, 128), BF16), v((1024, 256), BF16), v((512, 256), F32),
            v((8, 16, 16, 128), BF16), v((8, 16, 16, 128), BF16), v((16, 8, 16, 128), BF16),
            v((256, 128), F32), v((16, 16, 128), BF16), v((16, 16, 128), BF16),
            v((64, 384), BF16), v((64, 768), F32), v((64, 768), F32), v((384, 64), BF16),
            v((64, 128), F32), v((4, 48, 128), F32), v((64, 512), F32), v((512, 768), F32),
            v((512, 768), BF16), v((192, 768), BF16), v((64, 512), F32), v((512, 128), F32),
            v((2, 8, 32, 128), BF16), v((8, 2, 8, 32, 128), BF16), v((48, 512), BF16),
            v((16, 48, 512), BF16), v((64, 512), F32), v((256, 128), F32), v((8, 256, 128), F32),
            v((8, 256, 128), F32),
            v((4, 16, 48, 128), BF16), v((4, 16, 48, 128), BF16), v((4, 2, 4, 4, 32, 128), BF16),
            v((4, 4, 4, 32, 128), BF16), v((4, 4, 4, 32, 128), BF16), v((4, 4, 4, 32, 128), BF16),
            v((4, 64, 128), BF16), v((128, 128), BF16), v((256, 128), F32), v((16, 16, 128), BF16),
            v((2, 16, 16, 128), BF16),
            v((64, 768), F32), v((64, 768), F32), v((64, 128), F32), v((8, 8, 384), F32),
            v((16, 8, 384), F32), v((2, 8, 384), F32), v((8, 384), F32), v((8, 8, 384), F32),
            dma((3, 16)), dma((3, 16)), dma((2, 8)), dma((2, 8)), dma((2, 8)), dma((2, 8)),
            dma((2, 8)), dma((16,)), dma((16,)), dma((16,)), dma((4,)), dma((4,)),
            dma((4,)), dma((4,)), dma((16,)), dma((16,)),
            dma((4, 16)), dma((4, 16)), dma((4,)), dma((4,)), dma((4, 4)), dma((4, 4)),
            dma((2, 16)), dma((2, 16)), dma((8,)), dma((16,)), dma((1,)), dma((1,)),
            dma((16,)), dma((8,)), dma((30,)), dma((4,)), pltpu.SemaphoreType.REGULAR,
        ],
        compiler_params=pltpu.CompilerParams(
            collective_id=1, has_side_effects=True, vmem_limit_bytes=60 * 1024 * 1024
        ),
        name="step",
    )(
        residue_index, chain_index, token_mask, pair_in, relpos_weight, tri_proj, tri_out,
        bias_proj.T, single, ada_proj, noisy.reshape(512, 768), qkv_proj.transpose(1, 2, 0),
        out_proj, cotangent.transpose(0, 2, 1),
    )
    pair_out, block_t, grad_pair, grad_single = finished(
        (pair_out, block_t, grad_pair, grad_single)
    )
    return (
        pair_out,
        block_t.transpose(0, 2, 1),
        grad_pair.reshape(64, 32, 128),
        grad_single.reshape(64, 384),
    )


def solution(mesh):
    return jax.shard_map(
        on_device,
        mesh=mesh,
        in_specs=(
            P("row", "col", None), P(), P(), P(), P(), P(), P(), P(), P("row", None), P(),
            P("samp", "row", None), P(None, None, "col"), P("col", None), P("samp", "row", "col"),
        ),
        out_specs=(
            P("row", "col", None), P("samp", "row", "col"), P("row", "col", None), P("row", None),
        ),
        check_vma=False,
    )
```

```python
import jax
import jax.numpy as jnp
from jax import lax
from jax.experimental import pallas as pl
from jax.experimental.pallas import tpu as pltpu
from jax.sharding import PartitionSpec as P

HEAD_DIM = 48
REL_BINS = 66
EPSILON = 1e-05
MESH = pl.DeviceIdType.MESH
F32 = jnp.float32
BF16 = jnp.bfloat16
NCOL = 16
NROW = 8


def dg(a, b, ca, cb, **kw):
    return lax.dot_general(a, b, (((ca,), (cb,)), ((), ())), preferred_element_type=F32, **kw)


def place():
    return lax.axis_index("row"), lax.axis_index("col"), lax.axis_index("samp")


def rmod(a, n):
    return lax.rem(a, n)


def ring_shift(oz, from_core):
    if oz == 2:
        return 2 + 4 * from_core
    return (0, 1, None, 7)[oz]


def row_dest(oz, cx):
    row, col, samp = place()
    z, core = samp * 4 + row // 2, rmod(row, 2)
    to_core = rmod(core + cx, 2)
    to_z = rmod(z + ring_shift(oz, core), 8)
    return rmod(to_z, 4) * 2 + to_core, col, to_z // 4


def row_source(oz, cx):
    row, col, samp = place()
    z, core = samp * 4 + row // 2, rmod(row, 2)
    from_core = rmod(core + cx, 2)
    from_z = rmod(z + 8 - ring_shift(oz, from_core), 8)
    return rmod(from_z, 4) * 2 + from_core, col, from_z // 4


def spot(row):
    return rmod(row, 2) * 4 + row // 2


ROW_IDS = [(oz, cx) for oz in range(4) for cx in range(2) if (oz, cx) != (0, 0)]


def remote(src, dst, ssem, rsem, to):
    return pltpu.make_async_remote_copy(
        src_ref=src, dst_ref=dst, send_sem=ssem, recv_sem=rsem, device_id=to, device_id_type=MESH
    )


def col_start(src_of, slot_of, ssem, rsem):
    row, col, samp = place()

    def one(o, _):
        to = rmod(col + o, NCOL)
        remote(src_of(to), slot_of(col), ssem, rsem, (row, to, samp)).start()
        return 0

    lax.fori_loop(1, NCOL, one, 0)


def take(region, *sems):
    for sem in sems:
        pltpu.make_async_copy(region, region, sem).wait()


def row_start(src_of, slot_of, ssem, rsem):
    row = lax.axis_index("row")
    for oz, cx in ROW_IDS:
        to = row_dest(oz, cx)
        remote(src_of(to[0]), slot_of(row), ssem, rsem, to).start()


def signal(sem, to):
    pl.semaphore_signal(sem, inc=1, device_id=to, device_id_type=MESH)


def both(x, low, first):
    turned = pltpu.roll(x, 64, 1)
    return jnp.where(low, x, turned) if first else jnp.where(low, turned, x)


def sigmoid(x):
    return 0.5 * jnp.tanh(0.5 * x) + 0.5


def layer_norm(x, axis):
    mean = jnp.mean(x, axis, keepdims=True)
    cent = x - mean
    var = jnp.mean(cent * cent, axis, keepdims=True)
    return cent * lax.rsqrt(var + EPSILON)


def two_parts(x):
    coarse = x.astype(BF16)
    return jnp.concatenate([coarse, (x - coarse.astype(F32)).astype(BF16)], 0)


def step_kernel(
    res_ref, chain_ref, mask_ref,
    pair_hbm, relpos_hbm, tri_hbm, triout_hbm, biasp_hbm, single_hbm, ada_hbm, noisy_hbm,
    qkvw_hbm, outp_hbm, cot_hbm,
    pairout_hbm, block_hbm, gpair_hbm, gsingle_hbm,
    pairout_ref, block_ref, gpair_ref,
    pair_in, tri_w, ada_w, noisy, relpos_ref, triout_ref, biasp_ref, single_ref, qkvw_ref, outp_ref,
    cot_ref, idx_r, mrow, relpos_w,
    zl_s, tri_t, pf, gate, lrf, lbuf, recv_a, got, rcat, lcat, mtmp, tbuf, got_c, got_d, bias_f, bias_b, bias_got,
    cvec_s, scale_s, shift_s, wg_s, gate_t, g_t, noisy_t, normed, hidden, wqkv, q_t, kv_f,
    kv_own, kv_all, dmx_own, dmx_all, da_t, keyok, sraw, draw,
    mix_s, mix_r, dkv_s, dkv_m, dkv_o, dkv_r, dq_t, dkv_tok, dbias, db_s, db_r,
    dsc, dsh, dga, dc_s, dc_r, dc_p, gs_own, gs_all,
    sa, ra, sb, rb, sc, rc, sd, rd, se, re, skv, rkv, skf, rkf, sdm, rdm,
    sm, rm, sk, rk, sko, rko, sbb, rbb, st, rt, sp, rp_, sg, rg, loc, locm, ready,
):
    row, col, samp = place()
    core = rmod(row, 2)
    zlo = row // 2
    mate = (row + 1 - 2 * core, col, samp)
    far = (row, col, 1 - samp)
    barrier = pltpu.get_barrier_semaphore()

    loads = [
        pltpu.make_async_copy(s, d, loc.at[18 + i])
        for i, (s, d) in enumerate(
            [
                (pair_hbm, pair_in), (relpos_hbm, relpos_ref), (tri_hbm, tri_w),
                (single_hbm, single_ref), (qkvw_hbm, qkvw_ref), (ada_hbm, ada_w),
                (noisy_hbm, noisy), (cot_hbm, cot_ref), (triout_hbm, triout_ref),
                (biasp_hbm, biasp_ref), (outp_hbm, outp_ref),
            ]
        )
    ]
    for copy in loads:
        copy.start()
    for oz, cx in ROW_IDS:
        signal(barrier, row_source(oz, cx))

    def greet(o, _):
        signal(barrier, (row, rmod(col + o, NCOL), samp))
        return 0

    def greet_row(o, _):
        signal(barrier, (rmod(row + o, NROW), col, samp))
        return 0

    lax.fori_loop(1, NCOL, greet, 0)
    lax.fori_loop(1, NROW, greet_row, 0)
    signal(barrier, far)

    low = lax.broadcasted_iota(jnp.int32, (64, 128), 1) < 64
    low16 = lax.broadcasted_iota(jnp.int32, (16, 128), 1) < 64
    low1 = lax.broadcasted_iota(jnp.int32, (1, 128), 1) < 64
    diag = (lax.broadcasted_iota(jnp.int32, (128, 128), 0) < 64) == (
        lax.broadcasted_iota(jnp.int32, (128, 128), 1) < 64
    )

    def blockdiag(x):
        return jnp.where(diag, jnp.concatenate([x, x], 0), 0.0).astype(BF16)

    def indices(i, _):
        at = pl.ds(i, 1)
        idx_r[0, at, :] = jnp.full((1, 128), res_ref[row * 64 + i], jnp.int32)
        idx_r[1, at, :] = jnp.full((1, 128), chain_ref[row * 64 + i], jnp.int32)
        m = jnp.full((1, 128), mask_ref[row * 64 + i].astype(F32), F32)
        mrow[at, :] = m
        mrow[pl.ds(64 + i, 1), :] = m
        return 0

    lax.fori_loop(0, 64, indices, 0, unroll=4)
    mrow[...] = mrow[...].T
    relpos_w[...] = jnp.zeros_like(relpos_w)
    loads[1].wait()
    relpos_w[0:REL_BINS, :] = relpos_ref[...]
    loads[0].wait()

    def load(i, _):
        pf[pl.ds(i * 32, 32), :] = pair_in[i].astype(F32)
        return 0

    lax.fori_loop(0, 64, load, 0, unroll=4)
    bins = lax.broadcasted_iota(jnp.int32, (64, 128), 1)

    def normed_rows(t, _):
        parts = []
        for q in range(2):
            for hi in range(2):
                j = 2 * t + q + 16 * hi
                off = jnp.clip(idx_r[0] - res_ref[col * 32 + j] + 32, 0, 64)
                bucket = jnp.where(idx_r[1] == chain_ref[col * 32 + j], off, REL_BINS - 1)
                onehot = jnp.where(bucket == bins, 1.0, 0.0).astype(BF16)
                parts.append(
                    pf[pl.ds(j, 64, stride=32), :]
                    + jnp.dot(onehot, relpos_w[...], preferred_element_type=F32)
                )
        for q in range(2):
            for hi in range(2):
                pf[pl.ds(2 * t + q + 16 * hi, 64, stride=32), :] = parts[2 * q + hi]
        at = pl.ds(pl.multiple_of(t * 256, 256), 256)
        zl_s[at, :] = layer_norm(jnp.concatenate(parts, 0), -1).astype(BF16)
        return 0

    lax.fori_loop(0, 8, normed_rows, 0, unroll=2)
    loads[2].wait()
    tri_t[...] = tri_w[:, :512].astype(F32).T.astype(BF16)

    def project(h, t):
        at = pl.ds(pl.multiple_of(t * 256, 256), 256)
        pt = dg(tri_t[h * 256 : h * 256 + 256, :], zl_s[at, :], 1, 1)
        val = sigmoid(pt[128:]) * pt[:128]
        for q in range(2):
            lo = 2 * t + q
            mask = mrow[0:1, :] * jnp.where(
                low1, mask_ref[col * 32 + lo].astype(F32), mask_ref[col * 32 + 16 + lo].astype(F32)
            )
            lrf[pl.ds(h * 2048 + lo, 128, stride=16), :] = val[:, q * 128 : q * 128 + 128] * mask

    pieces = [(0, slice(0, 8)), (1, slice(0, 4)), (1, slice(4, 8))]
    a_src = [lambda to, h=h, p=p: lbuf.at[h, to, p] for h, p in pieces]
    a_slot = [lambda c, h=h, p=p: recv_a.at[h, c, p] for h, p in pieces]
    b_src = [lambda r, h=h: recv_a.at[h, :, spot(r)] for h in range(2)]
    b_slot = [lambda r, h=h: got.at[h, r] for h in range(2)]
    own_a = [pltpu.make_async_copy(lbuf.at[h, col], recv_a.at[h, col], loc.at[h]) for h in range(2)]
    own_b = [
        pltpu.make_async_copy(recv_a.at[h, :, spot(row)], got.at[h, row], loc.at[2 + h])
        for h in range(2)
    ]
    for h in range(2):

        def one_side(t, _):
            project(h, t)
            return 0

        lax.fori_loop(0, 8, one_side, 0, unroll=2)

        def pack(c, _):
            lbuf[h, c] = lrf[pl.ds(h * 2048 + c * 128, 128), :].astype(BF16).reshape(8, 16, 128)
            return 0

        lax.fori_loop(0, 16, pack, 0, unroll=2)
        if h == 0:
            pl.semaphore_wait(barrier, 7 + 15 + 7 + 1)
            signal(ready, far)
        own_a[h].start()
        for i in ((0,), (1, 2))[h]:
            col_start(a_src[i], a_slot[i], sa.at[i], ra.at[i])

    for copy in loads[3:6]:
        copy.wait()
    cvec = layer_norm(single_ref[...].astype(F32), -1).astype(BF16)
    cvec_s[...] = cvec
    wqkv[...] = jnp.zeros_like(wqkv)
    for p in range(3):
        wqkv[p * 64 : p * 64 + 48, :] = qkvw_ref[p]
    scale_s[...] = sigmoid(jnp.dot(cvec, ada_w[:, :768], preferred_element_type=F32))
    shift_s[...] = jnp.dot(cvec, ada_w[:, 768:1536], preferred_element_type=F32)
    for copy in loads[6:]:
        copy.wait()

    def sample(s, _):
        at = pl.ds(pl.multiple_of(s * 64, 64), 64)
        n = layer_norm(noisy[at, :].astype(F32), -1)
        normed[at, :] = n
        hidden[at, :] = (scale_s[...] * n + shift_s[...]).astype(BF16)
        return 0

    lax.fori_loop(0, 8, sample, 0)
    own_a[0].wait()
    take(recv_a.at[0, 0:15], sa.at[0], ra.at[0])
    own_b[0].start()
    row_start(b_src[0], b_slot[0], sb.at[0], rb.at[0])

    feat = lax.broadcasted_iota(jnp.int32, (768, 64), 1)
    sel = jnp.where(
        (lax.broadcasted_iota(jnp.int32, (768, 64), 0) == col * 48 + feat) & (feat < 48), 1.0, 0.0
    ).astype(BF16)
    wg_s[...] = jnp.dot(ada_w[:, 1536:], sel, preferred_element_type=F32).astype(BF16)
    gate_t[...] = sigmoid(
        dg(wg_s[...], jnp.concatenate([cvec_s[...], cvec_s[...]], 0), 0, 1)
    )
    lane = lax.broadcasted_iota(jnp.int32, (64, 128), 1)
    tok = lax.broadcasted_iota(jnp.int32, (64, 128), 0)
    put = [jnp.where(lane == tok + 64 * h, 1.0, 0.0).astype(BF16) for h in range(2)]
    for u in range(4):
        g = jnp.dot(cot_ref[2 * u], put[0], preferred_element_type=F32) + jnp.dot(
            cot_ref[2 * u + 1], put[1], preferred_element_type=F32
        )
        g_t[u] = g
        dmx_own[:, u * 128 : u * 128 + 128] = (g * gate_t[:48, :]).astype(BF16)
    dm_src, dm_slot = (lambda to: dmx_own), (lambda c: dmx_all.at[c])
    dm_keep = pltpu.make_async_copy(dmx_own, dmx_all.at[col], loc.at[5])
    dm_keep.start()
    col_start(dm_src, dm_slot, sdm.at[0], rdm.at[0])
    kv_f[...] = dg(hidden[...], wqkv[64:, :], 1, 1)

    def kv_pack(t, _):
        r0 = kv_f[pl.ds(t * 32, 16), :]
        r1 = kv_f[pl.ds(t * 32 + 16, 16), :]
        to = pl.ds(pl.multiple_of(rmod(t, 2) * 16, 16), 16)
        kv_own[0, t // 2, to, :] = jnp.where(low16, r0, pltpu.roll(r1, 64, 1)).astype(BF16)
        kv_own[1, t // 2, to, :] = jnp.where(low16, pltpu.roll(r0, 64, 1), r1).astype(BF16)
        return 0

    lax.fori_loop(0, 16, kv_pack, 0, unroll=2)
    kv_keep = pltpu.make_async_copy(kv_own, kv_all.at[row], loc.at[4])
    kv_keep.start()
    kv_out = []
    for o in range(1, 4):
        to = (rmod(zlo + o, 4) * 2 + core, col, samp)
        kv_out.append(remote(kv_own, kv_all.at[row], skv.at[o], rkv.at[o], to))
    kv_mate = remote(kv_own, kv_all.at[row], skf.at[0], rkf.at[0], mate)
    own_a[1].wait()
    for k in range(2):
        take(recv_a.at[1, 0:15, 0:4], sa.at[1 + k], ra.at[1 + k])
        cx = rmod(core + k, 2)
        for oz in (2, 1, 3):
            to = row_dest(oz, cx)
            remote(b_src[1](to[0]), b_slot[1](row), sb.at[1], rb.at[1], to).start()

        @pl.when(cx == 1)
        def _():
            remote(b_src[1](mate[0]), b_slot[1](row), sb.at[1], rb.at[1], mate).start()

    own_b[1].start()

    def gates(t, _):
        at = pl.ds(pl.multiple_of(t * 256, 256), 256)
        gate[at, :] = sigmoid(
            jnp.dot(zl_s[at, :], tri_w[:, 512:], preferred_element_type=F32)
        )
        return 0

    lax.fori_loop(0, 8, gates, 0)
    for h in (1, 0):
        own_b[h].wait()
        take(got.at[h, 0:7], sb.at[h], rb.at[h])

    def turn(r, _):
        x = got[1, r].reshape(256, 128).astype(F32).T.astype(BF16)
        at = pl.ds(pl.multiple_of(r * 64, 64), 64)
        rcat[at, 0:256] = x[:64]
        rcat[at, 256:512] = x[64:]
        return 0

    lax.fori_loop(0, 8, turn, 0, unroll=2)
    low256 = lax.broadcasted_iota(jnp.int32, (256, 128), 1) < 64
    turns = ((2, 1), (3, 0))
    for i, pair in enumerate(turns):
        for k, oz in enumerate(pair):
            z = rmod(zlo + oz, 4)
            la = got[0, 2 * z].reshape(256, 128).astype(F32)
            lb = got[0, 2 * z + 1].reshape(256, 128).astype(F32)
            lanes = slice(k * 128, k * 128 + 128)
            lcat[i, 0:256, lanes] = jnp.where(low256, la, pltpu.roll(lb, 64, 1)).astype(BF16)
            lcat[i, 256:512, lanes] = jnp.where(low256, pltpu.roll(la, 64, 1), lb).astype(BF16)
    c_src = [lambda r, p=p: tbuf.at[r, p] for p in (slice(0, 8), slice(8, 16))]
    c_slot = [lambda r, p=p: got_c.at[spot(r), p] for p in (slice(0, 8), slice(8, 16))]
    own_c = [
        pltpu.make_async_copy(c_src[h](row), c_slot[h](row), loc.at[6 + 3 * h]) for h in range(2)
    ]

    def tri(i, part):
        mtmp[...] = jnp.dot(
            rcat[part * 256 : part * 256 + 256, :], lcat[i], preferred_element_type=F32
        )

        def out(rj, _):
            for k, oz in enumerate(turns[i]):
                z = rmod(zlo + oz, 4)
                for jh in range(2):
                    at = rj * 64 + jh * 32
                    a = mtmp[pl.ds(at, 16), k * 128 : k * 128 + 128]
                    b = mtmp[pl.ds(at + 16, 16), k * 128 : k * 128 + 128]
                    even_row = jnp.where(low16, a, pltpu.roll(b, 64, 1))
                    odd_row = jnp.where(low16, pltpu.roll(a, 64, 1), b)
                    tbuf[2 * z, part * 8 + 2 * rj + jh] = even_row.astype(BF16)
                    tbuf[2 * z + 1, part * 8 + 2 * rj + jh] = odd_row.astype(BF16)
            return 0

        lax.fori_loop(0, 4, out, 0, unroll=2)

    for part in range(2):
        for i, pair in enumerate(turns):
            tri(i, part)
            for oz in pair:
                for cx in range(2):
                    if (oz, cx) != (0, 0):
                        to = row_dest(oz, cx)
                        remote(
                            c_src[part](to[0]), c_slot[part](row), sc.at[part], rc.at[part], to
                        ).start()
        own_c[part].start()
    kv_mate.start()
    for copy in kv_out:
        copy.start()
    d_own = pltpu.make_async_copy(got_c.at[:, col], got_d.at[col], loc.at[7])

    def d_start(part):
        def one(o, _):
            to = part * 8 + rmod(col + o, 8)

            @pl.when(to != col)
            def _():
                remote(got_c.at[:, to], got_d.at[col], sd.at[0], rd.at[0], (row, to, samp)).start()

            return 0

        lax.fori_loop(0, 8, one, 0)

    dm_keep.wait()
    take(dmx_all.at[0:15], sdm.at[0], rdm.at[0])
    da_t[...] = jnp.zeros_like(da_t)
    da_t[:48, :] = (
        jnp.dot(outp_ref[...], dmx_all[...].reshape(768, 512), preferred_element_type=F32)
        .astype(BF16)
        .astype(F32)
    )
    for part in range(2):
        own_c[part].wait()
        take(got_c.at[0:7, 0:8], sc.at[part], rc.at[part])
        d_start(part)
    d_own.start()

    q_t[...] = dg(wqkv[:64, :], hidden[...], 1, 1)
    noisy_t[...] = dg(sel, noisy[...], 0, 1)

    def key_mask(t, _):
        jb, lo = t // 16, rmod(t, 16)
        keyok[pl.ds(t, 1), :] = jnp.where(
            low1,
            mask_ref[jb * 32 + lo].astype(F32),
            mask_ref[jb * 32 + 16 + lo].astype(F32),
        )
        return 0

    lax.fori_loop(0, 256, key_mask, 0, unroll=4)

    for o in range(1, 4):
        came = rmod(zlo + 4 - o, 4) * 2 + core
        remote(kv_own, kv_all.at[came], skv.at[o], rkv.at[o], mate).wait_recv()
        remote(kv_all.at[came], kv_all.at[came], skf.at[o], rkf.at[o], mate).start()


    def half_of(ref, u, sh):
        tile = ref[:, pl.ds(pl.multiple_of(u * 128, 128), 128)].astype(F32)
        return blockdiag(both(tile, low, sh == 0))

    def keys(which, s):
        return jnp.concatenate([kv_all[r, which, s] for r in range(NROW)], 0)

    def raw(u, _):
        for sh in range(2):
            s = 2 * u + sh
            sraw[s] = jnp.dot(keys(0, s), half_of(q_t, u, sh), preferred_element_type=F32)
            draw[s] = jnp.dot(keys(1, s), half_of(da_t, u, sh), preferred_element_type=F32)
        return 0

    d_own.wait()
    take(got_d.at[0:15], sd.at[0], rd.at[0])

    def widen(c, _):
        lrf[pl.ds(c * 128, 128), :] = got_d[c].reshape(128, 128).astype(F32)
        return 0

    lax.fori_loop(0, 16, widen, 0)

    def stage3(t, _):
        tn = layer_norm(
            jnp.concatenate([lrf[pl.ds(2 * t + q, 128, stride=16), :] for q in range(2)], 1), 0
        ).astype(BF16)
        upd = dg(tn, triout_ref[...], 0, 0) * gate[pl.ds(pl.multiple_of(t * 256, 256), 256), :]
        spots = [pl.ds(2 * t + q + 16 * hi, 64, stride=32) for q in range(2) for hi in range(2)]
        outs = [
            (pf[at, :] + upd[i * 64 : i * 64 + 64]).astype(BF16) for i, at in enumerate(spots)
        ]
        for at, val in zip(spots, outs):
            pf[at, :] = val.astype(F32)
        tile = dg(biasp_ref[...], jnp.concatenate(outs, 0), 1, 1)
        for q in range(2):
            bias_f[pl.ds(2 * t + q, 16, stride=16), :] = tile[:, q * 128 : q * 128 + 128]
        return 0

    lax.fori_loop(0, 8, stage3, 0, unroll=4)
    bias_b[...] = bias_f[...].astype(BF16).reshape(16, 16, 128)
    e_src, e_slot = (lambda c: bias_b.at[c]), (lambda c: bias_got.at[c])
    own_e = pltpu.make_async_copy(bias_b.at[col], bias_got.at[col], loc.at[8])
    own_e.start()
    col_start(e_src, e_slot, se.at[0], re.at[0])

    kv_keep.wait()
    for copy in kv_out:
        copy.wait_send()
    kv_mate.wait_send()
    for o in range(4):
        came = rmod(zlo + 4 - o, 4) * 2
        remote(
            kv_all.at[came + core], kv_all.at[came + 1 - core], skf.at[o], rkf.at[o], mate
        ).wait_recv()
        if o > 0:
            remote(
                kv_all.at[came + core], kv_all.at[came + core], skf.at[o], rkf.at[o], mate
            ).wait_send()
    lax.fori_loop(0, 4, raw, 0)
    def store(i, _):
        pairout_ref[i] = pf[pl.ds(i * 32, 32), :].astype(BF16)
        return 0

    lax.fori_loop(0, 64, store, 0, unroll=4)
    out_pair = pltpu.make_async_copy(pairout_ref, pairout_hbm, loc.at[14])
    out_pair.start()
    dbias[...] = jnp.zeros_like(dbias)
    own_e.wait()
    take(bias_got.at[0:15], se.at[0], re.at[0])

    scale = 1.0 / HEAD_DIM**0.5

    def mix_src(u):
        return lambda f: mix_s.at[u, f]

    def mix_slot(u):
        return lambda h: mix_r.at[u, h]

    def to_mate(u):
        return remote(dkv_s.at[:, 1 - core, u], dkv_m.at[u], sk.at[u], rk.at[u], mate)

    def to_chip(u, o):
        z = rmod(zlo + o, 4)
        return remote(
            dkv_o.at[u, z], dkv_r.at[u, zlo], sko.at[u, o], rko.at[u, o], (z * 2 + core, col, samp)
        )

    def pass_on(u):
        to_mate(u).wait_recv()
        for z in range(4):
            dkv_o[u, z] = (
                dkv_s[z, core, u].astype(F32) + dkv_m[u, z].astype(F32)
            ).astype(BF16)
        for o in range(1, 4):
            to_chip(u, o).start()

    def pair_of_samples(u, _):
        folded, dqs = [], []
        for sh in range(2):
            s = 2 * u + sh
            kp, vp = keys(0, s), keys(1, s)
            qq, dd = half_of(q_t, u, sh), half_of(da_t, u, sh)
            sco = sraw[s] * scale + bias_got[...].reshape(256, 128).astype(F32)
            sco = jnp.where(keyok[...] > 0, sco, -1000000000.0)
            top = jnp.max(sco, 0, keepdims=True)
            top = jnp.maximum(top, pltpu.roll(top, 64, 1))
            ex = jnp.exp(sco - top)
            tot = jnp.sum(ex, 0, keepdims=True)
            probs = ex * (1.0 / (tot + pltpu.roll(tot, 64, 1)))
            pb = probs.astype(BF16)
            folded.append(dg(vp, pb, 0, 0))
            dp = draw[s]
            dot = jnp.sum(probs * dp, 0, keepdims=True)
            ds = probs * (dp - (dot + pltpu.roll(dot, 64, 1)))
            dbias[...] += ds
            dsb = (ds * scale).astype(BF16)
            dqs.append(dg(kp, dsb, 0, 0))
            dk = dg(dsb, qq, 1, 1).astype(BF16)
            dv = dg(pb, dd, 1, 1).astype(BF16)
            for r in range(NROW):
                dkv_s[r // 2, r % 2, u, sh] = dk[r * 32 : r * 32 + 32]
                dkv_s[r // 2, r % 2, u, 2 + sh] = dv[r * 32 : r * 32 + 32]

        def fold(m0, m1):
            return jnp.where(
                low,
                m0[:64] + pltpu.roll(m0[64:], 64, 1),
                pltpu.roll(m1[:64], 64, 1) + m1[64:],
            ).astype(BF16)

        att = fold(*folded)
        dq_t[u] = fold(*dqs)
        mix_s[u] = dg(outp_ref[...], att[:48], 0, 0).astype(BF16).reshape(16, 48, 128)
        pltpu.make_async_copy(mix_s.at[u, col], mix_r.at[u, col], locm.at[u]).start()
        to_mate(u).start()
        col_start(mix_src(u), mix_slot(u), sm.at[u], rm.at[u])

        @pl.when(u > 0)
        def _():
            pass_on(u - 1)

        return 0

    lax.fori_loop(0, 4, pair_of_samples, 0)

    db_s[...] = dbias[...].astype(BF16).reshape(16, 16, 128)
    own_db = pltpu.make_async_copy(db_s.at[col], db_r.at[samp, col], loc.at[29])
    own_db.start()

    def db_copy(o):
        to = rmod(col + o, NCOL)
        return remote(
            db_s.at[to], db_r.at[samp, col], sbb.at[1], rbb.at[1], (row, to, 1 - samp)
        )

    def db_send(o, _):
        db_copy(o).start()
        return 0

    pass_on(3)
    pl.semaphore_wait(ready, 1)
    lax.fori_loop(0, NCOL, db_send, 0)
    near_src, near_slot = (lambda c: db_s.at[c]), (lambda c: db_r.at[samp, c])
    col_start(near_src, near_slot, sbb.at[0], rbb.at[0])

    dga[...] = jnp.zeros_like(dga)

    def mixed_of(u, _):
        pltpu.make_async_copy(mix_s.at[u, col], mix_r.at[u, col], locm.at[u]).wait()
        take(mix_r.at[u, 0:15], sm.at[u], rm.at[u])
        total = mix_r[u, 0].astype(F32)
        for h in range(1, NCOL):
            total = total + mix_r[u, h].astype(F32)
        lanes = pl.ds(pl.multiple_of(u * 128, 128), 128)
        out = noisy_t[:48, lanes] + gate_t[:48, :] * total
        block_ref[2 * u] = out[:, :64].astype(BF16)
        block_ref[2 * u + 1] = pltpu.roll(out, 64, 1)[:, :64].astype(BF16)
        dga[:48, :] += g_t[u] * total
        return 0

    lax.fori_loop(0, 3, mixed_of, 0)

    dsc[...] = jnp.zeros_like(dsc)
    dsh[...] = jnp.zeros_like(dsh)

    def hidden_grad(u, _):
        to_mate(u).wait_send()
        for o in range(1, 4):
            came = rmod(zlo + 4 - o, 4)
            remote(
                dkv_o.at[u, came], dkv_r.at[u, came], sko.at[u, o], rko.at[u, o], mate
            ).wait_recv()
            to_chip(u, o).wait_send()
        dkv_r[u, zlo] = dkv_o[u, zlo]
        tot = dkv_r[u, 0].astype(F32)
        for z in range(1, 4):
            tot = tot + dkv_r[u, z].astype(F32)
        for sh in range(2):
            for jb in range(2):
                a = tot[sh, jb * 16 : jb * 16 + 16]
                b = tot[2 + sh, jb * 16 : jb * 16 + 16]
                base = sh * 64 + jb * 32
                dkv_tok[base : base + 16, :] = jnp.where(low16, a, pltpu.roll(b, 64, 1)).astype(BF16)
                dkv_tok[base + 16 : base + 32, :] = jnp.where(
                    low16, pltpu.roll(a, 64, 1), b
                ).astype(BF16)
        dh = dg(dq_t[u], wqkv[:64, :], 0, 0) + jnp.dot(
            dkv_tok[...], wqkv[64:, :], preferred_element_type=F32
        )
        n = normed[pl.ds(pl.multiple_of(u * 128, 128), 128), :]
        w = dh * n
        dsc[...] += w[:64] + w[64:]
        dsh[...] += dh[:64] + dh[64:]
        return 0

    lax.fori_loop(0, 3, hidden_grad, 0)
    mixed_of(3, 0)
    out_block = pltpu.make_async_copy(block_ref, block_hbm, loc.at[15])
    out_block.start()
    hidden_grad(3, 0)
    sg_ = scale_s[...]
    part = dg(two_parts(dsc[...] * sg_ * (1.0 - sg_)), ada_w[:, :768], 1, 1)
    part = part + dg(two_parts(dsh[...]), ada_w[:, 768:1536], 1, 1)
    part = part[:64] + part[64:]
    acc = dga[...]
    acc = (acc + pltpu.roll(acc, 64, 1)) * gate_t[...] * (1.0 - gate_t[...])
    coarse = acc.astype(BF16)
    fine = (acc - coarse.astype(F32)).astype(BF16)
    part = part + (dg(coarse, wg_s[...], 0, 1) + dg(fine, wg_s[...], 0, 1))[:64]
    dc_s[...] = part.reshape(8, 8, 384)

    half_col = col // 2
    even = rmod(col, 2) == 0

    def part_copy(o):
        g = rmod(half_col + o, 8)
        return remote(dc_s.at[g], dc_r.at[col], st.at[0], rt.at[0], (row, 2 * g, samp))

    @pl.when(jnp.logical_not(even))
    def _():
        part_copy(0).start()

    def part_send(o, _):
        part_copy(o).start()
        return 0

    lax.fori_loop(1, 8, part_send, 0)

    own_db.wait()
    take(db_r.at[0, 0:15], sbb.at[0], rbb.at[0])
    take(db_r.at[0], sbb.at[1], rbb.at[1])
    dbias[...] = (db_r[0].astype(F32) + db_r[1].astype(F32)).reshape(256, 128)
    biasp3 = jnp.concatenate([biasp_ref[...]] * 3, 0)

    def grad(lo, _):
        d = dbias[pl.ds(lo, 16, stride=16), :]
        d1 = d.astype(BF16)
        rest = d - d1.astype(F32)
        d2 = rest.astype(BF16)
        d3 = (rest - d2.astype(F32)).astype(BF16)
        g = dg(jnp.concatenate([d1, d2, d3], 0), biasp3, 0, 0)
        for hi in range(2):
            gpair_ref[pl.ds(lo + 16 * hi, 64, stride=32), :] = g[hi * 64 : hi * 64 + 64]
        return 0

    lax.fori_loop(0, 16, grad, 0, unroll=2)
    out_grad = pltpu.make_async_copy(gpair_ref, gpair_hbm, loc.at[16])
    out_grad.start()

    def own_copy(o):
        return remote(
            gs_own, gs_all.at[half_col], sg.at[0], rg.at[0], (row, rmod(col + o, NCOL), samp)
        )

    @pl.when(even)
    def _():
        dc_r[col] = dc_s[half_col]

        take(dc_r.at[0:15], rt.at[0])
        tot = dc_r[0]
        for c in range(1, NCOL):
            tot = tot + dc_r[c]
        dc_p[samp] = tot
        other = remote(dc_p.at[samp], dc_p.at[samp], sp.at[0], rp_.at[0], far)
        other.start()
        own = single_ref[...].astype(F32).reshape(8, 8, 384)
        mine = jnp.zeros((8, 384), F32)
        for g in range(8):
            mine = mine + jnp.where(half_col == g, own[g], 0.0)
        mean = jnp.mean(mine, -1, keepdims=True)
        cent = mine - mean
        inv = lax.rsqrt(jnp.mean(cent * cent, -1, keepdims=True) + EPSILON)
        unit = cent * inv
        remote(dc_p.at[samp], dc_p.at[1 - samp], sp.at[0], rp_.at[0], far).wait_recv()
        other.wait_send()
        up = dc_p[0] + dc_p[1]
        gs_own[...] = inv * (
            up - jnp.mean(up, -1, keepdims=True) - unit * jnp.mean(up * unit, -1, keepdims=True)
        )

        def tell(o, _):
            own_copy(o).start()
            return 0

        lax.fori_loop(1, NCOL, tell, 0)
        gs_all[half_col] = gs_own[...]

    @pl.when(even)
    def _():
        take(dc_s.at[0:7], st.at[0])
        take(dc_r.at[0:15], sg.at[0])
        take(gs_all.at[0:7], rg.at[0])

    @pl.when(jnp.logical_not(even))
    def _():
        take(dc_s, st.at[0])
        take(gs_all, rg.at[0])

    out_single = pltpu.make_async_copy(gs_all, gsingle_hbm, loc.at[17])
    out_single.start()
    for copy in (out_pair, out_block, out_grad, out_single):
        copy.wait()


def finish_kernel(*refs):
    n = 4
    ins, outs, bufs = refs[:n], refs[n : 2 * n], refs[2 * n : 3 * n]
    got, put = refs[3 * n], refs[3 * n + 1]
    reads = [pltpu.make_async_copy(ins[i], bufs[i], got.at[i]) for i in range(n)]
    writes = [pltpu.make_async_copy(bufs[i], outs[i], put.at[i]) for i in range(n)]
    for copy in reads:
        copy.start()
    for i in (3, 1, 0, 2):
        reads[i].wait()
        writes[i].start()
    for copy in writes:
        copy.wait()


def finished(arrays):
    hbm = pl.BlockSpec(memory_space=pl.ANY)
    return pl.pallas_call(
        finish_kernel,
        out_shape=[jax.ShapeDtypeStruct(x.shape, x.dtype) for x in arrays],
        in_specs=[hbm] * 4,
        out_specs=[hbm] * 4,
        scratch_shapes=[pltpu.VMEM(x.shape, x.dtype) for x in arrays]
        + [pltpu.SemaphoreType.DMA((4,)), pltpu.SemaphoreType.DMA((4,))],
        compiler_params=pltpu.CompilerParams(vmem_limit_bytes=60 * 1024 * 1024),
        name="finish",
    )(*arrays)


def on_device(
    pair_in, residue_index, chain_index, token_mask, relpos_weight, tri_proj, tri_out, bias_proj,
    single, ada_proj, noisy, qkv_proj, out_proj, cotangent,
):
    sm = pl.BlockSpec(memory_space=pltpu.SMEM)
    hbm = pl.BlockSpec(memory_space=pl.ANY)
    dma = pltpu.SemaphoreType.DMA
    v = pltpu.VMEM
    pair_out, block_t, grad_pair, grad_single = pl.pallas_call(
        step_kernel,
        out_shape=(
            jax.ShapeDtypeStruct((64, 32, 128), BF16),
            jax.ShapeDtypeStruct((8, 48, 64), BF16),
            jax.ShapeDtypeStruct((2048, 128), F32),
            jax.ShapeDtypeStruct((8, 8, 384), F32),
        ),
        in_specs=[sm] * 3 + [hbm] * 11,
        out_specs=(hbm,) * 4,
        scratch_shapes=[
            v((64, 32, 128), BF16), v((8, 48, 64), BF16), v((2048, 128), F32),
            v((64, 32, 128), BF16), v((128, 640), BF16), v((384, 2304), BF16), v((512, 768), BF16),
            v((REL_BINS, 128), BF16), v((128, 128), BF16), v((16, 128), BF16), v((64, 384), BF16),
            v((3, 48, 768), BF16), v((48, 768), BF16), v((8, 48, 64), BF16),
            v((2, 64, 128), jnp.int32), v((128, 128), F32), v((128, 128), BF16),
            v((2048, 128), BF16), v((512, 128), BF16), v((2048, 128), F32), v((2048, 128), F32),
            v((4096, 128), F32),
            v((2, 16, 8, 16, 128), BF16), v((2, 16, 8, 16, 128), BF16),
            v((2, 8, 16, 16, 128), BF16), v((512, 512), BF16), v((2, 512, 256), BF16),
            v((256, 256), F32),
            v((8, 16, 16, 128), BF16), v((8, 16, 16, 128), BF16), v((16, 8, 16, 128), BF16),
            v((256, 128), F32), v((16, 16, 128), BF16), v((16, 16, 128), BF16),
            v((64, 384), BF16), v((64, 768), F32), v((64, 768), F32), v((384, 64), BF16),
            v((64, 128), F32), v((4, 48, 128), F32), v((64, 512), F32), v((512, 768), F32),
            v((512, 768), BF16), v((192, 768), BF16), v((64, 512), F32), v((512, 128), F32),
            v((2, 8, 32, 128), BF16), v((8, 2, 8, 32, 128), BF16), v((48, 512), BF16),
            v((16, 48, 512), BF16), v((64, 512), F32), v((256, 128), F32), v((8, 256, 128), F32),
            v((8, 256, 128), F32),
            v((4, 16, 48, 128), BF16), v((4, 16, 48, 128), BF16), v((4, 2, 4, 4, 32, 128), BF16),
            v((4, 4, 4, 32, 128), BF16), v((4, 4, 4, 32, 128), BF16), v((4, 4, 4, 32, 128), BF16),
            v((4, 64, 128), BF16), v((128, 128), BF16), v((256, 128), F32), v((16, 16, 128), BF16),
            v((2, 16, 16, 128), BF16),
            v((64, 768), F32), v((64, 768), F32), v((64, 128), F32), v((8, 8, 384), F32),
            v((16, 8, 384), F32), v((2, 8, 384), F32), v((8, 384), F32), v((8, 8, 384), F32),
            dma((3,)), dma((3,)), dma((2,)), dma((2,)), dma((2,)), dma((2,)),
            dma((1,)), dma((1,)), dma((1,)), dma((1,)), dma((4,)), dma((4,)),
            dma((4,)), dma((4,)), dma((1,)), dma((1,)),
            dma((4,)), dma((4,)), dma((4,)), dma((4,)), dma((4, 4)), dma((4, 4)),
            dma((2,)), dma((2,)), dma((1,)), dma((1,)), dma((1,)), dma((1,)),
            dma((1,)), dma((1,)), dma((30,)), dma((4,)), pltpu.SemaphoreType.REGULAR,
        ],
        compiler_params=pltpu.CompilerParams(
            collective_id=1, has_side_effects=True, vmem_limit_bytes=60 * 1024 * 1024
        ),
        name="step",
    )(
        residue_index, chain_index, token_mask, pair_in, relpos_weight, tri_proj, tri_out,
        bias_proj.T, single, ada_proj, noisy.reshape(512, 768), qkv_proj.transpose(1, 2, 0),
        out_proj, cotangent.transpose(0, 2, 1),
    )
    pair_out, block_t, grad_pair, grad_single = finished(
        (pair_out, block_t, grad_pair, grad_single)
    )
    return (
        pair_out,
        block_t.transpose(0, 2, 1),
        grad_pair.reshape(64, 32, 128),
        grad_single.reshape(64, 384),
    )


def solution(mesh):
    return jax.shard_map(
        on_device,
        mesh=mesh,
        in_specs=(
            P("row", "col", None), P(), P(), P(), P(), P(), P(), P(), P("row", None), P(),
            P("samp", "row", None), P(None, None, "col"), P("col", None), P("samp", "row", "col"),
        ),
        out_specs=(
            P("row", "col", None), P("samp", "row", "col"), P("row", "col", None), P("row", None),
        ),
        check_vma=False,
    )
```

```python
import jax
import jax.numpy as jnp
from jax import lax
from jax.experimental import pallas as pl
from jax.experimental.pallas import tpu as pltpu
from jax.sharding import PartitionSpec as P

HEAD_DIM = 48
REL_BINS = 66
EPSILON = 1e-05
MESH = pl.DeviceIdType.MESH
F32 = jnp.float32
BF16 = jnp.bfloat16
NCOL = 16
NROW = 8


def dg(a, b, ca, cb, **kw):
    return lax.dot_general(a, b, (((ca,), (cb,)), ((), ())), preferred_element_type=F32, **kw)


def place():
    return lax.axis_index("row"), lax.axis_index("col"), lax.axis_index("samp")


def rmod(a, n):
    return lax.rem(a, n)


def ring_shift(oz, from_core):
    if oz == 2:
        return 2 + 4 * from_core
    return (0, 1, None, 7)[oz]


def row_dest(oz, cx):
    row, col, samp = place()
    z, core = samp * 4 + row // 2, rmod(row, 2)
    to_core = rmod(core + cx, 2)
    to_z = rmod(z + ring_shift(oz, core), 8)
    return rmod(to_z, 4) * 2 + to_core, col, to_z // 4


def row_source(oz, cx):
    row, col, samp = place()
    z, core = samp * 4 + row // 2, rmod(row, 2)
    from_core = rmod(core + cx, 2)
    from_z = rmod(z + 8 - ring_shift(oz, from_core), 8)
    return rmod(from_z, 4) * 2 + from_core, col, from_z // 4


def spot(row):
    return rmod(row, 2) * 4 + row // 2


ROW_IDS = [(oz, cx) for oz in range(4) for cx in range(2) if (oz, cx) != (0, 0)]


def remote(src, dst, ssem, rsem, to):
    return pltpu.make_async_remote_copy(
        src_ref=src, dst_ref=dst, send_sem=ssem, recv_sem=rsem, device_id=to, device_id_type=MESH
    )


def col_start(src_of, slot_of, ssem, rsem):
    row, col, samp = place()

    def one(o, _):
        to = rmod(col + o, NCOL)
        remote(src_of(to), slot_of(col), ssem, rsem, (row, to, samp)).start()
        return 0

    lax.fori_loop(1, NCOL, one, 0, unroll=5)


def take(region, *sems):
    for sem in sems:
        pltpu.make_async_copy(region, region, sem).wait()


def row_start(src_of, slot_of, ssem, rsem):
    row = lax.axis_index("row")
    for oz, cx in ROW_IDS:
        to = row_dest(oz, cx)
        remote(src_of(to[0]), slot_of(row), ssem, rsem, to).start()


def signal(sem, to):
    pl.semaphore_signal(sem, inc=1, device_id=to, device_id_type=MESH)


def both(x, low, first):
    turned = pltpu.roll(x, 64, 1)
    return jnp.where(low, x, turned) if first else jnp.where(low, turned, x)


def sigmoid(x):
    return 0.5 * jnp.tanh(0.5 * x) + 0.5


def layer_norm(x, axis):
    mean = jnp.mean(x, axis, keepdims=True)
    cent = x - mean
    var = jnp.mean(cent * cent, axis, keepdims=True)
    return cent * lax.rsqrt(var + EPSILON)


def two_parts(x):
    coarse = x.astype(BF16)
    return jnp.concatenate([coarse, (x - coarse.astype(F32)).astype(BF16)], 0)


def step_kernel(
    res_ref, chain_ref, mask_ref,
    pair_hbm, relpos_hbm, tri_hbm, triout_hbm, biasp_hbm, single_hbm, ada_hbm, noisy_hbm,
    qkvw_hbm, outp_hbm, cot_hbm,
    pairout_hbm, block_hbm, gpair_hbm, gsingle_hbm,
    pairout_ref, block_ref, gpair_ref,
    pair_in, tri_w, ada_w, noisy, relpos_ref, triout_ref, biasp_ref, single_ref, qkvw_ref, outp_ref,
    cot_ref, idx_r, mrow, relpos_w,
    zl_s, tri_t, pf, gate, lrf, lbuf, recv_a, got, rcat, lcat, mtmp, tbuf, got_c, got_d, bias_f, bias_b, bias_got,
    cvec_s, scale_s, shift_s, wg_s, gate_t, g_t, noisy_t, normed, hidden, wqkv, q_t, kv_f,
    kv_own, kv_all, dmx_own, dmx_all, da_t, keyok, sraw, draw, qq_s, dd_s,
    mix_s, mix_r, dkv_s, dkv_m, dkv_o, dkv_r, dq_t, dkv_tok, dbias, db_s, db_r,
    dsc, dsh, dga, dc_s, dc_r, dc_p, gs_own, gs_all,
    sa, ra, sb, rb, sc, rc, sd, rd, se, re, skv, rkv, skf, rkf, sdm, rdm,
    sm, rm, sk, rk, sko, rko, sbb, rbb, st, rt, sp, rp_, sg, rg, loc, locm, ready,
):
    row, col, samp = place()
    core = rmod(row, 2)
    zlo = row // 2
    mate = (row + 1 - 2 * core, col, samp)
    far = (row, col, 1 - samp)
    barrier = pltpu.get_barrier_semaphore()

    loads = [
        pltpu.make_async_copy(s, d, loc.at[18 + i])
        for i, (s, d) in enumerate(
            [
                (pair_hbm, pair_in), (relpos_hbm, relpos_ref), (tri_hbm, tri_w),
                (single_hbm, single_ref), (qkvw_hbm, qkvw_ref), (ada_hbm, ada_w),
                (noisy_hbm, noisy), (cot_hbm, cot_ref), (triout_hbm, triout_ref),
                (biasp_hbm, biasp_ref), (outp_hbm, outp_ref),
            ]
        )
    ]
    for copy in loads:
        copy.start()
    for oz, cx in ROW_IDS:
        signal(barrier, row_source(oz, cx))

    def greet(o, _):
        signal(barrier, (row, rmod(col + o, NCOL), samp))
        return 0

    def greet_row(o, _):
        signal(barrier, (rmod(row + o, NROW), col, samp))
        return 0

    lax.fori_loop(1, NCOL, greet, 0, unroll=5)
    lax.fori_loop(1, NROW, greet_row, 0, unroll=7)
    signal(barrier, far)

    low = lax.broadcasted_iota(jnp.int32, (64, 128), 1) < 64
    low16 = lax.broadcasted_iota(jnp.int32, (16, 128), 1) < 64
    low1 = lax.broadcasted_iota(jnp.int32, (1, 128), 1) < 64
    diag = (lax.broadcasted_iota(jnp.int32, (128, 128), 0) < 64) == (
        lax.broadcasted_iota(jnp.int32, (128, 128), 1) < 64
    )

    def blockdiag(x):
        return jnp.where(diag, jnp.concatenate([x, x], 0), 0.0).astype(BF16)

    def indices(i, _):
        at = pl.ds(i, 1)
        idx_r[0, at, :] = jnp.full((1, 128), res_ref[row * 64 + i], jnp.int32)
        idx_r[1, at, :] = jnp.full((1, 128), chain_ref[row * 64 + i], jnp.int32)
        m = jnp.full((1, 128), mask_ref[row * 64 + i].astype(F32), F32)
        mrow[at, :] = m
        mrow[pl.ds(64 + i, 1), :] = m
        return 0

    lax.fori_loop(0, 64, indices, 0, unroll=4)
    mrow[...] = mrow[...].T
    relpos_w[...] = jnp.zeros_like(relpos_w)
    loads[1].wait()
    relpos_w[0:REL_BINS, :] = relpos_ref[...]
    loads[0].wait()

    def load(i, _):
        pf[pl.ds(i * 32, 32), :] = pair_in[i].astype(F32)
        return 0

    lax.fori_loop(0, 64, load, 0, unroll=4)
    bins = lax.broadcasted_iota(jnp.int32, (64, 128), 1)

    def normed_rows(t, _):
        parts = []
        for q in range(2):
            for hi in range(2):
                j = 2 * t + q + 16 * hi
                off = jnp.clip(idx_r[0] - res_ref[col * 32 + j] + 32, 0, 64)
                bucket = jnp.where(idx_r[1] == chain_ref[col * 32 + j], off, REL_BINS - 1)
                onehot = jnp.where(bucket == bins, 1.0, 0.0).astype(BF16)
                parts.append(
                    pf[pl.ds(j, 64, stride=32), :]
                    + jnp.dot(onehot, relpos_w[...], preferred_element_type=F32)
                )
        for q in range(2):
            for hi in range(2):
                pf[pl.ds(2 * t + q + 16 * hi, 64, stride=32), :] = parts[2 * q + hi]
        at = pl.ds(pl.multiple_of(t * 256, 256), 256)
        zl_s[at, :] = layer_norm(jnp.concatenate(parts, 0), -1).astype(BF16)
        return 0

    lax.fori_loop(0, 8, normed_rows, 0, unroll=2)
    loads[2].wait()
    tri_t[...] = tri_w[:, :512].astype(F32).T.astype(BF16)

    def project(h, t):
        at = pl.ds(pl.multiple_of(t * 256, 256), 256)
        pt = dg(tri_t[h * 256 : h * 256 + 256, :], zl_s[at, :], 1, 1)
        val = sigmoid(pt[128:]) * pt[:128]
        for q in range(2):
            lo = 2 * t + q
            mask = mrow[0:1, :] * jnp.where(
                low1, mask_ref[col * 32 + lo].astype(F32), mask_ref[col * 32 + 16 + lo].astype(F32)
            )
            lrf[pl.ds(h * 2048 + lo, 128, stride=16), :] = val[:, q * 128 : q * 128 + 128] * mask

    pieces = [(0, slice(0, 8)), (1, slice(0, 4)), (1, slice(4, 8))]
    a_src = [lambda to, h=h, p=p: lbuf.at[h, to, p] for h, p in pieces]
    a_slot = [lambda c, h=h, p=p: recv_a.at[h, c, p] for h, p in pieces]
    b_src = [lambda r, h=h: recv_a.at[h, :, spot(r)] for h in range(2)]
    b_slot = [lambda r, h=h: got.at[h, r] for h in range(2)]
    own_a = [pltpu.make_async_copy(lbuf.at[h, col], recv_a.at[h, col], loc.at[h]) for h in range(2)]
    own_b = [
        pltpu.make_async_copy(recv_a.at[h, :, spot(row)], got.at[h, row], loc.at[2 + h])
        for h in range(2)
    ]
    for h in range(2):

        def one_side(t, _):
            project(h, t)
            return 0

        lax.fori_loop(0, 8, one_side, 0, unroll=2)

        def pack(c, _):
            lbuf[h, c] = lrf[pl.ds(h * 2048 + c * 128, 128), :].astype(BF16).reshape(8, 16, 128)
            return 0

        lax.fori_loop(0, 16, pack, 0, unroll=2)
        if h == 0:
            pl.semaphore_wait(barrier, 7 + 15 + 7 + 1)
            signal(ready, far)
        own_a[h].start()
        for i in ((0,), (1, 2))[h]:
            col_start(a_src[i], a_slot[i], sa.at[i], ra.at[i])

    for copy in loads[3:6]:
        copy.wait()
    cvec = layer_norm(single_ref[...].astype(F32), -1).astype(BF16)
    cvec_s[...] = cvec
    wqkv[...] = jnp.zeros_like(wqkv)
    for p in range(3):
        wqkv[p * 64 : p * 64 + 48, :] = qkvw_ref[p]
    scale_s[...] = sigmoid(jnp.dot(cvec, ada_w[:, :768], preferred_element_type=F32))
    shift_s[...] = jnp.dot(cvec, ada_w[:, 768:1536], preferred_element_type=F32)
    for copy in loads[6:]:
        copy.wait()

    def sample(s, _):
        at = pl.ds(pl.multiple_of(s * 64, 64), 64)
        n = layer_norm(noisy[at, :].astype(F32), -1)
        normed[at, :] = n
        hidden[at, :] = (scale_s[...] * n + shift_s[...]).astype(BF16)
        return 0

    lax.fori_loop(0, 8, sample, 0)
    own_a[0].wait()
    take(recv_a.at[0, 0:15], sa.at[0], ra.at[0])
    own_b[0].start()
    row_start(b_src[0], b_slot[0], sb.at[0], rb.at[0])

    feat = lax.broadcasted_iota(jnp.int32, (768, 64), 1)
    sel = jnp.where(
        (lax.broadcasted_iota(jnp.int32, (768, 64), 0) == col * 48 + feat) & (feat < 48), 1.0, 0.0
    ).astype(BF16)
    wg_s[...] = jnp.dot(ada_w[:, 1536:], sel, preferred_element_type=F32).astype(BF16)
    gate_t[...] = sigmoid(
        dg(wg_s[...], jnp.concatenate([cvec_s[...], cvec_s[...]], 0), 0, 1)
    )
    lane = lax.broadcasted_iota(jnp.int32, (64, 128), 1)
    tok = lax.broadcasted_iota(jnp.int32, (64, 128), 0)
    put = [jnp.where(lane == tok + 64 * h, 1.0, 0.0).astype(BF16) for h in range(2)]
    for u in range(4):
        g = jnp.dot(cot_ref[2 * u], put[0], preferred_element_type=F32) + jnp.dot(
            cot_ref[2 * u + 1], put[1], preferred_element_type=F32
        )
        g_t[u] = g
        dmx_own[:, u * 128 : u * 128 + 128] = (g * gate_t[:48, :]).astype(BF16)
    dm_src, dm_slot = (lambda to: dmx_own), (lambda c: dmx_all.at[c])
    dm_keep = pltpu.make_async_copy(dmx_own, dmx_all.at[col], loc.at[5])
    dm_keep.start()
    col_start(dm_src, dm_slot, sdm.at[0], rdm.at[0])
    kv_f[...] = dg(hidden[...], wqkv[64:, :], 1, 1)

    def kv_pack(t, _):
        r0 = kv_f[pl.ds(t * 32, 16), :]
        r1 = kv_f[pl.ds(t * 32 + 16, 16), :]
        to = pl.ds(pl.multiple_of(rmod(t, 2) * 16, 16), 16)
        kv_own[0, t // 2, to, :] = jnp.where(low16, r0, pltpu.roll(r1, 64, 1)).astype(BF16)
        kv_own[1, t // 2, to, :] = jnp.where(low16, pltpu.roll(r0, 64, 1), r1).astype(BF16)
        return 0

    lax.fori_loop(0, 16, kv_pack, 0, unroll=2)
    kv_keep = pltpu.make_async_copy(kv_own, kv_all.at[row], loc.at[4])
    kv_keep.start()
    kv_out = []
    for o in range(1, 4):
        to = (rmod(zlo + o, 4) * 2 + core, col, samp)
        kv_out.append(remote(kv_own, kv_all.at[row], skv.at[o], rkv.at[o], to))
    kv_mate = remote(kv_own, kv_all.at[row], skf.at[0], rkf.at[0], mate)
    own_a[1].wait()
    for k in range(2):
        take(recv_a.at[1, 0:15, 0:4], sa.at[1 + k], ra.at[1 + k])
        cx = rmod(core + k, 2)
        for oz in (2, 1, 3):
            to = row_dest(oz, cx)
            remote(b_src[1](to[0]), b_slot[1](row), sb.at[1], rb.at[1], to).start()

        @pl.when(cx == 1)
        def _():
            remote(b_src[1](mate[0]), b_slot[1](row), sb.at[1], rb.at[1], mate).start()

    own_b[1].start()

    def gates(t, _):
        at = pl.ds(pl.multiple_of(t * 256, 256), 256)
        gate[at, :] = sigmoid(
            jnp.dot(zl_s[at, :], tri_w[:, 512:], preferred_element_type=F32)
        )
        return 0

    lax.fori_loop(0, 8, gates, 0)
    for h in (1, 0):
        own_b[h].wait()
        take(got.at[h, 0:7], sb.at[h], rb.at[h])

    def turn(r, _):
        x = got[1, r].reshape(256, 128).astype(F32).T.astype(BF16)
        at = pl.ds(pl.multiple_of(r * 64, 64), 64)
        rcat[at, 0:256] = x[:64]
        rcat[at, 256:512] = x[64:]
        return 0

    lax.fori_loop(0, 8, turn, 0, unroll=2)
    low256 = lax.broadcasted_iota(jnp.int32, (256, 128), 1) < 64
    turns = ((2, 1), (3, 0))
    for i, pair in enumerate(turns):
        for k, oz in enumerate(pair):
            z = rmod(zlo + oz, 4)
            la = got[0, 2 * z].reshape(256, 128).astype(F32)
            lb = got[0, 2 * z + 1].reshape(256, 128).astype(F32)
            lanes = slice(k * 128, k * 128 + 128)
            lcat[i, 0:256, lanes] = jnp.where(low256, la, pltpu.roll(lb, 64, 1)).astype(BF16)
            lcat[i, 256:512, lanes] = jnp.where(low256, pltpu.roll(la, 64, 1), lb).astype(BF16)
    c_src = [lambda r, p=p: tbuf.at[r, p] for p in (slice(0, 8), slice(8, 16))]
    c_slot = [lambda r, p=p: got_c.at[spot(r), p] for p in (slice(0, 8), slice(8, 16))]
    own_c = [
        pltpu.make_async_copy(c_src[h](row), c_slot[h](row), loc.at[6 + 3 * h]) for h in range(2)
    ]

    def tri(i, part):
        mtmp[...] = jnp.dot(
            rcat[part * 256 : part * 256 + 256, :], lcat[i], preferred_element_type=F32
        )

        def out(rj, _):
            for k, oz in enumerate(turns[i]):
                z = rmod(zlo + oz, 4)
                for jh in range(2):
                    at = rj * 64 + jh * 32
                    a = mtmp[pl.ds(at, 16), k * 128 : k * 128 + 128]
                    b = mtmp[pl.ds(at + 16, 16), k * 128 : k * 128 + 128]
                    even_row = jnp.where(low16, a, pltpu.roll(b, 64, 1))
                    odd_row = jnp.where(low16, pltpu.roll(a, 64, 1), b)
                    tbuf[2 * z, part * 8 + 2 * rj + jh] = even_row.astype(BF16)
                    tbuf[2 * z + 1, part * 8 + 2 * rj + jh] = odd_row.astype(BF16)
            return 0

        lax.fori_loop(0, 4, out, 0, unroll=2)

    for part in range(2):
        for i, pair in enumerate(turns):
            tri(i, part)
            for oz in pair:
                for cx in range(2):
                    if (oz, cx) != (0, 0):
                        to = row_dest(oz, cx)
                        remote(
                            c_src[part](to[0]), c_slot[part](row), sc.at[part], rc.at[part], to
                        ).start()
        own_c[part].start()
    kv_mate.start()
    for copy in kv_out:
        copy.start()
    d_own = pltpu.make_async_copy(got_c.at[:, col], got_d.at[col], loc.at[7])

    def d_start(part):
        def one(o, _):
            to = part * 8 + rmod(col + o, 8)

            @pl.when(to != col)
            def _():
                remote(got_c.at[:, to], got_d.at[col], sd.at[0], rd.at[0], (row, to, samp)).start()

            return 0

        lax.fori_loop(0, 8, one, 0, unroll=4)

    dm_keep.wait()
    take(dmx_all.at[0:15], sdm.at[0], rdm.at[0])
    da_t[...] = jnp.zeros_like(da_t)
    da_t[:48, :] = (
        jnp.dot(outp_ref[...], dmx_all[...].reshape(768, 512), preferred_element_type=F32)
        .astype(BF16)
        .astype(F32)
    )
    for part in range(2):
        own_c[part].wait()
        take(got_c.at[0:7, 0:8], sc.at[part], rc.at[part])
        d_start(part)
    d_own.start()

    q_t[...] = dg(wqkv[:64, :], hidden[...], 1, 1)
    noisy_t[...] = dg(sel, noisy[...], 0, 1)

    def key_mask(t, _):
        jb, lo = t // 16, rmod(t, 16)
        keyok[pl.ds(t, 1), :] = jnp.where(
            low1,
            mask_ref[jb * 32 + lo].astype(F32),
            mask_ref[jb * 32 + 16 + lo].astype(F32),
        )
        return 0

    lax.fori_loop(0, 256, key_mask, 0, unroll=4)

    for o in range(1, 4):
        came = rmod(zlo + 4 - o, 4) * 2 + core
        remote(kv_own, kv_all.at[came], skv.at[o], rkv.at[o], mate).wait_recv()
        remote(kv_all.at[came], kv_all.at[came], skf.at[o], rkf.at[o], mate).start()


    def half_of(ref, u, sh):
        tile = ref[:, pl.ds(pl.multiple_of(u * 128, 128), 128)].astype(F32)
        return blockdiag(both(tile, low, sh == 0))

    def keys(which, s):
        return jnp.concatenate([kv_all[r, which, s] for r in range(NROW)], 0)

    scale = 1.0 / HEAD_DIM**0.5

    def raw(u, _):
        for sh in range(2):
            s = 2 * u + sh
            qq, dd = half_of(q_t, u, sh), half_of(da_t, u, sh)
            qq_s[s] = qq
            dd_s[s] = dd
            sraw[s] = jnp.dot(keys(0, s), qq, preferred_element_type=F32) * scale
            draw[s] = jnp.dot(keys(1, s), dd, preferred_element_type=F32)
        return 0

    d_own.wait()
    take(got_d.at[0:15], sd.at[0], rd.at[0])

    def widen(c, _):
        lrf[pl.ds(c * 128, 128), :] = got_d[c].reshape(128, 128).astype(F32)
        return 0

    lax.fori_loop(0, 16, widen, 0)

    def stage3(t, _):
        tn = layer_norm(
            jnp.concatenate([lrf[pl.ds(2 * t + q, 128, stride=16), :] for q in range(2)], 1), 0
        ).astype(BF16)
        upd = dg(tn, triout_ref[...], 0, 0) * gate[pl.ds(pl.multiple_of(t * 256, 256), 256), :]
        spots = [pl.ds(2 * t + q + 16 * hi, 64, stride=32) for q in range(2) for hi in range(2)]
        outs = [
            (pf[at, :] + upd[i * 64 : i * 64 + 64]).astype(BF16) for i, at in enumerate(spots)
        ]
        for at, val in zip(spots, outs):
            pf[at, :] = val.astype(F32)
        tile = dg(biasp_ref[...], jnp.concatenate(outs, 0), 1, 1)
        for q in range(2):
            bias_f[pl.ds(2 * t + q, 16, stride=16), :] = tile[:, q * 128 : q * 128 + 128]
        return 0

    lax.fori_loop(0, 8, stage3, 0, unroll=4)
    bias_b[...] = bias_f[...].astype(BF16).reshape(16, 16, 128)
    e_src, e_slot = (lambda c: bias_b.at[c]), (lambda c: bias_got.at[c])
    own_e = pltpu.make_async_copy(bias_b.at[col], bias_got.at[col], loc.at[8])
    own_e.start()
    col_start(e_src, e_slot, se.at[0], re.at[0])

    kv_keep.wait()
    for copy in kv_out:
        copy.wait_send()
    kv_mate.wait_send()
    for o in range(4):
        came = rmod(zlo + 4 - o, 4) * 2
        remote(
            kv_all.at[came + core], kv_all.at[came + 1 - core], skf.at[o], rkf.at[o], mate
        ).wait_recv()
        if o > 0:
            remote(
                kv_all.at[came + core], kv_all.at[came + core], skf.at[o], rkf.at[o], mate
            ).wait_send()
    lax.fori_loop(0, 4, raw, 0)
    def store(i, _):
        pairout_ref[i] = pf[pl.ds(i * 32, 32), :].astype(BF16)
        return 0

    lax.fori_loop(0, 64, store, 0, unroll=4)
    out_pair = pltpu.make_async_copy(pairout_ref, pairout_hbm, loc.at[14])
    out_pair.start()
    dbias[...] = jnp.zeros_like(dbias)
    own_e.wait()
    take(bias_got.at[0:15], se.at[0], re.at[0])

    bias_f[...] = bias_got[...].reshape(256, 128).astype(F32)

    def mix_src(u):
        return lambda f: mix_s.at[u, f]

    def mix_slot(u):
        return lambda h: mix_r.at[u, h]

    def to_mate(u):
        return remote(dkv_s.at[:, 1 - core, u], dkv_m.at[u], sk.at[u], rk.at[u], mate)

    def to_chip(u, o):
        z = rmod(zlo + o, 4)
        return remote(
            dkv_o.at[u, z], dkv_r.at[u, zlo], sko.at[u, o], rko.at[u, o], (z * 2 + core, col, samp)
        )

    def pass_on(u):
        to_mate(u).wait_recv()
        for z in range(4):
            dkv_o[u, z] = (
                dkv_s[z, core, u].astype(F32) + dkv_m[u, z].astype(F32)
            ).astype(BF16)
        for o in range(1, 4):
            to_chip(u, o).start()

    def pair_of_samples(u, _):
        folded, dqs, grads = [], [], []
        for sh in range(2):
            s = 2 * u + sh
            kp, vp = keys(0, s), keys(1, s)
            sco = jnp.where(keyok[...] > 0, sraw[s] + bias_f[...], -1000000000.0)
            top = jnp.max(sco, 0, keepdims=True)
            top = jnp.maximum(top, pltpu.roll(top, 64, 1))
            ex = jnp.exp(sco - top)
            tot = jnp.sum(ex, 0, keepdims=True)
            probs = ex * (1.0 / (tot + pltpu.roll(tot, 64, 1)))
            pb = probs.astype(BF16)
            folded.append(dg(vp, pb, 0, 0))
            dp = draw[s]
            dot = jnp.sum(probs * dp, 0, keepdims=True)
            ds = probs * (dp - (dot + pltpu.roll(dot, 64, 1)))
            grads.append(ds)
            dsb = (ds * scale).astype(BF16)
            dqs.append(dg(kp, dsb, 0, 0))
            dk = dg(dsb, qq_s[s], 1, 1).astype(BF16)
            dv = dg(pb, dd_s[s], 1, 1).astype(BF16)
            for r in range(NROW):
                dkv_s[r // 2, r % 2, u, sh] = dk[r * 32 : r * 32 + 32]
                dkv_s[r // 2, r % 2, u, 2 + sh] = dv[r * 32 : r * 32 + 32]

        def fold(m0, m1):
            return jnp.where(
                low,
                m0[:64] + pltpu.roll(m0[64:], 64, 1),
                pltpu.roll(m1[:64], 64, 1) + m1[64:],
            ).astype(BF16)

        dbias[...] += grads[0] + grads[1]
        att = fold(*folded)
        dq_t[u] = fold(*dqs)
        mix_s[u] = dg(outp_ref[...], att[:48], 0, 0).astype(BF16).reshape(16, 48, 128)
        pltpu.make_async_copy(mix_s.at[u, col], mix_r.at[u, col], locm.at[u]).start()
        to_mate(u).start()
        col_start(mix_src(u), mix_slot(u), sm.at[u], rm.at[u])

        @pl.when(u > 0)
        def _():
            pass_on(u - 1)

        return 0

    lax.fori_loop(0, 4, pair_of_samples, 0)

    db_s[...] = dbias[...].astype(BF16).reshape(16, 16, 128)
    own_db = pltpu.make_async_copy(db_s.at[col], db_r.at[samp, col], loc.at[29])
    own_db.start()

    def db_copy(o):
        to = rmod(col + o, NCOL)
        return remote(
            db_s.at[to], db_r.at[samp, col], sbb.at[1], rbb.at[1], (row, to, 1 - samp)
        )

    def db_send(o, _):
        db_copy(o).start()
        return 0

    pass_on(3)
    pl.semaphore_wait(ready, 1)
    lax.fori_loop(0, NCOL, db_send, 0, unroll=4)
    near_src, near_slot = (lambda c: db_s.at[c]), (lambda c: db_r.at[samp, c])
    col_start(near_src, near_slot, sbb.at[0], rbb.at[0])

    dga[...] = jnp.zeros_like(dga)

    def mixed_of(u, _):
        pltpu.make_async_copy(mix_s.at[u, col], mix_r.at[u, col], locm.at[u]).wait()
        take(mix_r.at[u, 0:15], sm.at[u], rm.at[u])
        total = mix_r[u, 0].astype(F32)
        for h in range(1, NCOL):
            total = total + mix_r[u, h].astype(F32)
        lanes = pl.ds(pl.multiple_of(u * 128, 128), 128)
        out = noisy_t[:48, lanes] + gate_t[:48, :] * total
        block_ref[2 * u] = out[:, :64].astype(BF16)
        block_ref[2 * u + 1] = pltpu.roll(out, 64, 1)[:, :64].astype(BF16)
        dga[:48, :] += g_t[u] * total
        return 0

    lax.fori_loop(0, 3, mixed_of, 0)

    dsc[...] = jnp.zeros_like(dsc)
    dsh[...] = jnp.zeros_like(dsh)

    def hidden_grad(u, _):
        to_mate(u).wait_send()
        for o in range(1, 4):
            came = rmod(zlo + 4 - o, 4)
            remote(
                dkv_o.at[u, came], dkv_r.at[u, came], sko.at[u, o], rko.at[u, o], mate
            ).wait_recv()
            to_chip(u, o).wait_send()
        dkv_r[u, zlo] = dkv_o[u, zlo]
        tot = dkv_r[u, 0].astype(F32)
        for z in range(1, 4):
            tot = tot + dkv_r[u, z].astype(F32)
        for sh in range(2):
            for jb in range(2):
                a = tot[sh, jb * 16 : jb * 16 + 16]
                b = tot[2 + sh, jb * 16 : jb * 16 + 16]
                base = sh * 64 + jb * 32
                dkv_tok[base : base + 16, :] = jnp.where(low16, a, pltpu.roll(b, 64, 1)).astype(BF16)
                dkv_tok[base + 16 : base + 32, :] = jnp.where(
                    low16, pltpu.roll(a, 64, 1), b
                ).astype(BF16)
        dh = dg(dq_t[u], wqkv[:64, :], 0, 0) + jnp.dot(
            dkv_tok[...], wqkv[64:, :], preferred_element_type=F32
        )
        n = normed[pl.ds(pl.multiple_of(u * 128, 128), 128), :]
        w = dh * n
        dsc[...] += w[:64] + w[64:]
        dsh[...] += dh[:64] + dh[64:]
        return 0

    lax.fori_loop(0, 3, hidden_grad, 0)
    mixed_of(3, 0)
    out_block = pltpu.make_async_copy(block_ref, block_hbm, loc.at[15])
    out_block.start()
    hidden_grad(3, 0)
    sg_ = scale_s[...]
    part = dg(two_parts(dsc[...] * sg_ * (1.0 - sg_)), ada_w[:, :768], 1, 1)
    part = part + dg(two_parts(dsh[...]), ada_w[:, 768:1536], 1, 1)
    part = part[:64] + part[64:]
    acc = dga[...]
    acc = (acc + pltpu.roll(acc, 64, 1)) * gate_t[...] * (1.0 - gate_t[...])
    coarse = acc.astype(BF16)
    fine = (acc - coarse.astype(F32)).astype(BF16)
    part = part + (dg(coarse, wg_s[...], 0, 1) + dg(fine, wg_s[...], 0, 1))[:64]
    dc_s[...] = part.reshape(8, 8, 384)

    half_col = col // 2
    even = rmod(col, 2) == 0

    def part_copy(o):
        g = rmod(half_col + o, 8)
        return remote(dc_s.at[g], dc_r.at[col], st.at[0], rt.at[0], (row, 2 * g, samp))

    @pl.when(jnp.logical_not(even))
    def _():
        part_copy(0).start()

    def part_send(o, _):
        part_copy(o).start()
        return 0

    lax.fori_loop(1, 8, part_send, 0, unroll=7)

    own_db.wait()
    take(db_r.at[0, 0:15], sbb.at[0], rbb.at[0])
    take(db_r.at[0], sbb.at[1], rbb.at[1])
    dbias[...] = (db_r[0].astype(F32) + db_r[1].astype(F32)).reshape(256, 128)
    biasp3 = jnp.concatenate([biasp_ref[...]] * 3, 0)

    def grad(t, _):
        d = jnp.concatenate([dbias[pl.ds(2 * t + q, 16, stride=16), :] for q in range(2)], 1)
        d1 = d.astype(BF16)
        rest = d - d1.astype(F32)
        d2 = rest.astype(BF16)
        d3 = (rest - d2.astype(F32)).astype(BF16)
        g = dg(jnp.concatenate([d1, d2, d3], 0), biasp3, 0, 0)
        for q in range(2):
            for hi in range(2):
                base = q * 128 + hi * 64
                gpair_ref[pl.ds(2 * t + q + 16 * hi, 64, stride=32), :] = g[base : base + 64]
        return 0

    lax.fori_loop(0, 4, grad, 0, unroll=2)

    def own_copy(o):
        return remote(
            gs_own, gs_all.at[half_col], sg.at[0], rg.at[0], (row, rmod(col + o, NCOL), samp)
        )

    @pl.when(even)
    def _():
        dc_r[col] = dc_s[half_col]

        take(dc_r.at[0:15], rt.at[0])
        tot = dc_r[0]
        for c in range(1, NCOL):
            tot = tot + dc_r[c]
        dc_p[samp] = tot
        remote(dc_p.at[samp], dc_p.at[samp], sp.at[0], rp_.at[0], far).start()

    lax.fori_loop(4, 8, grad, 0, unroll=2)
    out_grad = pltpu.make_async_copy(gpair_ref, gpair_hbm, loc.at[16])
    out_grad.start()

    @pl.when(even)
    def _():
        own = single_ref[...].astype(F32).reshape(8, 8, 384)
        mine = jnp.zeros((8, 384), F32)
        for g in range(8):
            mine = mine + jnp.where(half_col == g, own[g], 0.0)
        mean = jnp.mean(mine, -1, keepdims=True)
        cent = mine - mean
        inv = lax.rsqrt(jnp.mean(cent * cent, -1, keepdims=True) + EPSILON)
        unit = cent * inv
        remote(dc_p.at[samp], dc_p.at[1 - samp], sp.at[0], rp_.at[0], far).wait_recv()
        remote(dc_p.at[samp], dc_p.at[samp], sp.at[0], rp_.at[0], far).wait_send()
        up = dc_p[0] + dc_p[1]
        gs_own[...] = inv * (
            up - jnp.mean(up, -1, keepdims=True) - unit * jnp.mean(up * unit, -1, keepdims=True)
        )

        def tell(o, _):
            own_copy(o).start()
            return 0

        lax.fori_loop(1, NCOL, tell, 0, unroll=5)
        gs_all[half_col] = gs_own[...]

    @pl.when(even)
    def _():
        take(dc_s.at[0:7], st.at[0])
        take(dc_r.at[0:15], sg.at[0])
        take(gs_all.at[0:7], rg.at[0])

    @pl.when(jnp.logical_not(even))
    def _():
        take(dc_s, st.at[0])
        take(gs_all, rg.at[0])

    out_single = pltpu.make_async_copy(gs_all, gsingle_hbm, loc.at[17])
    out_single.start()
    for copy in (out_pair, out_block, out_grad, out_single):
        copy.wait()


def finish_kernel(*refs):
    n = 4
    ins, outs, bufs = refs[:n], refs[n : 2 * n], refs[2 * n : 3 * n]
    got, put = refs[3 * n], refs[3 * n + 1]
    reads = [pltpu.make_async_copy(ins[i], bufs[i], got.at[i]) for i in range(n)]
    writes = [pltpu.make_async_copy(bufs[i], outs[i], put.at[i]) for i in range(n)]
    for copy in reads:
        copy.start()
    for i in (3, 1, 0, 2):
        reads[i].wait()
        writes[i].start()
    for copy in writes:
        copy.wait()


def finished(arrays):
    hbm = pl.BlockSpec(memory_space=pl.ANY)
    return pl.pallas_call(
        finish_kernel,
        out_shape=[jax.ShapeDtypeStruct(x.shape, x.dtype) for x in arrays],
        in_specs=[hbm] * 4,
        out_specs=[hbm] * 4,
        scratch_shapes=[pltpu.VMEM(x.shape, x.dtype) for x in arrays]
        + [pltpu.SemaphoreType.DMA((4,)), pltpu.SemaphoreType.DMA((4,))],
        compiler_params=pltpu.CompilerParams(vmem_limit_bytes=60 * 1024 * 1024),
        name="finish",
    )(*arrays)


def on_device(
    pair_in, residue_index, chain_index, token_mask, relpos_weight, tri_proj, tri_out, bias_proj,
    single, ada_proj, noisy, qkv_proj, out_proj, cotangent,
):
    sm = pl.BlockSpec(memory_space=pltpu.SMEM)
    hbm = pl.BlockSpec(memory_space=pl.ANY)
    dma = pltpu.SemaphoreType.DMA
    v = pltpu.VMEM
    pair_out, block_t, grad_pair, grad_single = pl.pallas_call(
        step_kernel,
        out_shape=(
            jax.ShapeDtypeStruct((64, 32, 128), BF16),
            jax.ShapeDtypeStruct((8, 48, 64), BF16),
            jax.ShapeDtypeStruct((2048, 128), F32),
            jax.ShapeDtypeStruct((8, 8, 384), F32),
        ),
        in_specs=[sm] * 3 + [hbm] * 11,
        out_specs=(hbm,) * 4,
        scratch_shapes=[
            v((64, 32, 128), BF16), v((8, 48, 64), BF16), v((2048, 128), F32),
            v((64, 32, 128), BF16), v((128, 640), BF16), v((384, 2304), BF16), v((512, 768), BF16),
            v((REL_BINS, 128), BF16), v((128, 128), BF16), v((16, 128), BF16), v((64, 384), BF16),
            v((3, 48, 768), BF16), v((48, 768), BF16), v((8, 48, 64), BF16),
            v((2, 64, 128), jnp.int32), v((128, 128), F32), v((128, 128), BF16),
            v((2048, 128), BF16), v((512, 128), BF16), v((2048, 128), F32), v((2048, 128), F32),
            v((4096, 128), F32),
            v((2, 16, 8, 16, 128), BF16), v((2, 16, 8, 16, 128), BF16),
            v((2, 8, 16, 16, 128), BF16), v((512, 512), BF16), v((2, 512, 256), BF16),
            v((256, 256), F32),
            v((8, 16, 16, 128), BF16), v((8, 16, 16, 128), BF16), v((16, 8, 16, 128), BF16),
            v((256, 128), F32), v((16, 16, 128), BF16), v((16, 16, 128), BF16),
            v((64, 384), BF16), v((64, 768), F32), v((64, 768), F32), v((384, 64), BF16),
            v((64, 128), F32), v((4, 48, 128), F32), v((64, 512), F32), v((512, 768), F32),
            v((512, 768), BF16), v((192, 768), BF16), v((64, 512), F32), v((512, 128), F32),
            v((2, 8, 32, 128), BF16), v((8, 2, 8, 32, 128), BF16), v((48, 512), BF16),
            v((16, 48, 512), BF16), v((64, 512), F32), v((256, 128), F32), v((8, 256, 128), F32),
            v((8, 256, 128), F32), v((8, 128, 128), BF16), v((8, 128, 128), BF16),
            v((4, 16, 48, 128), BF16), v((4, 16, 48, 128), BF16), v((4, 2, 4, 4, 32, 128), BF16),
            v((4, 4, 4, 32, 128), BF16), v((4, 4, 4, 32, 128), BF16), v((4, 4, 4, 32, 128), BF16),
            v((4, 64, 128), BF16), v((128, 128), BF16), v((256, 128), F32), v((16, 16, 128), BF16),
            v((2, 16, 16, 128), BF16),
            v((64, 768), F32), v((64, 768), F32), v((64, 128), F32), v((8, 8, 384), F32),
            v((16, 8, 384), F32), v((2, 8, 384), F32), v((8, 384), F32), v((8, 8, 384), F32),
            dma((3,)), dma((3,)), dma((2,)), dma((2,)), dma((2,)), dma((2,)),
            dma((1,)), dma((1,)), dma((1,)), dma((1,)), dma((4,)), dma((4,)),
            dma((4,)), dma((4,)), dma((1,)), dma((1,)),
            dma((4,)), dma((4,)), dma((4,)), dma((4,)), dma((4, 4)), dma((4, 4)),
            dma((2,)), dma((2,)), dma((1,)), dma((1,)), dma((1,)), dma((1,)),
            dma((1,)), dma((1,)), dma((30,)), dma((4,)), pltpu.SemaphoreType.REGULAR,
        ],
        compiler_params=pltpu.CompilerParams(
            collective_id=1, has_side_effects=True, vmem_limit_bytes=60 * 1024 * 1024
        ),
        name="step",
    )(
        residue_index, chain_index, token_mask, pair_in, relpos_weight, tri_proj, tri_out,
        bias_proj.T, single, ada_proj, noisy.reshape(512, 768), qkv_proj.transpose(1, 2, 0),
        out_proj, cotangent.transpose(0, 2, 1),
    )
    pair_out, block_t, grad_pair, grad_single = finished(
        (pair_out, block_t, grad_pair, grad_single)
    )
    return (
        pair_out,
        block_t.transpose(0, 2, 1),
        grad_pair.reshape(64, 32, 128),
        grad_single.reshape(64, 384),
    )


def solution(mesh):
    return jax.shard_map(
        on_device,
        mesh=mesh,
        in_specs=(
            P("row", "col", None), P(), P(), P(), P(), P(), P(), P(), P("row", None), P(),
            P("samp", "row", None), P(None, None, "col"), P("col", None), P("samp", "row", "col"),
        ),
        out_specs=(
            P("row", "col", None), P("samp", "row", "col"), P("row", "col", None), P("row", None),
        ),
        check_vma=False,
    )
```

```python
import jax
import jax.numpy as jnp
from jax import lax
from jax.experimental import pallas as pl
from jax.experimental.pallas import tpu as pltpu
from jax.sharding import PartitionSpec as P

HEAD_DIM = 48
REL_BINS = 66
EPSILON = 1e-05
MESH = pl.DeviceIdType.MESH
F32 = jnp.float32
BF16 = jnp.bfloat16
NCOL = 16
NROW = 8


def dg(a, b, ca, cb, **kw):
    return lax.dot_general(a, b, (((ca,), (cb,)), ((), ())), preferred_element_type=F32, **kw)


def place():
    return lax.axis_index("row"), lax.axis_index("col"), lax.axis_index("samp")


def rmod(a, n):
    return lax.rem(a, n)


def ring_shift(oz, from_core):
    if oz == 2:
        return 2 + 4 * from_core
    return (0, 1, None, 7)[oz]


def row_dest(oz, cx):
    row, col, samp = place()
    z, core = samp * 4 + row // 2, rmod(row, 2)
    to_core = rmod(core + cx, 2)
    to_z = rmod(z + ring_shift(oz, core), 8)
    return rmod(to_z, 4) * 2 + to_core, col, to_z // 4


def row_source(oz, cx):
    row, col, samp = place()
    z, core = samp * 4 + row // 2, rmod(row, 2)
    from_core = rmod(core + cx, 2)
    from_z = rmod(z + 8 - ring_shift(oz, from_core), 8)
    return rmod(from_z, 4) * 2 + from_core, col, from_z // 4


def spot(row):
    return rmod(row, 2) * 4 + row // 2


ROW_IDS = [(oz, cx) for oz in range(4) for cx in range(2) if (oz, cx) != (0, 0)]


def remote(src, dst, ssem, rsem, to):
    return pltpu.make_async_remote_copy(
        src_ref=src, dst_ref=dst, send_sem=ssem, recv_sem=rsem, device_id=to, device_id_type=MESH
    )


def col_start(src_of, slot_of, ssem, rsem):
    row, col, samp = place()

    def one(o, _):
        to = rmod(col + o, NCOL)
        remote(src_of(to), slot_of(col), ssem, rsem, (row, to, samp)).start()
        return 0

    lax.fori_loop(1, NCOL, one, 0)


def take(region, *sems):
    for sem in sems:
        pltpu.make_async_copy(region, region, sem).wait()


def row_start(src_of, slot_of, ssem, rsem):
    row = lax.axis_index("row")
    for oz, cx in ROW_IDS:
        to = row_dest(oz, cx)
        remote(src_of(to[0]), slot_of(row), ssem, rsem, to).start()


def signal(sem, to):
    pl.semaphore_signal(sem, inc=1, device_id=to, device_id_type=MESH)


def both(x, low, first):
    turned = pltpu.roll(x, 64, 1)
    return jnp.where(low, x, turned) if first else jnp.where(low, turned, x)


def sigmoid(x):
    return 0.5 * jnp.tanh(0.5 * x) + 0.5


def layer_norm(x, axis):
    mean = jnp.mean(x, axis, keepdims=True)
    cent = x - mean
    var = jnp.mean(cent * cent, axis, keepdims=True)
    return cent * lax.rsqrt(var + EPSILON)


def two_parts(x):
    coarse = x.astype(BF16)
    return jnp.concatenate([coarse, (x - coarse.astype(F32)).astype(BF16)], 0)


def step_kernel(
    res_ref, chain_ref, mask_ref,
    pair_hbm, relpos_hbm, tri_hbm, triout_hbm, biasp_hbm, single_hbm, ada_hbm, noisy_hbm,
    qkvw_hbm, outp_hbm, cot_hbm,
    pairout_hbm, block_hbm, gpair_hbm, gsingle_hbm,
    pairout_ref, block_ref, gpair_ref,
    pair_in, tri_w, ada_w, noisy, relpos_ref, triout_ref, biasp_ref, single_ref, qkvw_ref, outp_ref,
    cot_ref, idx_r, mrow, relpos_w,
    zl_s, tri_t, pf, gate, lrf, lbuf, recv_a, got, rcat, lcat, mtmp, tbuf, got_c, got_d, bias_f, bias_b, bias_got,
    cvec_s, scale_s, shift_s, wg_s, gate_t, g_t, noisy_t, normed, hidden, wqkv, q_t, kv_f,
    kv_own, kv_all, dmx_own, dmx_all, da_t, keyok, sraw, draw,
    mix_s, mix_r, dkv_s, dkv_m, dkv_o, dkv_r, dq_t, dkv_tok, dbias, db_s, db_r,
    dsc, dsh, dga, dc_s, dc_r, dc_p, gs_own, gs_all,
    sa, ra, sb, rb, sc, rc, sd, rd, se, re, skv, rkv, skf, rkf, sdm, rdm,
    sm, rm, sk, rk, sko, rko, sbb, rbb, st, rt, sp, rp_, sg, rg, loc, locm, ready,
):
    row, col, samp = place()
    core = rmod(row, 2)
    zlo = row // 2
    mate = (row + 1 - 2 * core, col, samp)
    far = (row, col, 1 - samp)
    barrier = pltpu.get_barrier_semaphore()

    loads = [
        pltpu.make_async_copy(s, d, loc.at[18 + i])
        for i, (s, d) in enumerate(
            [
                (pair_hbm, pair_in), (relpos_hbm, relpos_ref), (tri_hbm, tri_w),
                (single_hbm, single_ref), (qkvw_hbm, qkvw_ref), (ada_hbm, ada_w),
                (noisy_hbm, noisy), (cot_hbm, cot_ref), (triout_hbm, triout_ref),
                (biasp_hbm, biasp_ref), (outp_hbm, outp_ref),
            ]
        )
    ]
    for copy in loads:
        copy.start()
    for oz, cx in ROW_IDS:
        signal(barrier, row_source(oz, cx))

    def greet(o, _):
        signal(barrier, (row, rmod(col + o, NCOL), samp))
        return 0

    def greet_row(o, _):
        signal(barrier, (rmod(row + o, NROW), col, samp))
        return 0

    lax.fori_loop(1, NCOL, greet, 0)
    lax.fori_loop(1, NROW, greet_row, 0)
    signal(barrier, far)

    low = lax.broadcasted_iota(jnp.int32, (64, 128), 1) < 64
    low16 = lax.broadcasted_iota(jnp.int32, (16, 128), 1) < 64
    low1 = lax.broadcasted_iota(jnp.int32, (1, 128), 1) < 64
    diag = (lax.broadcasted_iota(jnp.int32, (128, 128), 0) < 64) == (
        lax.broadcasted_iota(jnp.int32, (128, 128), 1) < 64
    )

    def blockdiag(x):
        return jnp.where(diag, jnp.concatenate([x, x], 0), 0.0).astype(BF16)

    def indices(i, _):
        at = pl.ds(i, 1)
        idx_r[0, at, :] = jnp.full((1, 128), res_ref[row * 64 + i], jnp.int32)
        idx_r[1, at, :] = jnp.full((1, 128), chain_ref[row * 64 + i], jnp.int32)
        m = jnp.full((1, 128), mask_ref[row * 64 + i].astype(F32), F32)
        mrow[at, :] = m
        mrow[pl.ds(64 + i, 1), :] = m
        return 0

    lax.fori_loop(0, 64, indices, 0, unroll=4)
    mrow[...] = mrow[...].T
    relpos_w[...] = jnp.zeros_like(relpos_w)
    loads[1].wait()
    relpos_w[0:REL_BINS, :] = relpos_ref[...]
    loads[0].wait()

    def load(i, _):
        pf[pl.ds(i * 32, 32), :] = pair_in[i].astype(F32)
        return 0

    lax.fori_loop(0, 64, load, 0, unroll=4)
    bins = lax.broadcasted_iota(jnp.int32, (64, 128), 1)

    def normed_rows(t, _):
        parts = []
        for q in range(2):
            for hi in range(2):
                j = 2 * t + q + 16 * hi
                off = jnp.clip(idx_r[0] - res_ref[col * 32 + j] + 32, 0, 64)
                bucket = jnp.where(idx_r[1] == chain_ref[col * 32 + j], off, REL_BINS - 1)
                onehot = jnp.where(bucket == bins, 1.0, 0.0).astype(BF16)
                parts.append(
                    pf[pl.ds(j, 64, stride=32), :]
                    + jnp.dot(onehot, relpos_w[...], preferred_element_type=F32)
                )
        for q in range(2):
            for hi in range(2):
                pf[pl.ds(2 * t + q + 16 * hi, 64, stride=32), :] = parts[2 * q + hi]
        at = pl.ds(pl.multiple_of(t * 256, 256), 256)
        zl_s[at, :] = layer_norm(jnp.concatenate(parts, 0), -1).astype(BF16)
        return 0

    lax.fori_loop(0, 8, normed_rows, 0, unroll=2)
    loads[2].wait()
    tri_t[...] = tri_w[:, :512].astype(F32).T.astype(BF16)

    def project(h, t):
        at = pl.ds(pl.multiple_of(t * 256, 256), 256)
        pt = dg(tri_t[h * 256 : h * 256 + 256, :], zl_s[at, :], 1, 1)
        val = sigmoid(pt[128:]) * pt[:128]
        for q in range(2):
            lo = 2 * t + q
            mask = mrow[0:1, :] * jnp.where(
                low1, mask_ref[col * 32 + lo].astype(F32), mask_ref[col * 32 + 16 + lo].astype(F32)
            )
            lrf[pl.ds(h * 2048 + lo, 128, stride=16), :] = val[:, q * 128 : q * 128 + 128] * mask

    pieces = [(0, slice(0, 8)), (1, slice(0, 4)), (1, slice(4, 8))]
    a_src = [lambda to, h=h, p=p: lbuf.at[h, to, p] for h, p in pieces]
    a_slot = [lambda c, h=h, p=p: recv_a.at[h, c, p] for h, p in pieces]
    b_src = [lambda r, h=h: recv_a.at[h, :, spot(r)] for h in range(2)]
    b_slot = [lambda r, h=h: got.at[h, r] for h in range(2)]
    own_a = [pltpu.make_async_copy(lbuf.at[h, col], recv_a.at[h, col], loc.at[h]) for h in range(2)]
    own_b = [
        pltpu.make_async_copy(recv_a.at[h, :, spot(row)], got.at[h, row], loc.at[2 + h])
        for h in range(2)
    ]
    for h in range(2):

        def one_side(t, _):
            project(h, t)
            return 0

        lax.fori_loop(0, 8, one_side, 0, unroll=2)

        def pack(c, _):
            lbuf[h, c] = lrf[pl.ds(h * 2048 + c * 128, 128), :].astype(BF16).reshape(8, 16, 128)
            return 0

        lax.fori_loop(0, 16, pack, 0, unroll=2)
        if h == 0:
            pl.semaphore_wait(barrier, 7 + 15 + 7 + 1)
            signal(ready, far)
        own_a[h].start()
        for i in ((0,), (1, 2))[h]:
            col_start(a_src[i], a_slot[i], sa.at[i], ra.at[i])

    for copy in loads[3:6]:
        copy.wait()
    cvec = layer_norm(single_ref[...].astype(F32), -1).astype(BF16)
    cvec_s[...] = cvec
    wqkv[...] = jnp.zeros_like(wqkv)
    for p in range(3):
        wqkv[p * 64 : p * 64 + 48, :] = qkvw_ref[p]
    scale_s[...] = sigmoid(jnp.dot(cvec, ada_w[:, :768], preferred_element_type=F32))
    shift_s[...] = jnp.dot(cvec, ada_w[:, 768:1536], preferred_element_type=F32)
    for copy in loads[6:]:
        copy.wait()

    def sample(s, _):
        at = pl.ds(pl.multiple_of(s * 64, 64), 64)
        n = layer_norm(noisy[at, :].astype(F32), -1)
        normed[at, :] = n
        hidden[at, :] = (scale_s[...] * n + shift_s[...]).astype(BF16)
        return 0

    lax.fori_loop(0, 8, sample, 0)
    own_a[0].wait()
    take(recv_a.at[0, 0:15], sa.at[0], ra.at[0])
    own_b[0].start()
    row_start(b_src[0], b_slot[0], sb.at[0], rb.at[0])

    feat = lax.broadcasted_iota(jnp.int32, (768, 64), 1)
    sel = jnp.where(
        (lax.broadcasted_iota(jnp.int32, (768, 64), 0) == col * 48 + feat) & (feat < 48), 1.0, 0.0
    ).astype(BF16)
    wg_s[...] = jnp.dot(ada_w[:, 1536:], sel, preferred_element_type=F32).astype(BF16)
    gate_t[...] = sigmoid(
        dg(wg_s[...], jnp.concatenate([cvec_s[...], cvec_s[...]], 0), 0, 1)
    )
    lane = lax.broadcasted_iota(jnp.int32, (64, 128), 1)
    tok = lax.broadcasted_iota(jnp.int32, (64, 128), 0)
    put = [jnp.where(lane == tok + 64 * h, 1.0, 0.0).astype(BF16) for h in range(2)]
    for u in range(4):
        g = jnp.dot(cot_ref[2 * u], put[0], preferred_element_type=F32) + jnp.dot(
            cot_ref[2 * u + 1], put[1], preferred_element_type=F32
        )
        g_t[u] = g
        dmx_own[:, u * 128 : u * 128 + 128] = (g * gate_t[:48, :]).astype(BF16)
    dm_src, dm_slot = (lambda to: dmx_own), (lambda c: dmx_all.at[c])
    dm_keep = pltpu.make_async_copy(dmx_own, dmx_all.at[col], loc.at[5])
    dm_keep.start()
    col_start(dm_src, dm_slot, sdm.at[0], rdm.at[0])
    kv_f[...] = dg(hidden[...], wqkv[64:, :], 1, 1)

    def kv_pack(t, _):
        r0 = kv_f[pl.ds(t * 32, 16), :]
        r1 = kv_f[pl.ds(t * 32 + 16, 16), :]
        to = pl.ds(pl.multiple_of(rmod(t, 2) * 16, 16), 16)
        kv_own[0, t // 2, to, :] = jnp.where(low16, r0, pltpu.roll(r1, 64, 1)).astype(BF16)
        kv_own[1, t // 2, to, :] = jnp.where(low16, pltpu.roll(r0, 64, 1), r1).astype(BF16)
        return 0

    lax.fori_loop(0, 16, kv_pack, 0, unroll=2)
    kv_keep = pltpu.make_async_copy(kv_own, kv_all.at[row], loc.at[4])
    kv_keep.start()
    kv_out = []
    for w in range(2):
        kv_out.append(remote(kv_own.at[w], kv_all.at[row, w], skf.at[w, 0], rkf.at[w, 0], mate))
        for o in range(1, 4):
            to = (rmod(zlo + o, 4) * 2 + core, col, samp)
            kv_out.append(
                remote(kv_own.at[w], kv_all.at[row, w], skv.at[w, o], rkv.at[w, o], to)
            )
    own_a[1].wait()
    for k in range(2):
        take(recv_a.at[1, 0:15, 0:4], sa.at[1 + k], ra.at[1 + k])
        cx = rmod(core + k, 2)
        for oz in (2, 1, 3):
            to = row_dest(oz, cx)
            remote(b_src[1](to[0]), b_slot[1](row), sb.at[1], rb.at[1], to).start()

        @pl.when(cx == 1)
        def _():
            remote(b_src[1](mate[0]), b_slot[1](row), sb.at[1], rb.at[1], mate).start()

    own_b[1].start()

    def gates(t, _):
        at = pl.ds(pl.multiple_of(t * 256, 256), 256)
        gate[at, :] = sigmoid(
            jnp.dot(zl_s[at, :], tri_w[:, 512:], preferred_element_type=F32)
        )
        return 0

    lax.fori_loop(0, 8, gates, 0)
    for h in (1, 0):
        own_b[h].wait()
        take(got.at[h, 0:7], sb.at[h], rb.at[h])

    def turn(r, _):
        x = got[1, r].reshape(256, 128).astype(F32).T.astype(BF16)
        at = pl.ds(pl.multiple_of(r * 64, 64), 64)
        rcat[at, 0:256] = x[:64]
        rcat[at, 256:512] = x[64:]
        return 0

    lax.fori_loop(0, 8, turn, 0, unroll=2)
    low256 = lax.broadcasted_iota(jnp.int32, (256, 128), 1) < 64
    turns = ((2, 1), (3, 0))
    for i, pair in enumerate(turns):
        for k, oz in enumerate(pair):
            z = rmod(zlo + oz, 4)
            la = got[0, 2 * z].reshape(256, 128).astype(F32)
            lb = got[0, 2 * z + 1].reshape(256, 128).astype(F32)
            lanes = slice(k * 128, k * 128 + 128)
            lcat[i, 0:256, lanes] = jnp.where(low256, la, pltpu.roll(lb, 64, 1)).astype(BF16)
            lcat[i, 256:512, lanes] = jnp.where(low256, pltpu.roll(la, 64, 1), lb).astype(BF16)
    c_src = [lambda r, p=p: tbuf.at[r, p] for p in (slice(0, 8), slice(8, 16))]
    c_slot = [lambda r, p=p: got_c.at[spot(r), p] for p in (slice(0, 8), slice(8, 16))]
    own_c = [
        pltpu.make_async_copy(c_src[h](row), c_slot[h](row), loc.at[6 + 3 * h]) for h in range(2)
    ]

    def tri(i, part):
        mtmp[...] = jnp.dot(
            rcat[part * 256 : part * 256 + 256, :], lcat[i], preferred_element_type=F32
        )

        def out(rj, _):
            for k, oz in enumerate(turns[i]):
                z = rmod(zlo + oz, 4)
                for jh in range(2):
                    at = rj * 64 + jh * 32
                    a = mtmp[pl.ds(at, 16), k * 128 : k * 128 + 128]
                    b = mtmp[pl.ds(at + 16, 16), k * 128 : k * 128 + 128]
                    even_row = jnp.where(low16, a, pltpu.roll(b, 64, 1))
                    odd_row = jnp.where(low16, pltpu.roll(a, 64, 1), b)
                    tbuf[2 * z, part * 8 + 2 * rj + jh] = even_row.astype(BF16)
                    tbuf[2 * z + 1, part * 8 + 2 * rj + jh] = odd_row.astype(BF16)
            return 0

        lax.fori_loop(0, 4, out, 0, unroll=2)

    for part in range(2):
        for i, pair in enumerate(turns):
            tri(i, part)
            for oz in pair:
                for cx in range(2):
                    if (oz, cx) != (0, 0):
                        to = row_dest(oz, cx)
                        remote(
                            c_src[part](to[0]), c_slot[part](row), sc.at[part], rc.at[part], to
                        ).start()
        own_c[part].start()
    for copy in kv_out:
        copy.start()
    d_own = pltpu.make_async_copy(got_c.at[:, col], got_d.at[col], loc.at[7])

    def d_start(part):
        def one(o, _):
            to = part * 8 + rmod(col + o, 8)

            @pl.when(to != col)
            def _():
                remote(got_c.at[:, to], got_d.at[col], sd.at[0], rd.at[0], (row, to, samp)).start()

            return 0

        lax.fori_loop(0, 8, one, 0)

    dm_keep.wait()
    take(dmx_all.at[0:15], sdm.at[0], rdm.at[0])
    da_t[...] = jnp.zeros_like(da_t)
    da_t[:48, :] = (
        jnp.dot(outp_ref[...], dmx_all[...].reshape(768, 512), preferred_element_type=F32)
        .astype(BF16)
        .astype(F32)
    )
    for part in range(2):
        own_c[part].wait()
        take(got_c.at[0:7, 0:8], sc.at[part], rc.at[part])
        d_start(part)
    d_own.start()

    q_t[...] = dg(wqkv[:64, :], hidden[...], 1, 1)
    noisy_t[...] = dg(sel, noisy[...], 0, 1)

    def key_mask(t, _):
        jb, lo = t // 16, rmod(t, 16)
        keyok[pl.ds(t, 1), :] = jnp.where(
            low1,
            mask_ref[jb * 32 + lo].astype(F32),
            mask_ref[jb * 32 + 16 + lo].astype(F32),
        )
        return 0

    lax.fori_loop(0, 256, key_mask, 0, unroll=4)

    def pass_keys(w):
        for o in range(1, 4):
            came = rmod(zlo + 4 - o, 4) * 2 + core
            remote(
                kv_own.at[w], kv_all.at[came, w], skv.at[w, o], rkv.at[w, o], mate
            ).wait_recv()
            remote(
                kv_all.at[came, w], kv_all.at[came, w], skf.at[w, o], rkf.at[w, o], mate
            ).start()

    def keys_passed(w):
        for o in range(4):
            came = rmod(zlo + 4 - o, 4) * 2
            remote(
                kv_all.at[came + core, w], kv_all.at[came + 1 - core, w], skf.at[w, o],
                rkf.at[w, o], mate,
            ).wait_recv()
            if o > 0:
                remote(
                    kv_all.at[came + core, w], kv_all.at[came + core, w], skf.at[w, o],
                    rkf.at[w, o], mate,
                ).wait_send()

    def half_of(ref, u, sh):
        tile = ref[:, pl.ds(pl.multiple_of(u * 128, 128), 128)].astype(F32)
        return blockdiag(both(tile, low, sh == 0))

    def keys(which, s):
        return jnp.concatenate([kv_all[r, which, s] for r in range(NROW)], 0)

    def raw(w):
        def one(u, _):
            for sh in range(2):
                s = 2 * u + sh
                (sraw, draw)[w][s] = jnp.dot(
                    keys(w, s), half_of((q_t, da_t)[w], u, sh), preferred_element_type=F32
                )
            return 0

        lax.fori_loop(0, 4, one, 0)

    d_own.wait()
    take(got_d.at[0:15], sd.at[0], rd.at[0])

    def widen(c, _):
        lrf[pl.ds(c * 128, 128), :] = got_d[c].reshape(128, 128).astype(F32)
        return 0

    lax.fori_loop(0, 16, widen, 0)

    def stage3(t, _):
        tn = layer_norm(
            jnp.concatenate([lrf[pl.ds(2 * t + q, 128, stride=16), :] for q in range(2)], 1), 0
        ).astype(BF16)
        upd = dg(tn, triout_ref[...], 0, 0) * gate[pl.ds(pl.multiple_of(t * 256, 256), 256), :]
        spots = [pl.ds(2 * t + q + 16 * hi, 64, stride=32) for q in range(2) for hi in range(2)]
        outs = [
            (pf[at, :] + upd[i * 64 : i * 64 + 64]).astype(BF16) for i, at in enumerate(spots)
        ]
        for at, val in zip(spots, outs):
            pf[at, :] = val.astype(F32)
        tile = dg(biasp_ref[...], jnp.concatenate(outs, 0), 1, 1)
        for q in range(2):
            bias_f[pl.ds(2 * t + q, 16, stride=16), :] = tile[:, q * 128 : q * 128 + 128]
        return 0

    lax.fori_loop(0, 8, stage3, 0, unroll=4)
    bias_b[...] = bias_f[...].astype(BF16).reshape(16, 16, 128)
    e_src, e_slot = (lambda c: bias_b.at[c]), (lambda c: bias_got.at[c])
    own_e = pltpu.make_async_copy(bias_b.at[col], bias_got.at[col], loc.at[8])
    own_e.start()
    col_start(e_src, e_slot, se.at[0], re.at[0])

    kv_keep.wait()
    pass_keys(0)

    def store(i, _):
        pairout_ref[i] = pf[pl.ds(i * 32, 32), :].astype(BF16)
        return 0

    lax.fori_loop(0, 64, store, 0, unroll=4)
    out_pair = pltpu.make_async_copy(pairout_ref, pairout_hbm, loc.at[14])
    out_pair.start()
    keys_passed(0)
    raw(0)
    pass_keys(1)
    for copy in kv_out:
        copy.wait_send()
    keys_passed(1)
    raw(1)
    dbias[...] = jnp.zeros_like(dbias)
    own_e.wait()
    take(bias_got.at[0:15], se.at[0], re.at[0])

    scale = 1.0 / HEAD_DIM**0.5

    def mix_src(u):
        return lambda f: mix_s.at[u, f]

    def mix_slot(u):
        return lambda h: mix_r.at[u, h]

    def to_mate(u):
        return remote(dkv_s.at[:, 1 - core, u], dkv_m.at[u], sk.at[u], rk.at[u], mate)

    def to_chip(u, o):
        z = rmod(zlo + o, 4)
        return remote(
            dkv_o.at[u, z], dkv_r.at[u, zlo], sko.at[u, o], rko.at[u, o], (z * 2 + core, col, samp)
        )

    def pass_on(u):
        to_mate(u).wait_recv()
        for z in range(4):
            dkv_o[u, z] = (
                dkv_s[z, core, u].astype(F32) + dkv_m[u, z].astype(F32)
            ).astype(BF16)
        for o in range(1, 4):
            to_chip(u, o).start()

    def pair_of_samples(u, _):
        folded, dqs = [], []
        for sh in range(2):
            s = 2 * u + sh
            kp, vp = keys(0, s), keys(1, s)
            qq, dd = half_of(q_t, u, sh), half_of(da_t, u, sh)
            sco = sraw[s] * scale + bias_got[...].reshape(256, 128).astype(F32)
            sco = jnp.where(keyok[...] > 0, sco, -1000000000.0)
            top = jnp.max(sco, 0, keepdims=True)
            top = jnp.maximum(top, pltpu.roll(top, 64, 1))
            ex = jnp.exp(sco - top)
            tot = jnp.sum(ex, 0, keepdims=True)
            probs = ex * (1.0 / (tot + pltpu.roll(tot, 64, 1)))
            pb = probs.astype(BF16)
            folded.append(dg(vp, pb, 0, 0))
            dp = draw[s]
            dot = jnp.sum(probs * dp, 0, keepdims=True)
            ds = probs * (dp - (dot + pltpu.roll(dot, 64, 1)))
            dbias[...] += ds
            dsb = (ds * scale).astype(BF16)
            dqs.append(dg(kp, dsb, 0, 0))
            dk = dg(dsb, qq, 1, 1).astype(BF16)
            dv = dg(pb, dd, 1, 1).astype(BF16)
            for r in range(NROW):
                dkv_s[r // 2, r % 2, u, sh] = dk[r * 32 : r * 32 + 32]
                dkv_s[r // 2, r % 2, u, 2 + sh] = dv[r * 32 : r * 32 + 32]

        def fold(m0, m1):
            return jnp.where(
                low,
                m0[:64] + pltpu.roll(m0[64:], 64, 1),
                pltpu.roll(m1[:64], 64, 1) + m1[64:],
            ).astype(BF16)

        att = fold(*folded)
        dq_t[u] = fold(*dqs)
        mix_s[u] = dg(outp_ref[...], att[:48], 0, 0).astype(BF16).reshape(16, 48, 128)
        pltpu.make_async_copy(mix_s.at[u, col], mix_r.at[u, col], locm.at[u]).start()
        to_mate(u).start()
        col_start(mix_src(u), mix_slot(u), sm.at[u], rm.at[u])

        @pl.when(u > 0)
        def _():
            pass_on(u - 1)

        return 0

    lax.fori_loop(0, 4, pair_of_samples, 0)

    db_s[...] = dbias[...].astype(BF16).reshape(16, 16, 128)
    own_db = pltpu.make_async_copy(db_s.at[col], db_r.at[samp, col], loc.at[29])
    own_db.start()

    def db_copy(o):
        to = rmod(col + o, NCOL)
        return remote(
            db_s.at[to], db_r.at[samp, col], sbb.at[1], rbb.at[1], (row, to, 1 - samp)
        )

    def db_send(o, _):
        db_copy(o).start()
        return 0

    pass_on(3)
    pl.semaphore_wait(ready, 1)
    lax.fori_loop(0, NCOL, db_send, 0)
    near_src, near_slot = (lambda c: db_s.at[c]), (lambda c: db_r.at[samp, c])
    col_start(near_src, near_slot, sbb.at[0], rbb.at[0])

    dga[...] = jnp.zeros_like(dga)

    def mixed_of(u, _):
        pltpu.make_async_copy(mix_s.at[u, col], mix_r.at[u, col], locm.at[u]).wait()
        take(mix_r.at[u, 0:15], sm.at[u], rm.at[u])
        total = mix_r[u, 0].astype(F32)
        for h in range(1, NCOL):
            total = total + mix_r[u, h].astype(F32)
        lanes = pl.ds(pl.multiple_of(u * 128, 128), 128)
        out = noisy_t[:48, lanes] + gate_t[:48, :] * total
        block_ref[2 * u] = out[:, :64].astype(BF16)
        block_ref[2 * u + 1] = pltpu.roll(out, 64, 1)[:, :64].astype(BF16)
        dga[:48, :] += g_t[u] * total
        return 0

    lax.fori_loop(0, 3, mixed_of, 0)

    dsc[...] = jnp.zeros_like(dsc)
    dsh[...] = jnp.zeros_like(dsh)

    def hidden_grad(u, _):
        to_mate(u).wait_send()
        for o in range(1, 4):
            came = rmod(zlo + 4 - o, 4)
            remote(
                dkv_o.at[u, came], dkv_r.at[u, came], sko.at[u, o], rko.at[u, o], mate
            ).wait_recv()
            to_chip(u, o).wait_send()
        dkv_r[u, zlo] = dkv_o[u, zlo]
        tot = dkv_r[u, 0].astype(F32)
        for z in range(1, 4):
            tot = tot + dkv_r[u, z].astype(F32)
        for sh in range(2):
            for jb in range(2):
                a = tot[sh, jb * 16 : jb * 16 + 16]
                b = tot[2 + sh, jb * 16 : jb * 16 + 16]
                base = sh * 64 + jb * 32
                dkv_tok[base : base + 16, :] = jnp.where(low16, a, pltpu.roll(b, 64, 1)).astype(BF16)
                dkv_tok[base + 16 : base + 32, :] = jnp.where(
                    low16, pltpu.roll(a, 64, 1), b
                ).astype(BF16)
        dh = dg(dq_t[u], wqkv[:64, :], 0, 0) + jnp.dot(
            dkv_tok[...], wqkv[64:, :], preferred_element_type=F32
        )
        n = normed[pl.ds(pl.multiple_of(u * 128, 128), 128), :]
        w = dh * n
        dsc[...] += w[:64] + w[64:]
        dsh[...] += dh[:64] + dh[64:]
        return 0

    lax.fori_loop(0, 3, hidden_grad, 0)
    mixed_of(3, 0)
    out_block = pltpu.make_async_copy(block_ref, block_hbm, loc.at[15])
    out_block.start()
    hidden_grad(3, 0)
    sg_ = scale_s[...]
    part = dg(two_parts(dsc[...] * sg_ * (1.0 - sg_)), ada_w[:, :768], 1, 1)
    part = part + dg(two_parts(dsh[...]), ada_w[:, 768:1536], 1, 1)
    part = part[:64] + part[64:]
    acc = dga[...]
    acc = (acc + pltpu.roll(acc, 64, 1)) * gate_t[...] * (1.0 - gate_t[...])
    coarse = acc.astype(BF16)
    fine = (acc - coarse.astype(F32)).astype(BF16)
    part = part + (dg(coarse, wg_s[...], 0, 1) + dg(fine, wg_s[...], 0, 1))[:64]
    dc_s[...] = part.reshape(8, 8, 384)

    half_col = col // 2
    even = rmod(col, 2) == 0

    def part_copy(o):
        g = rmod(half_col + o, 8)
        return remote(dc_s.at[g], dc_r.at[col], st.at[0], rt.at[0], (row, 2 * g, samp))

    @pl.when(jnp.logical_not(even))
    def _():
        part_copy(0).start()

    def part_send(o, _):
        part_copy(o).start()
        return 0

    lax.fori_loop(1, 8, part_send, 0)

    own_db.wait()
    take(db_r.at[0, 0:15], sbb.at[0], rbb.at[0])
    take(db_r.at[0], sbb.at[1], rbb.at[1])
    dbias[...] = (db_r[0].astype(F32) + db_r[1].astype(F32)).reshape(256, 128)
    biasp3 = jnp.concatenate([biasp_ref[...]] * 3, 0)

    def grad(lo, _):
        d = dbias[pl.ds(lo, 16, stride=16), :]
        d1 = d.astype(BF16)
        rest = d - d1.astype(F32)
        d2 = rest.astype(BF16)
        d3 = (rest - d2.astype(F32)).astype(BF16)
        g = dg(jnp.concatenate([d1, d2, d3], 0), biasp3, 0, 0)
        for hi in range(2):
            gpair_ref[pl.ds(lo + 16 * hi, 64, stride=32), :] = g[hi * 64 : hi * 64 + 64]
        return 0

    lax.fori_loop(0, 16, grad, 0, unroll=2)
    out_grad = pltpu.make_async_copy(gpair_ref, gpair_hbm, loc.at[16])
    out_grad.start()

    def own_copy(o):
        return remote(
            gs_own, gs_all.at[half_col], sg.at[0], rg.at[0], (row, rmod(col + o, NCOL), samp)
        )

    @pl.when(even)
    def _():
        dc_r[col] = dc_s[half_col]

        take(dc_r.at[0:15], rt.at[0])
        tot = dc_r[0]
        for c in range(1, NCOL):
            tot = tot + dc_r[c]
        dc_p[samp] = tot
        other = remote(dc_p.at[samp], dc_p.at[samp], sp.at[0], rp_.at[0], far)
        other.start()
        own = single_ref[...].astype(F32).reshape(8, 8, 384)
        mine = jnp.zeros((8, 384), F32)
        for g in range(8):
            mine = mine + jnp.where(half_col == g, own[g], 0.0)
        mean = jnp.mean(mine, -1, keepdims=True)
        cent = mine - mean
        inv = lax.rsqrt(jnp.mean(cent * cent, -1, keepdims=True) + EPSILON)
        unit = cent * inv
        remote(dc_p.at[samp], dc_p.at[1 - samp], sp.at[0], rp_.at[0], far).wait_recv()
        other.wait_send()
        up = dc_p[0] + dc_p[1]
        gs_own[...] = inv * (
            up - jnp.mean(up, -1, keepdims=True) - unit * jnp.mean(up * unit, -1, keepdims=True)
        )

        def tell(o, _):
            own_copy(o).start()
            return 0

        lax.fori_loop(1, NCOL, tell, 0)
        gs_all[half_col] = gs_own[...]

    @pl.when(even)
    def _():
        take(dc_s.at[0:7], st.at[0])
        take(dc_r.at[0:15], sg.at[0])
        take(gs_all.at[0:7], rg.at[0])

    @pl.when(jnp.logical_not(even))
    def _():
        take(dc_s, st.at[0])
        take(gs_all, rg.at[0])

    out_single = pltpu.make_async_copy(gs_all, gsingle_hbm, loc.at[17])
    out_single.start()
    for copy in (out_pair, out_block, out_grad, out_single):
        copy.wait()


def finish_kernel(*refs):
    n = 4
    ins, outs, bufs = refs[:n], refs[n : 2 * n], refs[2 * n : 3 * n]
    got, put = refs[3 * n], refs[3 * n + 1]
    reads = [pltpu.make_async_copy(ins[i], bufs[i], got.at[i]) for i in range(n)]
    writes = [pltpu.make_async_copy(bufs[i], outs[i], put.at[i]) for i in range(n)]
    for copy in reads:
        copy.start()
    for i in (3, 1, 0, 2):
        reads[i].wait()
        writes[i].start()
    for copy in writes:
        copy.wait()


def finished(arrays):
    hbm = pl.BlockSpec(memory_space=pl.ANY)
    return pl.pallas_call(
        finish_kernel,
        out_shape=[jax.ShapeDtypeStruct(x.shape, x.dtype) for x in arrays],
        in_specs=[hbm] * 4,
        out_specs=[hbm] * 4,
        scratch_shapes=[pltpu.VMEM(x.shape, x.dtype) for x in arrays]
        + [pltpu.SemaphoreType.DMA((4,)), pltpu.SemaphoreType.DMA((4,))],
        compiler_params=pltpu.CompilerParams(vmem_limit_bytes=60 * 1024 * 1024),
        name="finish",
    )(*arrays)


def on_device(
    pair_in, residue_index, chain_index, token_mask, relpos_weight, tri_proj, tri_out, bias_proj,
    single, ada_proj, noisy, qkv_proj, out_proj, cotangent,
):
    sm = pl.BlockSpec(memory_space=pltpu.SMEM)
    hbm = pl.BlockSpec(memory_space=pl.ANY)
    dma = pltpu.SemaphoreType.DMA
    v = pltpu.VMEM
    pair_out, block_t, grad_pair, grad_single = pl.pallas_call(
        step_kernel,
        out_shape=(
            jax.ShapeDtypeStruct((64, 32, 128), BF16),
            jax.ShapeDtypeStruct((8, 48, 64), BF16),
            jax.ShapeDtypeStruct((2048, 128), F32),
            jax.ShapeDtypeStruct((8, 8, 384), F32),
        ),
        in_specs=[sm] * 3 + [hbm] * 11,
        out_specs=(hbm,) * 4,
        scratch_shapes=[
            v((64, 32, 128), BF16), v((8, 48, 64), BF16), v((2048, 128), F32),
            v((64, 32, 128), BF16), v((128, 640), BF16), v((384, 2304), BF16), v((512, 768), BF16),
            v((REL_BINS, 128), BF16), v((128, 128), BF16), v((16, 128), BF16), v((64, 384), BF16),
            v((3, 48, 768), BF16), v((48, 768), BF16), v((8, 48, 64), BF16),
            v((2, 64, 128), jnp.int32), v((128, 128), F32), v((128, 128), BF16),
            v((2048, 128), BF16), v((512, 128), BF16), v((2048, 128), F32), v((2048, 128), F32),
            v((4096, 128), F32),
            v((2, 16, 8, 16, 128), BF16), v((2, 16, 8, 16, 128), BF16),
            v((2, 8, 16, 16, 128), BF16), v((512, 512), BF16), v((2, 512, 256), BF16),
            v((256, 256), F32),
            v((8, 16, 16, 128), BF16), v((8, 16, 16, 128), BF16), v((16, 8, 16, 128), BF16),
            v((256, 128), F32), v((16, 16, 128), BF16), v((16, 16, 128), BF16),
            v((64, 384), BF16), v((64, 768), F32), v((64, 768), F32), v((384, 64), BF16),
            v((64, 128), F32), v((4, 48, 128), F32), v((64, 512), F32), v((512, 768), F32),
            v((512, 768), BF16), v((192, 768), BF16), v((64, 512), F32), v((512, 128), F32),
            v((2, 8, 32, 128), BF16), v((8, 2, 8, 32, 128), BF16), v((48, 512), BF16),
            v((16, 48, 512), BF16), v((64, 512), F32), v((256, 128), F32), v((8, 256, 128), F32),
            v((8, 256, 128), F32),
            v((4, 16, 48, 128), BF16), v((4, 16, 48, 128), BF16), v((4, 2, 4, 4, 32, 128), BF16),
            v((4, 4, 4, 32, 128), BF16), v((4, 4, 4, 32, 128), BF16), v((4, 4, 4, 32, 128), BF16),
            v((4, 64, 128), BF16), v((128, 128), BF16), v((256, 128), F32), v((16, 16, 128), BF16),
            v((2, 16, 16, 128), BF16),
            v((64, 768), F32), v((64, 768), F32), v((64, 128), F32), v((8, 8, 384), F32),
            v((16, 8, 384), F32), v((2, 8, 384), F32), v((8, 384), F32), v((8, 8, 384), F32),
            dma((3,)), dma((3,)), dma((2,)), dma((2,)), dma((2,)), dma((2,)),
            dma((1,)), dma((1,)), dma((1,)), dma((1,)), dma((2, 4)), dma((2, 4)),
            dma((2, 4)), dma((2, 4)), dma((1,)), dma((1,)),
            dma((4,)), dma((4,)), dma((4,)), dma((4,)), dma((4, 4)), dma((4, 4)),
            dma((2,)), dma((2,)), dma((1,)), dma((1,)), dma((1,)), dma((1,)),
            dma((1,)), dma((1,)), dma((30,)), dma((4,)), pltpu.SemaphoreType.REGULAR,
        ],
        compiler_params=pltpu.CompilerParams(
            collective_id=1, has_side_effects=True, vmem_limit_bytes=60 * 1024 * 1024
        ),
        name="step",
    )(
        residue_index, chain_index, token_mask, pair_in, relpos_weight, tri_proj, tri_out,
        bias_proj.T, single, ada_proj, noisy.reshape(512, 768), qkv_proj.transpose(1, 2, 0),
        out_proj, cotangent.transpose(0, 2, 1),
    )
    pair_out, block_t, grad_pair, grad_single = finished(
        (pair_out, block_t, grad_pair, grad_single)
    )
    return (
        pair_out,
        block_t.transpose(0, 2, 1),
        grad_pair.reshape(64, 32, 128),
        grad_single.reshape(64, 384),
    )


def solution(mesh):
    return jax.shard_map(
        on_device,
        mesh=mesh,
        in_specs=(
            P("row", "col", None), P(), P(), P(), P(), P(), P(), P(), P("row", None), P(),
            P("samp", "row", None), P(None, None, "col"), P("col", None), P("samp", "row", "col"),
        ),
        out_specs=(
            P("row", "col", None), P("samp", "row", "col"), P("row", "col", None), P("row", None),
        ),
        check_vma=False,
    )
```

```python
import jax
import jax.numpy as jnp
from jax import lax
from jax.experimental import pallas as pl
from jax.experimental.pallas import tpu as pltpu
from jax.sharding import PartitionSpec as P

HEAD_DIM = 48
REL_BINS = 66
EPSILON = 1e-05
MESH = pl.DeviceIdType.MESH
F32 = jnp.float32
BF16 = jnp.bfloat16
NCOL = 16
NROW = 8


def dg(a, b, ca, cb, **kw):
    return lax.dot_general(a, b, (((ca,), (cb,)), ((), ())), preferred_element_type=F32, **kw)


def place():
    return lax.axis_index("row"), lax.axis_index("col"), lax.axis_index("samp")


def rmod(a, n):
    return lax.rem(a, n)


def ring_shift(oz, from_core):
    if oz == 2:
        return 2 + 4 * from_core
    return (0, 1, None, 7)[oz]


def row_dest(oz, cx):
    row, col, samp = place()
    z, core = samp * 4 + row // 2, rmod(row, 2)
    to_core = rmod(core + cx, 2)
    to_z = rmod(z + ring_shift(oz, core), 8)
    return rmod(to_z, 4) * 2 + to_core, col, to_z // 4


def row_source(oz, cx):
    row, col, samp = place()
    z, core = samp * 4 + row // 2, rmod(row, 2)
    from_core = rmod(core + cx, 2)
    from_z = rmod(z + 8 - ring_shift(oz, from_core), 8)
    return rmod(from_z, 4) * 2 + from_core, col, from_z // 4


def spot(row):
    return rmod(row, 2) * 4 + row // 2


ROW_IDS = [(oz, cx) for oz in range(4) for cx in range(2) if (oz, cx) != (0, 0)]


def remote(src, dst, ssem, rsem, to):
    return pltpu.make_async_remote_copy(
        src_ref=src, dst_ref=dst, send_sem=ssem, recv_sem=rsem, device_id=to, device_id_type=MESH
    )


def col_start(src_of, slot_of, ssem, rsem):
    row, col, samp = place()

    def one(o, _):
        to = rmod(col + o, NCOL)
        remote(src_of(to), slot_of(col), ssem, rsem, (row, to, samp)).start()
        return 0

    lax.fori_loop(1, NCOL, one, 0)


def take(region, *sems):
    for sem in sems:
        pltpu.make_async_copy(region, region, sem).wait()


def row_start(src_of, slot_of, ssem, rsem):
    row = lax.axis_index("row")
    for oz, cx in ROW_IDS:
        to = row_dest(oz, cx)
        remote(src_of(to[0]), slot_of(row), ssem, rsem, to).start()


def signal(sem, to):
    pl.semaphore_signal(sem, inc=1, device_id=to, device_id_type=MESH)


def both(x, low, first):
    turned = pltpu.roll(x, 64, 1)
    return jnp.where(low, x, turned) if first else jnp.where(low, turned, x)


def sigmoid(x):
    return 0.5 * jnp.tanh(0.5 * x) + 0.5


def layer_norm(x, axis):
    mean = jnp.mean(x, axis, keepdims=True)
    cent = x - mean
    var = jnp.mean(cent * cent, axis, keepdims=True)
    return cent * lax.rsqrt(var + EPSILON)


def two_parts(x):
    coarse = x.astype(BF16)
    return jnp.concatenate([coarse, (x - coarse.astype(F32)).astype(BF16)], 0)


def step_kernel(
    res_ref, chain_ref, mask_ref,
    pair_hbm, relpos_hbm, tri_hbm, triout_hbm, biasp_hbm, single_hbm, ada_hbm, noisy_hbm,
    qkvw_hbm, outp_hbm, cot_hbm,
    pairout_hbm, block_hbm, gpair_hbm, gsingle_hbm,
    pairout_ref, block_ref, gpair_ref,
    pair_in, tri_w, ada_w, noisy, relpos_ref, triout_ref, biasp_ref, single_ref, qkvw_ref, outp_ref,
    cot_ref, idx_r, mrow, relpos_w,
    zl_s, tri_t, pf, gate, lrf, lbuf, recv_a, got, rcat, lcat, mtmp, tbuf, got_c, got_d, bias_f, bias_b, bias_got,
    cvec_s, scale_s, shift_s, wg_s, gate_t, g_t, noisy_t, normed, hidden, wqkv, q_t, kv_f,
    kv_own, kv_all, dmx_own, dmx_all, da_t, keyok, sraw, draw,
    mix_s, mix_r, dkv_s, dkv_m, dkv_o, dkv_r, dq_t, dkv_tok, dbias, db_s, db_r,
    dsc, dsh, dga, dc_s, dc_r, dc_p, gs_own, gs_all,
    sa, ra, sb, rb, sc, rc, sd, rd, se, re, skv, rkv, skf, rkf, sdm, rdm,
    sm, rm, sk, rk, sko, rko, sbb, rbb, st, rt, sp, rp_, sg, rg, loc, locm, ready,
):
    row, col, samp = place()
    core = rmod(row, 2)
    zlo = row // 2
    mate = (row + 1 - 2 * core, col, samp)
    far = (row, col, 1 - samp)
    barrier = pltpu.get_barrier_semaphore()

    loads = [
        pltpu.make_async_copy(s, d, loc.at[18 + i])
        for i, (s, d) in enumerate(
            [
                (pair_hbm, pair_in), (relpos_hbm, relpos_ref), (tri_hbm, tri_w),
                (single_hbm, single_ref), (qkvw_hbm, qkvw_ref), (ada_hbm, ada_w),
                (noisy_hbm, noisy), (cot_hbm, cot_ref), (triout_hbm, triout_ref),
                (biasp_hbm, biasp_ref), (outp_hbm, outp_ref),
            ]
        )
    ]
    for copy in loads:
        copy.start()
    for oz, cx in ROW_IDS:
        signal(barrier, row_source(oz, cx))

    def greet(o, _):
        signal(barrier, (row, rmod(col + o, NCOL), samp))
        return 0

    def greet_row(o, _):
        signal(barrier, (rmod(row + o, NROW), col, samp))
        return 0

    lax.fori_loop(1, NCOL, greet, 0)
    lax.fori_loop(1, NROW, greet_row, 0)
    signal(barrier, far)

    low = lax.broadcasted_iota(jnp.int32, (64, 128), 1) < 64
    low16 = lax.broadcasted_iota(jnp.int32, (16, 128), 1) < 64
    low1 = lax.broadcasted_iota(jnp.int32, (1, 128), 1) < 64
    diag = (lax.broadcasted_iota(jnp.int32, (128, 128), 0) < 64) == (
        lax.broadcasted_iota(jnp.int32, (128, 128), 1) < 64
    )

    def blockdiag(x):
        return jnp.where(diag, jnp.concatenate([x, x], 0), 0.0).astype(BF16)

    def indices(i, _):
        at = pl.ds(i, 1)
        idx_r[0, at, :] = jnp.full((1, 128), res_ref[row * 64 + i], jnp.int32)
        idx_r[1, at, :] = jnp.full((1, 128), chain_ref[row * 64 + i], jnp.int32)
        m = jnp.full((1, 128), mask_ref[row * 64 + i].astype(F32), F32)
        mrow[at, :] = m
        mrow[pl.ds(64 + i, 1), :] = m
        return 0

    lax.fori_loop(0, 64, indices, 0, unroll=4)
    mrow[...] = mrow[...].T
    relpos_w[...] = jnp.zeros_like(relpos_w)
    loads[1].wait()
    relpos_w[0:REL_BINS, :] = relpos_ref[...]
    loads[0].wait()

    def load(i, _):
        pf[pl.ds(i * 32, 32), :] = pair_in[i].astype(F32)
        return 0

    lax.fori_loop(0, 64, load, 0, unroll=4)
    bins = lax.broadcasted_iota(jnp.int32, (64, 128), 1)

    def normed_rows(t, _):
        parts = []
        for q in range(2):
            for hi in range(2):
                j = 2 * t + q + 16 * hi
                off = jnp.clip(idx_r[0] - res_ref[col * 32 + j] + 32, 0, 64)
                bucket = jnp.where(idx_r[1] == chain_ref[col * 32 + j], off, REL_BINS - 1)
                onehot = jnp.where(bucket == bins, 1.0, 0.0).astype(BF16)
                parts.append(
                    pf[pl.ds(j, 64, stride=32), :]
                    + jnp.dot(onehot, relpos_w[...], preferred_element_type=F32)
                )
        for q in range(2):
            for hi in range(2):
                pf[pl.ds(2 * t + q + 16 * hi, 64, stride=32), :] = parts[2 * q + hi]
        at = pl.ds(pl.multiple_of(t * 256, 256), 256)
        zl_s[at, :] = layer_norm(jnp.concatenate(parts, 0), -1).astype(BF16)
        return 0

    lax.fori_loop(0, 8, normed_rows, 0, unroll=4)
    loads[2].wait()
    tri_t[...] = tri_w[:, :512].astype(F32).T.astype(BF16)

    def project(h, t):
        at = pl.ds(pl.multiple_of(t * 256, 256), 256)
        pt = dg(tri_t[h * 256 : h * 256 + 256, :], zl_s[at, :], 1, 1)
        val = sigmoid(pt[128:]) * pt[:128]
        for q in range(2):
            lo = 2 * t + q
            mask = mrow[0:1, :] * jnp.where(
                low1, mask_ref[col * 32 + lo].astype(F32), mask_ref[col * 32 + 16 + lo].astype(F32)
            )
            lrf[pl.ds(h * 2048 + lo, 128, stride=16), :] = val[:, q * 128 : q * 128 + 128] * mask

    pieces = [(0, slice(0, 8)), (1, slice(0, 4)), (1, slice(4, 8))]
    a_src = [lambda to, h=h, p=p: lbuf.at[h, to, p] for h, p in pieces]
    a_slot = [lambda c, h=h, p=p: recv_a.at[h, c, p] for h, p in pieces]
    b_src = [lambda r, h=h: recv_a.at[h, :, spot(r)] for h in range(2)]
    b_slot = [lambda r, h=h: got.at[h, r] for h in range(2)]
    own_a = [pltpu.make_async_copy(lbuf.at[h, col], recv_a.at[h, col], loc.at[h]) for h in range(2)]
    own_b = [
        pltpu.make_async_copy(recv_a.at[h, :, spot(row)], got.at[h, row], loc.at[2 + h])
        for h in range(2)
    ]
    for h in range(2):

        def one_side(t, _):
            project(h, t)
            return 0

        lax.fori_loop(0, 8, one_side, 0, unroll=2)

        def pack(c, _):
            lbuf[h, c] = lrf[pl.ds(h * 2048 + c * 128, 128), :].astype(BF16).reshape(8, 16, 128)
            return 0

        lax.fori_loop(0, 16, pack, 0, unroll=2)
        if h == 0:
            pl.semaphore_wait(barrier, 7 + 15 + 7 + 1)
            signal(ready, far)
        own_a[h].start()
        for i in ((0,), (1, 2))[h]:
            col_start(a_src[i], a_slot[i], sa.at[i], ra.at[i])

    for copy in loads[3:6]:
        copy.wait()
    cvec = layer_norm(single_ref[...].astype(F32), -1).astype(BF16)
    cvec_s[...] = cvec
    wqkv[...] = jnp.zeros_like(wqkv)
    for p in range(3):
        wqkv[p * 64 : p * 64 + 48, :] = qkvw_ref[p]
    scale_s[...] = sigmoid(jnp.dot(cvec, ada_w[:, :768], preferred_element_type=F32))
    shift_s[...] = jnp.dot(cvec, ada_w[:, 768:1536], preferred_element_type=F32)
    for copy in loads[6:]:
        copy.wait()

    def sample(s, _):
        at = pl.ds(pl.multiple_of(s * 64, 64), 64)
        n = layer_norm(noisy[at, :].astype(F32), -1)
        normed[at, :] = n
        hidden[at, :] = (scale_s[...] * n + shift_s[...]).astype(BF16)
        return 0

    lax.fori_loop(0, 8, sample, 0)
    own_a[0].wait()
    take(recv_a.at[0, 0:15], sa.at[0], ra.at[0])
    own_b[0].start()
    row_start(b_src[0], b_slot[0], sb.at[0], rb.at[0])

    feat = lax.broadcasted_iota(jnp.int32, (768, 64), 1)
    sel = jnp.where(
        (lax.broadcasted_iota(jnp.int32, (768, 64), 0) == col * 48 + feat) & (feat < 48), 1.0, 0.0
    ).astype(BF16)
    wg_s[...] = jnp.dot(ada_w[:, 1536:], sel, preferred_element_type=F32).astype(BF16)
    gate_t[...] = sigmoid(
        dg(wg_s[...], jnp.concatenate([cvec_s[...], cvec_s[...]], 0), 0, 1)
    )
    lane = lax.broadcasted_iota(jnp.int32, (64, 128), 1)
    tok = lax.broadcasted_iota(jnp.int32, (64, 128), 0)
    put = [jnp.where(lane == tok + 64 * h, 1.0, 0.0).astype(BF16) for h in range(2)]
    for u in range(4):
        g = jnp.dot(cot_ref[2 * u], put[0], preferred_element_type=F32) + jnp.dot(
            cot_ref[2 * u + 1], put[1], preferred_element_type=F32
        )
        g_t[u] = g
        dmx_own[:, u * 128 : u * 128 + 128] = (g * gate_t[:48, :]).astype(BF16)
    dm_src, dm_slot = (lambda to: dmx_own), (lambda c: dmx_all.at[c])
    dm_keep = pltpu.make_async_copy(dmx_own, dmx_all.at[col], loc.at[5])
    dm_keep.start()
    col_start(dm_src, dm_slot, sdm.at[0], rdm.at[0])
    kv_f[...] = dg(hidden[...], wqkv[64:, :], 1, 1)

    def kv_pack(t, _):
        r0 = kv_f[pl.ds(t * 32, 16), :]
        r1 = kv_f[pl.ds(t * 32 + 16, 16), :]
        to = pl.ds(pl.multiple_of(rmod(t, 2) * 16, 16), 16)
        kv_own[0, t // 2, to, :] = jnp.where(low16, r0, pltpu.roll(r1, 64, 1)).astype(BF16)
        kv_own[1, t // 2, to, :] = jnp.where(low16, pltpu.roll(r0, 64, 1), r1).astype(BF16)
        return 0

    lax.fori_loop(0, 16, kv_pack, 0, unroll=2)
    kv_keep = pltpu.make_async_copy(kv_own, kv_all.at[row], loc.at[4])
    kv_keep.start()
    kv_out = []
    for w in range(2):
        kv_out.append(remote(kv_own.at[w], kv_all.at[row, w], skf.at[w, 0], rkf.at[w, 0], mate))
        for o in range(1, 4):
            to = (rmod(zlo + o, 4) * 2 + core, col, samp)
            kv_out.append(
                remote(kv_own.at[w], kv_all.at[row, w], skv.at[w, o], rkv.at[w, o], to)
            )
    own_a[1].wait()
    for k in range(2):
        take(recv_a.at[1, 0:15, 0:4], sa.at[1 + k], ra.at[1 + k])
        cx = rmod(core + k, 2)
        for oz in (2, 1, 3):
            to = row_dest(oz, cx)
            remote(b_src[1](to[0]), b_slot[1](row), sb.at[1], rb.at[1], to).start()

        @pl.when(cx == 1)
        def _():
            remote(b_src[1](mate[0]), b_slot[1](row), sb.at[1], rb.at[1], mate).start()

    own_b[1].start()

    def gates(t, _):
        at = pl.ds(pl.multiple_of(t * 256, 256), 256)
        gate[at, :] = sigmoid(
            jnp.dot(zl_s[at, :], tri_w[:, 512:], preferred_element_type=F32)
        )
        return 0

    lax.fori_loop(0, 8, gates, 0)
    for h in (1, 0):
        own_b[h].wait()
        take(got.at[h, 0:7], sb.at[h], rb.at[h])

    def turn(r, _):
        x = got[1, r].reshape(256, 128).astype(F32).T.astype(BF16)
        at = pl.ds(pl.multiple_of(r * 64, 64), 64)
        rcat[at, 0:256] = x[:64]
        rcat[at, 256:512] = x[64:]
        return 0

    lax.fori_loop(0, 8, turn, 0, unroll=2)
    low256 = lax.broadcasted_iota(jnp.int32, (256, 128), 1) < 64
    turns = ((2, 1), (3, 0))
    for i, pair in enumerate(turns):
        for k, oz in enumerate(pair):
            z = rmod(zlo + oz, 4)
            la = got[0, 2 * z].reshape(256, 128).astype(F32)
            lb = got[0, 2 * z + 1].reshape(256, 128).astype(F32)
            lanes = slice(k * 128, k * 128 + 128)
            lcat[i, 0:256, lanes] = jnp.where(low256, la, pltpu.roll(lb, 64, 1)).astype(BF16)
            lcat[i, 256:512, lanes] = jnp.where(low256, pltpu.roll(la, 64, 1), lb).astype(BF16)
    c_src = [lambda r, p=p: tbuf.at[r, p] for p in (slice(0, 8), slice(8, 16))]
    c_slot = [lambda r, p=p: got_c.at[spot(r), p] for p in (slice(0, 8), slice(8, 16))]
    own_c = [
        pltpu.make_async_copy(c_src[h](row), c_slot[h](row), loc.at[6 + 3 * h]) for h in range(2)
    ]

    def tri(i, part):
        mtmp[...] = jnp.dot(
            rcat[part * 256 : part * 256 + 256, :], lcat[i], preferred_element_type=F32
        )

        def out(rj, _):
            for k, oz in enumerate(turns[i]):
                z = rmod(zlo + oz, 4)
                for jh in range(2):
                    at = rj * 64 + jh * 32
                    a = mtmp[pl.ds(at, 16), k * 128 : k * 128 + 128]
                    b = mtmp[pl.ds(at + 16, 16), k * 128 : k * 128 + 128]
                    even_row = jnp.where(low16, a, pltpu.roll(b, 64, 1))
                    odd_row = jnp.where(low16, pltpu.roll(a, 64, 1), b)
                    tbuf[2 * z, part * 8 + 2 * rj + jh] = even_row.astype(BF16)
                    tbuf[2 * z + 1, part * 8 + 2 * rj + jh] = odd_row.astype(BF16)
            return 0

        lax.fori_loop(0, 4, out, 0, unroll=2)

    for part in range(2):
        for i, pair in enumerate(turns):
            tri(i, part)
            for oz in pair:
                for cx in range(2):
                    if (oz, cx) != (0, 0):
                        to = row_dest(oz, cx)
                        remote(
                            c_src[part](to[0]), c_slot[part](row), sc.at[part], rc.at[part], to
                        ).start()
        own_c[part].start()
    for copy in kv_out:
        copy.start()
    d_own = pltpu.make_async_copy(got_c.at[:, col], got_d.at[col], loc.at[7])

    def d_start(part):
        def one(o, _):
            to = part * 8 + rmod(col + o, 8)

            @pl.when(to != col)
            def _():
                remote(got_c.at[:, to], got_d.at[col], sd.at[0], rd.at[0], (row, to, samp)).start()

            return 0

        lax.fori_loop(0, 8, one, 0)

    dm_keep.wait()
    take(dmx_all.at[0:15], sdm.at[0], rdm.at[0])
    da_t[...] = jnp.zeros_like(da_t)
    da_t[:48, :] = (
        jnp.dot(outp_ref[...], dmx_all[...].reshape(768, 512), preferred_element_type=F32)
        .astype(BF16)
        .astype(F32)
    )
    for part in range(2):
        own_c[part].wait()
        take(got_c.at[0:7, 0:8], sc.at[part], rc.at[part])
        d_start(part)
    d_own.start()

    q_t[...] = dg(wqkv[:64, :], hidden[...], 1, 1)
    noisy_t[...] = dg(sel, noisy[...], 0, 1)

    def key_mask(t, _):
        jb, lo = t // 16, rmod(t, 16)
        keyok[pl.ds(t, 1), :] = jnp.where(
            low1,
            mask_ref[jb * 32 + lo].astype(F32),
            mask_ref[jb * 32 + 16 + lo].astype(F32),
        )
        return 0

    lax.fori_loop(0, 256, key_mask, 0, unroll=4)

    def pass_keys(w):
        for o in range(1, 4):
            came = rmod(zlo + 4 - o, 4) * 2 + core
            remote(
                kv_own.at[w], kv_all.at[came, w], skv.at[w, o], rkv.at[w, o], mate
            ).wait_recv()
            remote(
                kv_all.at[came, w], kv_all.at[came, w], skf.at[w, o], rkf.at[w, o], mate
            ).start()

    def keys_passed(w):
        for o in range(4):
            came = rmod(zlo + 4 - o, 4) * 2
            remote(
                kv_all.at[came + core, w], kv_all.at[came + 1 - core, w], skf.at[w, o],
                rkf.at[w, o], mate,
            ).wait_recv()
            if o > 0:
                remote(
                    kv_all.at[came + core, w], kv_all.at[came + core, w], skf.at[w, o],
                    rkf.at[w, o], mate,
                ).wait_send()

    def half_of(ref, u, sh):
        tile = ref[:, pl.ds(pl.multiple_of(u * 128, 128), 128)].astype(F32)
        return blockdiag(both(tile, low, sh == 0))

    def keys(which, s):
        return jnp.concatenate([kv_all[r, which, s] for r in range(NROW)], 0)

    def raw(w):
        def one(u, _):
            for sh in range(2):
                s = 2 * u + sh
                (sraw, draw)[w][s] = jnp.dot(
                    keys(w, s), half_of((q_t, da_t)[w], u, sh), preferred_element_type=F32
                )
            return 0

        lax.fori_loop(0, 4, one, 0, unroll=2)

    d_own.wait()
    take(got_d.at[0:15], sd.at[0], rd.at[0])

    def widen(c, _):
        lrf[pl.ds(c * 128, 128), :] = got_d[c].reshape(128, 128).astype(F32)
        return 0

    lax.fori_loop(0, 16, widen, 0, unroll=4)

    def stage3(t, _):
        tn = layer_norm(
            jnp.concatenate([lrf[pl.ds(2 * t + q, 128, stride=16), :] for q in range(2)], 1), 0
        ).astype(BF16)
        upd = dg(tn, triout_ref[...], 0, 0) * gate[pl.ds(pl.multiple_of(t * 256, 256), 256), :]
        spots = [pl.ds(2 * t + q + 16 * hi, 64, stride=32) for q in range(2) for hi in range(2)]
        outs = [
            (pf[at, :] + upd[i * 64 : i * 64 + 64]).astype(BF16) for i, at in enumerate(spots)
        ]
        for at, val in zip(spots, outs):
            pf[at, :] = val.astype(F32)
        tile = dg(biasp_ref[...], jnp.concatenate(outs, 0), 1, 1)
        for q in range(2):
            bias_f[pl.ds(2 * t + q, 16, stride=16), :] = tile[:, q * 128 : q * 128 + 128]
        return 0

    lax.fori_loop(0, 8, stage3, 0, unroll=4)
    bias_b[...] = bias_f[...].astype(BF16).reshape(16, 16, 128)
    e_src, e_slot = (lambda c: bias_b.at[c]), (lambda c: bias_got.at[c])
    own_e = pltpu.make_async_copy(bias_b.at[col], bias_got.at[col], loc.at[8])
    own_e.start()
    col_start(e_src, e_slot, se.at[0], re.at[0])

    kv_keep.wait()
    pass_keys(0)

    def store(i, _):
        pairout_ref[i] = pf[pl.ds(i * 32, 32), :].astype(BF16)
        return 0

    lax.fori_loop(0, 64, store, 0, unroll=4)
    out_pair = pltpu.make_async_copy(pairout_ref, pairout_hbm, loc.at[14])
    out_pair.start()
    keys_passed(0)
    raw(0)
    pass_keys(1)
    for copy in kv_out:
        copy.wait_send()
    keys_passed(1)
    raw(1)
    dbias[...] = jnp.zeros_like(dbias)
    own_e.wait()
    take(bias_got.at[0:15], se.at[0], re.at[0])

    scale = 1.0 / HEAD_DIM**0.5

    def mix_src(u):
        return lambda f: mix_s.at[u, f]

    def mix_slot(u):
        return lambda h: mix_r.at[u, h]

    def to_mate(u):
        return remote(dkv_s.at[:, 1 - core, u], dkv_m.at[u], sk.at[u], rk.at[u], mate)

    def to_chip(u, o):
        z = rmod(zlo + o, 4)
        return remote(
            dkv_o.at[u, z], dkv_r.at[u, zlo], sko.at[u, o], rko.at[u, o], (z * 2 + core, col, samp)
        )

    def pass_on(u):
        to_mate(u).wait_recv()
        for z in range(4):
            dkv_o[u, z] = (
                dkv_s[z, core, u].astype(F32) + dkv_m[u, z].astype(F32)
            ).astype(BF16)
        for o in range(1, 4):
            to_chip(u, o).start()

    def pair_of_samples(u, _):
        folded, dqs = [], []
        for sh in range(2):
            s = 2 * u + sh
            kp, vp = keys(0, s), keys(1, s)
            qq, dd = half_of(q_t, u, sh), half_of(da_t, u, sh)
            sco = sraw[s] * scale + bias_got[...].reshape(256, 128).astype(F32)
            sco = jnp.where(keyok[...] > 0, sco, -1000000000.0)
            top = jnp.max(sco, 0, keepdims=True)
            top = jnp.maximum(top, pltpu.roll(top, 64, 1))
            ex = jnp.exp(sco - top)
            tot = jnp.sum(ex, 0, keepdims=True)
            probs = ex * (1.0 / (tot + pltpu.roll(tot, 64, 1)))
            pb = probs.astype(BF16)
            folded.append(dg(vp, pb, 0, 0))
            dp = draw[s]
            dot = jnp.sum(probs * dp, 0, keepdims=True)
            ds = probs * (dp - (dot + pltpu.roll(dot, 64, 1)))
            dbias[...] += ds
            dsb = (ds * scale).astype(BF16)
            dqs.append(dg(kp, dsb, 0, 0))
            dk = dg(dsb, qq, 1, 1).astype(BF16)
            dv = dg(pb, dd, 1, 1).astype(BF16)
            for r in range(NROW):
                dkv_s[r // 2, r % 2, u, sh] = dk[r * 32 : r * 32 + 32]
                dkv_s[r // 2, r % 2, u, 2 + sh] = dv[r * 32 : r * 32 + 32]

        def fold(m0, m1):
            return jnp.where(
                low,
                m0[:64] + pltpu.roll(m0[64:], 64, 1),
                pltpu.roll(m1[:64], 64, 1) + m1[64:],
            ).astype(BF16)

        att = fold(*folded)
        dq_t[u] = fold(*dqs)
        mix_s[u] = dg(outp_ref[...], att[:48], 0, 0).astype(BF16).reshape(16, 48, 128)
        pltpu.make_async_copy(mix_s.at[u, col], mix_r.at[u, col], locm.at[u]).start()
        to_mate(u).start()
        col_start(mix_src(u), mix_slot(u), sm.at[u], rm.at[u])

        @pl.when(u > 0)
        def _():
            pass_on(u - 1)

        return 0

    lax.fori_loop(0, 4, pair_of_samples, 0)

    db_s[...] = dbias[...].astype(BF16).reshape(16, 16, 128)
    own_db = pltpu.make_async_copy(db_s.at[col], db_r.at[samp, col], loc.at[29])
    own_db.start()

    def db_copy(o):
        to = rmod(col + o, NCOL)
        return remote(
            db_s.at[to], db_r.at[samp, col], sbb.at[1], rbb.at[1], (row, to, 1 - samp)
        )

    def db_send(o, _):
        db_copy(o).start()
        return 0

    pass_on(3)
    pl.semaphore_wait(ready, 1)
    lax.fori_loop(0, NCOL, db_send, 0)
    near_src, near_slot = (lambda c: db_s.at[c]), (lambda c: db_r.at[samp, c])
    col_start(near_src, near_slot, sbb.at[0], rbb.at[0])

    dga[...] = jnp.zeros_like(dga)

    def mixed_of(u, _):
        pltpu.make_async_copy(mix_s.at[u, col], mix_r.at[u, col], locm.at[u]).wait()
        take(mix_r.at[u, 0:15], sm.at[u], rm.at[u])
        total = mix_r[u, 0].astype(F32)
        for h in range(1, NCOL):
            total = total + mix_r[u, h].astype(F32)
        lanes = pl.ds(pl.multiple_of(u * 128, 128), 128)
        out = noisy_t[:48, lanes] + gate_t[:48, :] * total
        block_ref[2 * u] = out[:, :64].astype(BF16)
        block_ref[2 * u + 1] = pltpu.roll(out, 64, 1)[:, :64].astype(BF16)
        dga[:48, :] += g_t[u] * total
        return 0

    lax.fori_loop(0, 3, mixed_of, 0)

    dsc[...] = jnp.zeros_like(dsc)
    dsh[...] = jnp.zeros_like(dsh)

    def hidden_grad(u, _):
        to_mate(u).wait_send()
        for o in range(1, 4):
            came = rmod(zlo + 4 - o, 4)
            remote(
                dkv_o.at[u, came], dkv_r.at[u, came], sko.at[u, o], rko.at[u, o], mate
            ).wait_recv()
            to_chip(u, o).wait_send()
        dkv_r[u, zlo] = dkv_o[u, zlo]
        tot = dkv_r[u, 0].astype(F32)
        for z in range(1, 4):
            tot = tot + dkv_r[u, z].astype(F32)
        for sh in range(2):
            for jb in range(2):
                a = tot[sh, jb * 16 : jb * 16 + 16]
                b = tot[2 + sh, jb * 16 : jb * 16 + 16]
                base = sh * 64 + jb * 32
                dkv_tok[base : base + 16, :] = jnp.where(low16, a, pltpu.roll(b, 64, 1)).astype(BF16)
                dkv_tok[base + 16 : base + 32, :] = jnp.where(
                    low16, pltpu.roll(a, 64, 1), b
                ).astype(BF16)
        dh = dg(dq_t[u], wqkv[:64, :], 0, 0) + jnp.dot(
            dkv_tok[...], wqkv[64:, :], preferred_element_type=F32
        )
        n = normed[pl.ds(pl.multiple_of(u * 128, 128), 128), :]
        w = dh * n
        dsc[...] += w[:64] + w[64:]
        dsh[...] += dh[:64] + dh[64:]
        return 0

    lax.fori_loop(0, 3, hidden_grad, 0)
    mixed_of(3, 0)
    out_block = pltpu.make_async_copy(block_ref, block_hbm, loc.at[15])
    out_block.start()
    hidden_grad(3, 0)
    sg_ = scale_s[...]
    part = dg(two_parts(dsc[...] * sg_ * (1.0 - sg_)), ada_w[:, :768], 1, 1)
    part = part + dg(two_parts(dsh[...]), ada_w[:, 768:1536], 1, 1)
    part = part[:64] + part[64:]
    acc = dga[...]
    acc = (acc + pltpu.roll(acc, 64, 1)) * gate_t[...] * (1.0 - gate_t[...])
    coarse = acc.astype(BF16)
    fine = (acc - coarse.astype(F32)).astype(BF16)
    part = part + (dg(coarse, wg_s[...], 0, 1) + dg(fine, wg_s[...], 0, 1))[:64]
    dc_s[...] = part.reshape(8, 8, 384)

    half_col = col // 2
    even = rmod(col, 2) == 0

    def part_copy(o):
        g = rmod(half_col + o, 8)
        return remote(dc_s.at[g], dc_r.at[col], st.at[0], rt.at[0], (row, 2 * g, samp))

    @pl.when(jnp.logical_not(even))
    def _():
        part_copy(0).start()

    def part_send(o, _):
        part_copy(o).start()
        return 0

    lax.fori_loop(1, 8, part_send, 0)

    own_db.wait()
    take(db_r.at[0, 0:15], sbb.at[0], rbb.at[0])
    take(db_r.at[0], sbb.at[1], rbb.at[1])
    dbias[...] = (db_r[0].astype(F32) + db_r[1].astype(F32)).reshape(256, 128)
    biasp3 = jnp.concatenate([biasp_ref[...]] * 3, 0)

    def grad(lo, _):
        d = dbias[pl.ds(lo, 16, stride=16), :]
        d1 = d.astype(BF16)
        rest = d - d1.astype(F32)
        d2 = rest.astype(BF16)
        d3 = (rest - d2.astype(F32)).astype(BF16)
        g = dg(jnp.concatenate([d1, d2, d3], 0), biasp3, 0, 0)
        for hi in range(2):
            gpair_ref[pl.ds(lo + 16 * hi, 64, stride=32), :] = g[hi * 64 : hi * 64 + 64]
        return 0

    lax.fori_loop(0, 16, grad, 0, unroll=2)
    out_grad = pltpu.make_async_copy(gpair_ref, gpair_hbm, loc.at[16])
    out_grad.start()

    def own_copy(o):
        return remote(
            gs_own, gs_all.at[half_col], sg.at[0], rg.at[0], (row, rmod(col + o, NCOL), samp)
        )

    @pl.when(even)
    def _():
        dc_r[col] = dc_s[half_col]

        take(dc_r.at[0:15], rt.at[0])
        tot = dc_r[0]
        for c in range(1, NCOL):
            tot = tot + dc_r[c]
        dc_p[samp] = tot
        other = remote(dc_p.at[samp], dc_p.at[samp], sp.at[0], rp_.at[0], far)
        other.start()
        own = single_ref[...].astype(F32).reshape(8, 8, 384)
        mine = jnp.zeros((8, 384), F32)
        for g in range(8):
            mine = mine + jnp.where(half_col == g, own[g], 0.0)
        mean = jnp.mean(mine, -1, keepdims=True)
        cent = mine - mean
        inv = lax.rsqrt(jnp.mean(cent * cent, -1, keepdims=True) + EPSILON)
        unit = cent * inv
        remote(dc_p.at[samp], dc_p.at[1 - samp], sp.at[0], rp_.at[0], far).wait_recv()
        other.wait_send()
        up = dc_p[0] + dc_p[1]
        gs_own[...] = inv * (
            up - jnp.mean(up, -1, keepdims=True) - unit * jnp.mean(up * unit, -1, keepdims=True)
        )

        def tell(o, _):
            own_copy(o).start()
            return 0

        lax.fori_loop(1, NCOL, tell, 0)
        gs_all[half_col] = gs_own[...]

    @pl.when(even)
    def _():
        take(dc_s.at[0:7], st.at[0])
        take(dc_r.at[0:15], sg.at[0])
        take(gs_all.at[0:7], rg.at[0])

    @pl.when(jnp.logical_not(even))
    def _():
        take(dc_s, st.at[0])
        take(gs_all, rg.at[0])

    out_single = pltpu.make_async_copy(gs_all, gsingle_hbm, loc.at[17])
    out_single.start()
    for copy in (out_pair, out_block, out_grad, out_single):
        copy.wait()


def finish_kernel(*refs):
    n = 4
    ins, outs, bufs = refs[:n], refs[n : 2 * n], refs[2 * n : 3 * n]
    got, put = refs[3 * n], refs[3 * n + 1]
    reads = [pltpu.make_async_copy(ins[i], bufs[i], got.at[i]) for i in range(n)]
    writes = [pltpu.make_async_copy(bufs[i], outs[i], put.at[i]) for i in range(n)]
    for copy in reads:
        copy.start()
    for i in (3, 1, 0, 2):
        reads[i].wait()
        writes[i].start()
    for copy in writes:
        copy.wait()


def finished(arrays):
    hbm = pl.BlockSpec(memory_space=pl.ANY)
    return pl.pallas_call(
        finish_kernel,
        out_shape=[jax.ShapeDtypeStruct(x.shape, x.dtype) for x in arrays],
        in_specs=[hbm] * 4,
        out_specs=[hbm] * 4,
        scratch_shapes=[pltpu.VMEM(x.shape, x.dtype) for x in arrays]
        + [pltpu.SemaphoreType.DMA((4,)), pltpu.SemaphoreType.DMA((4,))],
        compiler_params=pltpu.CompilerParams(vmem_limit_bytes=60 * 1024 * 1024),
        name="finish",
    )(*arrays)


def on_device(
    pair_in, residue_index, chain_index, token_mask, relpos_weight, tri_proj, tri_out, bias_proj,
    single, ada_proj, noisy, qkv_proj, out_proj, cotangent,
):
    sm = pl.BlockSpec(memory_space=pltpu.SMEM)
    hbm = pl.BlockSpec(memory_space=pl.ANY)
    dma = pltpu.SemaphoreType.DMA
    v = pltpu.VMEM
    pair_out, block_t, grad_pair, grad_single = pl.pallas_call(
        step_kernel,
        out_shape=(
            jax.ShapeDtypeStruct((64, 32, 128), BF16),
            jax.ShapeDtypeStruct((8, 48, 64), BF16),
            jax.ShapeDtypeStruct((2048, 128), F32),
            jax.ShapeDtypeStruct((8, 8, 384), F32),
        ),
        in_specs=[sm] * 3 + [hbm] * 11,
        out_specs=(hbm,) * 4,
        scratch_shapes=[
            v((64, 32, 128), BF16), v((8, 48, 64), BF16), v((2048, 128), F32),
            v((64, 32, 128), BF16), v((128, 640), BF16), v((384, 2304), BF16), v((512, 768), BF16),
            v((REL_BINS, 128), BF16), v((128, 128), BF16), v((16, 128), BF16), v((64, 384), BF16),
            v((3, 48, 768), BF16), v((48, 768), BF16), v((8, 48, 64), BF16),
            v((2, 64, 128), jnp.int32), v((128, 128), F32), v((128, 128), BF16),
            v((2048, 128), BF16), v((512, 128), BF16), v((2048, 128), F32), v((2048, 128), F32),
            v((4096, 128), F32),
            v((2, 16, 8, 16, 128), BF16), v((2, 16, 8, 16, 128), BF16),
            v((2, 8, 16, 16, 128), BF16), v((512, 512), BF16), v((2, 512, 256), BF16),
            v((256, 256), F32),
            v((8, 16, 16, 128), BF16), v((8, 16, 16, 128), BF16), v((16, 8, 16, 128), BF16),
            v((256, 128), F32), v((16, 16, 128), BF16), v((16, 16, 128), BF16),
            v((64, 384), BF16), v((64, 768), F32), v((64, 768), F32), v((384, 64), BF16),
            v((64, 128), F32), v((4, 48, 128), F32), v((64, 512), F32), v((512, 768), F32),
            v((512, 768), BF16), v((192, 768), BF16), v((64, 512), F32), v((512, 128), F32),
            v((2, 8, 32, 128), BF16), v((8, 2, 8, 32, 128), BF16), v((48, 512), BF16),
            v((16, 48, 512), BF16), v((64, 512), F32), v((256, 128), F32), v((8, 256, 128), F32),
            v((8, 256, 128), F32),
            v((4, 16, 48, 128), BF16), v((4, 16, 48, 128), BF16), v((4, 2, 4, 4, 32, 128), BF16),
            v((4, 4, 4, 32, 128), BF16), v((4, 4, 4, 32, 128), BF16), v((4, 4, 4, 32, 128), BF16),
            v((4, 64, 128), BF16), v((128, 128), BF16), v((256, 128), F32), v((16, 16, 128), BF16),
            v((2, 16, 16, 128), BF16),
            v((64, 768), F32), v((64, 768), F32), v((64, 128), F32), v((8, 8, 384), F32),
            v((16, 8, 384), F32), v((2, 8, 384), F32), v((8, 384), F32), v((8, 8, 384), F32),
            dma((3,)), dma((3,)), dma((2,)), dma((2,)), dma((2,)), dma((2,)),
            dma((1,)), dma((1,)), dma((1,)), dma((1,)), dma((2, 4)), dma((2, 4)),
            dma((2, 4)), dma((2, 4)), dma((1,)), dma((1,)),
            dma((4,)), dma((4,)), dma((4,)), dma((4,)), dma((4, 4)), dma((4, 4)),
            dma((2,)), dma((2,)), dma((1,)), dma((1,)), dma((1,)), dma((1,)),
            dma((1,)), dma((1,)), dma((30,)), dma((4,)), pltpu.SemaphoreType.REGULAR,
        ],
        compiler_params=pltpu.CompilerParams(
            collective_id=1, has_side_effects=True, vmem_limit_bytes=60 * 1024 * 1024
        ),
        name="step",
    )(
        residue_index, chain_index, token_mask, pair_in, relpos_weight, tri_proj, tri_out,
        bias_proj.T, single, ada_proj, noisy.reshape(512, 768), qkv_proj.transpose(1, 2, 0),
        out_proj, cotangent.transpose(0, 2, 1),
    )
    pair_out, block_t, grad_pair, grad_single = finished(
        (pair_out, block_t, grad_pair, grad_single)
    )
    return (
        pair_out,
        block_t.transpose(0, 2, 1),
        grad_pair.reshape(64, 32, 128),
        grad_single.reshape(64, 384),
    )


def solution(mesh):
    return jax.shard_map(
        on_device,
        mesh=mesh,
        in_specs=(
            P("row", "col", None), P(), P(), P(), P(), P(), P(), P(), P("row", None), P(),
            P("samp", "row", None), P(None, None, "col"), P("col", None), P("samp", "row", "col"),
        ),
        out_specs=(
            P("row", "col", None), P("samp", "row", "col"), P("row", "col", None), P("row", None),
        ),
        check_vma=False,
    )
```
